32 devices in a mesh: blk: 8 (over z, x), rows: 4 (over y, core).
Axes of the slice: x: 2, y: 2, z: 4, core: 2. Of those that a mesh axis runs over, the one named last changes fastest.
Arguments:
- features: bfloat16 [8192, 2048], P(('blk', 'rows')), may hold values from -6 to 6
- head_weight: bfloat16 [2048, 768], replicated, may hold values from -0.0048828125 to 0.0048828125
- labels: int32 [8192], P(('blk', 'rows')), may hold values from 0 to 11317
- pos_index: int32 [8192, 3], P(('blk', 'rows')), may hold values from 0 to 1023
- pair_mask: int32 [8, 3], P('blk'), may hold values from 0 to 1, as said below
- loss_weight: float32 [8192], P(('blk', 'rows')), may hold values from 0.25 to 1
Outputs:
- anchor_loss: float32 [8192], P(('blk', 'rows'))
- weight_grad: float32 [2048, 768], P(('blk', 'rows'))
The draws below stay inside these ranges and needn't reach their ends.
Inputs may be any that keep to these rules, and one draw needn't show every extreme that they name: `pair_mask`: entry [t, s] is 1 where anchor tile t scores the rows of tile (t - s) mod 8, else 0. The rows of tiles 0 to 2 and of tile 8 - 1 are all ones.
All inputs are finite; a program needn't handle non-finite values.
Results may differ from the reference program's by a relative error of at most 0.0034.
Values may be sent and summed in bfloat16 or wider, within the bound.
A program may use at most 128 MiB of HBM per device.

```python
import math
import jax
import jax.numpy as jnp
import numpy as np
from jax import lax

D = 768
F = 2048
POSITIVES = 3
WIN = 2
CLASSES = 11318
BAND = 3
TILE = 1024
BATCH = 8192
N_BLK = 8


def draw_pair_mask(key, part):
    level_key, score_key = jax.random.split(jax.random.fold_in(key, 17))
    levels = jax.random.randint(level_key, (N_BLK, 1), 1, BAND + 1)
    scores = jax.random.randint(score_key, (N_BLK, BAND), 0, BAND * BAND * BAND)
    base = (scores < levels * levels * levels).astype(jnp.int32)
    tile_ids = jnp.arange(N_BLK, dtype=jnp.int32)[:, None]
    forced = (tile_ids <= WIN) | (tile_ids >= N_BLK - 1)
    return jnp.where(forced, jnp.ones_like(base), base).astype(jnp.int32)


def plant(drawn, rng, low, largest):
    shape = drawn.shape
    spot = [jax.random.randint(jax.random.fold_in(rng, axis), (), 0, shape[axis]) for axis in range(len(shape))]
    drawn = drawn.at[tuple(spot)].set(low)
    longest = shape.index(max(shape))
    spot[longest] = (spot[longest] + 1) % shape[longest]
    return drawn.at[tuple(spot)].set(largest)


def spiked(array, own_key, source, target, blocks, factor):
    def block_of(axis_at):
        return (jnp.arange(array.shape[axis_at]) // (array.shape[axis_at] // blocks)).reshape((-1,) + (1,) * (array.ndim - 1 - axis_at))

    near = jax.random.permutation(own_key, blocks)[block_of(target)]
    other_side = (block_of(target) + blocks // 2) % blocks
    return jnp.where((block_of(source) == near) | (block_of(source) == other_side), factor * array, array)


def block_scale(rng, extent, pieces, low, largest):
    gain, own = 1.0, jax.random.fold_in(rng, 6)
    for axis_at, parts in pieces:
        heights = jnp.exp(jax.random.uniform(jax.random.fold_in(own, axis_at), (parts,), jnp.float32, low / len(pieces), largest / len(pieces)))
        gain = gain * jnp.repeat(heights, extent[axis_at] // parts).reshape([-1 if axis == axis_at else 1 for axis in range(len(extent))])
    return gain


def cumulative_ranks(count, slope):
    loads = [(1 << 20) // math.isqrt(standing ** slope) + 1 for standing in range(1, count + 1)]
    spread = 1 + sum(loads) // (1 << 30)
    return np.cumsum(np.array([max(1, weight // spread) for weight in loads]))


def skewed_ids(stream_key, dims, count, skew):
    grid = cumulative_ranks(count, skew)
    pick = jax.random.randint(jax.random.fold_in(stream_key, 1), dims, 0, int(grid[count - 1]))
    standing = jnp.searchsorted(jnp.asarray(grid, jnp.int32), pick, side="right")
    return jax.random.permutation(jax.random.fold_in(stream_key, 2), count)[standing].astype(jnp.int32)


def bell_draw(own_key, shape, scale, bound, cuts=(), held_as=jnp.bfloat16):
    result = scale * jax.random.normal(own_key, shape, jnp.float32)
    if cuts:
        result = result * block_scale(own_key, shape, cuts, -0.22, 0.18)
    return jnp.clip(result, -bound, bound).astype(held_as)


def bell_draw_with(key, extent, deviation, limit, pieces, heavy, kind=jnp.bfloat16):
    values = deviation * jax.random.normal(key, extent, jnp.float32)
    if pieces:
        values = values * block_scale(key, extent, pieces, -0.22, 0.18)
    return jnp.clip(spiked(values, jax.random.fold_in(key, 3), *heavy), -limit, limit).astype(kind)


def setup_inputs(seed: int = 0) -> dict:
    arg_keys = jax.random.split(jax.random.key(seed), 7)
    features = bell_draw_with(arg_keys[0], (BATCH, F), 1.0, 6.0, ((0, 32),), (0, 1, 32, 2.75))
    head_weight = bell_draw(arg_keys[1], (F, D), (F * D) ** -0.5, 0.0048828125)
    labels = plant(skewed_ids(arg_keys[2], (BATCH,), CLASSES, 3), jax.random.fold_in(arg_keys[2], 3), 0, CLASSES - 1).astype(jnp.int32)
    pos_index = plant(jax.random.randint(arg_keys[3], (BATCH, POSITIVES), 0, TILE), jax.random.fold_in(arg_keys[3], 1), 0, TILE - 1).astype(jnp.int32)
    pair_mask = draw_pair_mask(jax.random.fold_in(arg_keys[6], 71), 0)
    loss_weight = jnp.clip(jnp.exp(math.log(1.0) - 1.3862944 * jax.random.uniform(arg_keys[5], (BATCH,), jnp.float32) ** block_scale(arg_keys[5], (BATCH,), ((0, 32),), -0.2, 0.2)), 0.25, 1.0)
    return {"features": features, "head_weight": head_weight, "labels": labels, "pos_index": pos_index, "pair_mask": pair_mask, "loss_weight": loss_weight}


SMOOTHING_SCALE = 16.0
SLACK_GAP = 0.1


def score_tile(anchors, anchor_sq, anchor_labels, matching_separation, weights, tile_rows, tile_labels, listed):
    matching_samples = matching_separation.shape[1]
    block_tally = tile_rows.shape[0]
    anchor_count = anchors.shape[0]

    def compute(unused):
        products = lax.dot_general(anchors, tile_rows, (((1,), (1,)), ((), ())), preferred_element_type=jnp.float32)
        widened = tile_rows.astype(jnp.float32)
        tile_sq = jnp.sum(widened * widened, axis=1)
        couple_separation = anchor_sq[:, None] + tile_sq[None, :] - 2.0 * products
        valid = (anchor_labels[:, None] != tile_labels[None, :]).astype(jnp.float32)
        weighting = weights / (matching_samples * block_tally)
        objective_accrued = jnp.zeros((anchor_count,), jnp.float32)
        coefficient = jnp.zeros((anchor_count, block_tally), jnp.float32)
        totals = []
        for target_slot in range(matching_samples):
            slack_excess = SMOOTHING_SCALE * (matching_separation[:, target_slot:target_slot + 1] - couple_separation + SLACK_GAP)
            objective_accrued = objective_accrued + jnp.sum(valid * jax.nn.softplus(slack_excess), axis=1)
            sigmoids = valid * jax.nn.sigmoid(slack_excess)
            coefficient = coefficient + sigmoids
            totals.append(jnp.sum(sigmoids, axis=1))
        objective_accrued = objective_accrued / (SMOOTHING_SCALE * matching_samples * block_tally)
        coefficient = coefficient * weighting[:, None]
        pos_coef = jnp.stack(totals, axis=1) * weighting[:, None]
        coef_low = coefficient.astype(jnp.bfloat16)
        anchor_grad = 2.0 * jnp.dot(coef_low, tile_rows, preferred_element_type=jnp.float32)
        pulled = lax.dot_general(coef_low, anchors, (((0,), (0,)), ((), ())), preferred_element_type=jnp.float32)
        tile_grad = 2.0 * (pulled - jnp.sum(coefficient, axis=0)[:, None] * widened)
        return objective_accrued, pos_coef, anchor_grad, tile_grad

    def skip(unused):
        return (jnp.zeros((anchor_count,), jnp.float32),
                jnp.zeros((anchor_count, matching_samples), jnp.float32),
                jnp.zeros((anchor_count, anchors.shape[1]), jnp.float32),
                jnp.zeros((block_tally, anchors.shape[1]), jnp.float32))

    return lax.cond(listed, compute, skip, 0)


def reference(features, head_weight, labels, pos_index, pair_mask, loss_weight):
    embedded = jnp.dot(features, head_weight, preferred_element_type=jnp.float32).astype(jnp.bfloat16)
    widened = embedded.astype(jnp.float32)
    squares = jnp.sum(widened * widened, axis=1)
    tile_emb = embedded.reshape(N_BLK, TILE, D)
    tile_sq = squares.reshape(N_BLK, TILE)
    tile_lab = labels.reshape(N_BLK, TILE)
    tile_pos = pos_index.reshape(N_BLK, TILE, POSITIVES)
    tile_weight = loss_weight.reshape(N_BLK, TILE)

    def per_tile(term_total, inputs):
        index, anchors, anchor_sq, anchor_labels, positions, weights, mask_row = inputs
        pos_rows = anchors[positions]
        pos_wide = pos_rows.astype(jnp.float32)
        pos_sq = anchor_sq[positions]
        matching_separation = anchor_sq[:, None] + pos_sq - 2.0 * jnp.einsum(
            "ad,akd->ak", anchors.astype(jnp.float32), pos_wide)
        loss_total = jnp.zeros((TILE,), jnp.float32)
        coef_total = jnp.zeros((TILE, POSITIVES), jnp.float32)
        grad_total = jnp.zeros((TILE, D), jnp.float32)
        for offset in range(BAND):
            target = (index - offset) % N_BLK
            tile_rows = lax.dynamic_index_in_dim(tile_emb, target, 0, keepdims=False)
            tile_labels = lax.dynamic_index_in_dim(tile_lab, target, 0, keepdims=False)
            loss_part, coef_part, grad_part, term_part = score_tile(
                anchors, anchor_sq, anchor_labels, matching_separation, weights, tile_rows, tile_labels, mask_row[offset] > 0)
            loss_total = loss_total + loss_part
            coef_total = coef_total + coef_part
            grad_total = grad_total + grad_part
            current = lax.dynamic_index_in_dim(term_total, target, 0, keepdims=False)
            term_total = lax.dynamic_update_index_in_dim(term_total, current + term_part, target, 0)
        grad_total = grad_total - 2.0 * jnp.sum(coef_total[:, :, None] * pos_wide, axis=1)
        pushed = 2.0 * coef_total[:, :, None] * (pos_wide - anchors.astype(jnp.float32)[:, None, :])
        own_term = jnp.zeros((TILE, D), jnp.float32).at[positions.reshape(-1)].add(pushed.reshape(-1, D))
        current = lax.dynamic_index_in_dim(term_total, index, 0, keepdims=False)
        term_total = lax.dynamic_update_index_in_dim(term_total, current + own_term, index, 0)
        return term_total, (loss_total, grad_total)

    start_terms = jnp.zeros((N_BLK, TILE, D), jnp.float32)
    term_total, outputs = lax.scan(per_tile, start_terms, (jnp.arange(N_BLK, dtype=jnp.int32), tile_emb, tile_sq, tile_lab, tile_pos, tile_weight, pair_mask))
    loss_tiles, grad_tiles = outputs
    emb_grad = grad_tiles.reshape(BATCH, D) + term_total.reshape(BATCH, D)
    grad_low = emb_grad.astype(jnp.bfloat16)
    weight_grad = jnp.dot(features.T, grad_low, preferred_element_type=jnp.float32)
    return loss_tiles.reshape(BATCH), weight_grad
```

```python
import contextlib
import math

import jax
import jax.numpy as jnp
from jax import lax
from jax.experimental import pallas as pl
from jax.experimental.pallas import tpu as pltpu
from jax.sharding import PartitionSpec as P

SMOOTHING_SCALE = 16.0
SLACK_GAP = 0.1


def passed_along(block, axis, distance):
    devices = range(lax.axis_size(axis))
    route = [((i - distance) % len(devices), i) for i in devices]
    return lax.ppermute(block, axis, route)


def score_tile(
    anchors, anchor_sq, anchor_labels, matching_separation, weights, tile_rows, tile_labels, listed
):
    matching_samples = matching_separation.shape[1]
    block_tally = tile_rows.shape[0]
    anchor_count = anchors.shape[0]

    def compute(unused):
        products = lax.dot_general(
            anchors, tile_rows, (((1,), (1,)), ((), ())), preferred_element_type=jnp.float32
        )
        widened = tile_rows.astype(jnp.float32)
        tile_sq = jnp.sum(widened * widened, axis=1)
        couple_separation = anchor_sq[:, None] + tile_sq[None, :] - 2.0 * products
        valid = (anchor_labels[:, None] != tile_labels[None, :]).astype(jnp.float32)
        weighting = weights / (matching_samples * block_tally)
        objective_accrued = jnp.zeros((anchor_count,), jnp.float32)
        coefficient = jnp.zeros((anchor_count, block_tally), jnp.float32)
        totals = []
        for target_slot in range(matching_samples):
            slack_excess = SMOOTHING_SCALE * (
                matching_separation[:, target_slot : target_slot + 1]
                - couple_separation
                + SLACK_GAP
            )
            objective_accrued = objective_accrued + jnp.sum(
                valid * jax.nn.softplus(slack_excess), axis=1
            )
            sigmoids = valid * jax.nn.sigmoid(slack_excess)
            coefficient = coefficient + sigmoids
            totals.append(jnp.sum(sigmoids, axis=1))
        objective_accrued = objective_accrued / (SMOOTHING_SCALE * matching_samples * block_tally)
        coefficient = coefficient * weighting[:, None]
        pos_coef = jnp.stack(totals, axis=1) * weighting[:, None]
        coef_low = coefficient.astype(jnp.bfloat16)
        anchor_grad = 2.0 * jnp.dot(coef_low, tile_rows, preferred_element_type=jnp.float32)
        pulled = lax.dot_general(
            coef_low, anchors, (((0,), (0,)), ((), ())), preferred_element_type=jnp.float32
        )
        col_sums = jnp.sum(coefficient, axis=0)
        tile_grad = 2.0 * (pulled - col_sums[:, None] * widened)
        return (objective_accrued, pos_coef, anchor_grad, tile_grad, coef_low, col_sums)

    def skip(unused):
        return (
            jnp.zeros((anchor_count,), jnp.float32),
            jnp.zeros((anchor_count, matching_samples), jnp.float32),
            jnp.zeros((anchor_count, anchors.shape[1]), jnp.float32),
            jnp.zeros((block_tally, anchors.shape[1]), jnp.float32),
            jnp.zeros((anchor_count, block_tally), jnp.bfloat16),
            jnp.zeros((block_tally,), jnp.float32),
        )

    return lax.cond(listed, compute, skip, 0)


def local(features, head_weight, labels, pos_index, pair_mask, loss_weight):
    embedded = jnp.dot(features, head_weight, preferred_element_type=jnp.float32).astype(
        jnp.bfloat16
    )
    widened = embedded.astype(jnp.float32)
    anchor_sq = jnp.sum(widened * widened, axis=1)
    tile_rows, tile_labels = (
        lax.all_gather(embedded, "rows", axis=0, tiled=True),
        lax.all_gather(labels, "rows", axis=0, tiled=True),
    )
    pos_rows = tile_rows[pos_index]
    pos_wide = pos_rows.astype(jnp.float32)
    pos_sq = jnp.sum(pos_wide * pos_wide, axis=2)
    matching_separation = (
        anchor_sq[:, None]
        + pos_sq
        - 2.0 * jnp.einsum("ad,akd->ak", embedded, pos_rows, preferred_element_type=jnp.float32)
    )
    offsets = pair_mask.shape[1]
    loss_total, coef_total, grad_total, own_term, first_low, first_sums = score_tile(
        embedded,
        anchor_sq,
        labels,
        matching_separation,
        loss_weight,
        tile_rows,
        tile_labels,
        pair_mask[0, 0] > 0,
    )
    received = jnp.zeros_like(own_term)
    walk_rows, walk_labels = (tile_rows, tile_labels)
    for offset in range(1, offsets):
        walk_rows, walk_labels = passed_along((walk_rows, walk_labels), "blk", 1)
        loss_part, coef_part, grad_part, term_part, low_part, sums_part = score_tile(
            embedded,
            anchor_sq,
            labels,
            matching_separation,
            loss_weight,
            walk_rows,
            walk_labels,
            pair_mask[0, offset] > 0,
        )
        loss_total = loss_total + loss_part
        coef_total = coef_total + coef_part
        grad_total = grad_total + grad_part
        received = received + passed_along(term_part.astype(jnp.bfloat16), "blk", -offset).astype(
            term_part.dtype
        )
    grad_total = grad_total - 2.0 * jnp.sum(coef_total[:, :, None] * pos_wide, axis=1)
    pushed = 2.0 * coef_total[:, :, None] * (pos_wide - widened[:, None, :])
    own_term = own_term.at[pos_index.reshape(-1)].add(pushed.reshape(-1, pushed.shape[2]))
    quarter_sum = lax.psum_scatter(own_term + received, "rows", scatter_dimension=0, tiled=True)
    emb_grad = grad_total + quarter_sum
    grad_low = emb_grad.astype(jnp.bfloat16)
    weight_grad = lax.psum_scatter(
        lax.dot_general(
            features, grad_low, (((0,), (0,)), ((), ())), preferred_element_type=jnp.float32
        ),
        ("blk", "rows"),
        scatter_dimension=0,
        tiled=True,
    )
    return (loss_total, weight_grad)


MESH = pl.DeviceIdType.MESH
NT = (((1,), (1,)), ((), ()))
TN = (((0,), (0,)), ((), ()))


def dot(a, b, dims=(((1,), (0,)), ((), ()))):
    return lax.dot_general(a, b, dims, preferred_element_type=jnp.float32)


LOG2E = math.log2(math.e)
LN2 = math.log(2.0)
CEILING = 40.0
FAR = 1e38
PIECES = 3
SUB = 32
STEPS = 12
FIRST = 1
LAGS = (1, 2)
TILE_CODE = sum(s << (2 * i) for i, s in enumerate((1, 0, 1, 1, 1, 0, 0, 2, 2, 2, 2, 0)))
PEER_CODE = sum(p << (2 * i) for i, p in enumerate((0, 0, 3, 2, 1, 3, 2, 3, 2, 1, 0, 1)))


def scope(name):
    return contextlib.nullcontext()


def spread_rows(row):
    return jnp.transpose(jnp.broadcast_to(row, (128, row.shape[1])))


def twice(block):
    return jnp.concatenate([block, block], axis=1)


def by_eights(block):
    total = block[0:8]
    for i in range(1, block.shape[0] // 8):
        total = total + block[8 * i : 8 * i + 8]
    return total


def kernel(
    f_hbm, w_hbm, lab_ref, pos_ref, wgt_ref, mask_ref, loss_ref, out_ref,
    fv, wv, ea, nr, meta, metan, scored, fc, fct, acc, pul, cs, prod, low, dpr, sqc, labc, sqn, stp, st, strec, tot,
    tst, trec, ast0, arec0, ast1, arec1, hst, hrec, ga, yown, yst, yrec, pst, prec,
    f_l, w_l, ea_s, ea_r, ma_s, ma_r, en_s, en_r, mn_s, mn_r, fc_s, fc_r, d_s, d_r, t_s, t_r, a0_s, a0_r, a1_s, a1_r,
    h_s, h_r, st_s, st_r, g_s, g_r, y_s, y_r, p_s, p_r,
):
    nb = lax.axis_size("blk")
    t = lax.axis_index("blk")
    r = lax.axis_index("rows")
    z, x = t // 2, t % 2
    y, c = r // 2, r % 2
    tx = 2 * z + 1 - x
    mate = 2 * y + 1 - c
    across = 2 * (1 - y) + c
    diag = 2 * (1 - y) + 1 - c
    peers = (mate, across, diag)
    q = 2 * x + c
    q_mate, q_side, q_diag = 2 * x + 1 - c, 2 * (1 - x) + c, 2 * (1 - x) + 1 - c
    quarter, depth = f_hbm.shape
    width = w_hbm.shape[1]
    tile = 4 * quarter
    pieces = ga.shape[0]
    piece = width // pieces
    half = out_ref.shape[0]
    f32, bf16 = jnp.float32, jnp.bfloat16
    scale = SMOOTHING_SCALE * LOG2E

    def remote(src, dst, ss, rs, dev):
        return pltpu.make_async_remote_copy(
            src_ref=src, dst_ref=dst, send_sem=ss, recv_sem=rs, device_id=dev, device_id_type=MESH
        )

    drains = []

    def push(src, dst, ss, rs, dev):
        remote(src, dst, ss, rs, dev).start()

    def push_drained(src, dst, ss, rs, dev):
        push(src, dst, ss, rs, dev)
        drains.append((src, ss))

    def landed(dst, rs):
        remote(dst, dst, ea_s.at[0, 0], rs, (t, mate)).wait_recv()

    def drained(src, ss):
        remote(src, src, ss, ea_r.at[0, 0], (t, mate)).wait_send()

    f_copy = pltpu.make_async_copy(f_hbm, fv, f_l)
    f_copy.start()
    w_copies = []
    columns = width // wv.shape[0]
    for j in range(wv.shape[0]):
        copy = pltpu.make_async_copy(w_hbm.at[:, j * columns : (j + 1) * columns], wv.at[j], w_l.at[j])
        copy.start()
        w_copies.append(copy)

    barrier = pltpu.get_barrier_semaphore()
    for step in range(nb):
        for row in range(4):
            if step or row:
                pl.semaphore_signal(barrier, inc=1, device_id=((t + step) % nb, (r + row) % 4), device_id_type=MESH)

    meta[r] = jnp.zeros(meta.shape[1:], f32)
    meta[r, 0:1, :] = lab_ref[...].astype(f32)
    meta[r, 1:4, :] = pos_ref[...].astype(f32)
    meta[r, 4:5, :] = wgt_ref[...]
    for s in range(3):
        scored[s] = jnp.broadcast_to((mask_ref[0:1, s : s + 1] > 0).astype(f32), (8, quarter))
    f_copy.wait()
    square = jnp.zeros((quarter, 1), f32)
    for j in range(wv.shape[0]):
        with scope("embed"):
            w_copies[j].wait()
            cut = slice(j * columns, (j + 1) * columns)
            part = dot(fv[...], wv[j]).astype(bf16)
            ea[r, :, cut] = part
            nr[0, :, cut] = part
            wide = part.astype(f32)
            square = square + jnp.sum(wide * wide, axis=1, keepdims=True)
        if j == 0:
            with scope("barrier"):
                pl.semaphore_wait(barrier, 4 * nb - 1)
        for n, peer in ((1, across), (0, mate)):
            push_drained(ea.at[r, :, cut], ea.at[r, :, cut], ea_s.at[n, j], ea_r.at[r, j], (t, peer))
        push_drained(nr.at[0, :, cut], nr.at[1, :, cut], en_s.at[0, j], en_r.at[0, j], ((t + 1) % nb, r))
    meta[r, 5:6, :] = jnp.transpose(jnp.broadcast_to(square, (quarter, 128)))[0:1, :]
    for n, peer in enumerate(peers):
        push_drained(meta.at[r], meta.at[r], ma_s.at[n], ma_r.at[r], (t, peer))
    for s in (1, 2):
        push_drained(meta.at[r], metan.at[s - 1], mn_s.at[s - 1], mn_r.at[s - 1], ((t + s) % nb, r))
    for j in range(wv.shape[0]):
        cut = slice(j * columns, (j + 1) * columns)
        push_drained(nr.at[0, :, cut], nr.at[2, :, cut], en_s.at[1, j], en_r.at[1, j], ((t + 2) % nb, r))

    def block_column(px, pc, i):
        return pl.multiple_of((4 * (2 * pc + i % 2) + 2 * px + i // 2) * 128, 128)

    for n, (px, pc) in enumerate(((x, 1 - c), (1 - x, c), (1 - x, 1 - c))):
        dev = (2 * z + px, 2 * y + pc)
        for i in range(4):
            push_drained(fv.at[:, pl.ds(block_column(px, pc, i), 128)], fc.at[q, i], fc_s.at[n, i], fc_r.at[q, i], dev)
    for i in range(4):
        fc[q, i] = fv[:, pl.ds(block_column(x, c, i), 128)]

    labc[0] = spread_rows(meta[r, 0:1, :])
    for a in range(4):
        stp[a] = jnp.zeros(stp.shape[1:], f32)
        acc[a] = jnp.zeros((quarter, width), f32)
    for s in range(3):
        pul[s] = jnp.zeros((quarter, width), f32)
        cs[s] = jnp.zeros((quarter, 128), f32)

    with scope("rows"):
        for j in range(wv.shape[0]):
            cut = slice(j * columns, (j + 1) * columns)
            landed(ea.at[across, :, cut], ea_r.at[across, j])
            push_drained(ea.at[across, :, cut], ea.at[across, :, cut], ea_s.at[2, j], ea_r.at[across, j], (t, mate))
        for peer in (mate, diag):
            for j in range(wv.shape[0]):
                landed(ea.at[peer, :, j * columns : (j + 1) * columns], ea_r.at[peer, j])
        for peer in peers:
            landed(meta.at[peer], ma_r.at[peer])

    sub = lax.broadcasted_iota(jnp.int32, (SUB, quarter), 0).astype(f32)
    with scope("positives"):
        own_anchors = ea[r]
        own_places = [meta[r, 1 + k : 2 + k, :] for k in range(3)]

        def positives(n, found):
            prod[...] = dot(ea[n], own_anchors, NT)
            sqc[...] = spread_rows(meta[n, 5:6, :])

            def rows(i, found):
                start = pl.multiple_of(i * SUB, SUB)
                d = twice(sqc[pl.ds(start, SUB)]) - 2.0 * prod[pl.ds(start, SUB)]
                base = (n * quarter + i * SUB).astype(f32)
                return tuple(
                    found[k] + by_eights(jnp.where(sub == own_places[k] - base, d, 0.0)) for k in range(3)
                )

            return lax.fori_loop(0, quarter // SUB, rows, found)

        found = lax.fori_loop(0, 4, positives, tuple(jnp.zeros((8, quarter), f32) for _ in range(3)))
        for k in range(3):
            dpr[r, k : k + 1, :] = scale * (jnp.sum(found[k], axis=0, keepdims=True) + SLACK_GAP)
        dpr[r, 3:8, :] = jnp.zeros((5, quarter), f32)
    for n, peer in enumerate(peers):
        push_drained(dpr.at[r], dpr.at[r], d_s.at[n], d_r.at[r], (t, peer))


    def tile_columns(s, block):
        labc[s] = spread_rows(block[0:1, :])
        sqn[s] = scale * spread_rows(block[5:6, :])

    tile_columns(0, meta[r])

    def chunk(s, a):
        prod[...] = dot(nr[s], ea[a], NT)
        on = scored[s, 0:1, :] > 0.0
        tops = [jnp.where(on, dpr[a, k : k + 1, :], -FAR) for k in range(3)]
        names = meta[a, 0:1, :]
        weight = meta[a, 4:5, :] * (1.0 / (3.0 * tile))

        def rows(i, sums):
            at = pl.ds(pl.multiple_of(i * SUB, SUB), SUB)
            spread = twice(sqn[s, at]) - (2.0 * scale) * prod[at]
            spread = jnp.where(twice(labc[s, at]) != names, spread, FAR)
            e, over = [], None
            for k in range(3):
                h = tops[k] - spread
                m = jnp.minimum(h, CEILING)
                e.append(jnp.exp2(m))
                over = h - m if over is None else over + (h - m)
            p = e[0] + e[1] + e[0] * e[1]
            p = p + e[2] + p * e[2]
            u = 1.0 + p
            inv = 1.0 / u
            logs = LN2 * (jnp.log2(u) + over) + (p - (u - 1.0)) * inv
            one = [1.0 + v for v in e]
            last = inv * one[2]
            sig = (e[0] * (last * one[1]), e[1] * (last * one[0]), e[2] * (inv * (one[0] * one[1])))
            coef = (sig[0] + sig[1] + sig[2]) * weight
            low[at] = coef.astype(bf16)
            cs[s, at] += coef[:, :128] + coef[:, 128:]
            return tuple(v + by_eights(w) for v, w in zip(sums, (logs,) + sig))

        zero = jnp.zeros((8, quarter), f32)
        with scope("pairs"):
            sums = lax.fori_loop(0, quarter // SUB, rows, (zero,) * 4)
        for k in range(4):
            stp[a, k] += sums[k]
        with scope("products"):
            pul[s] += dot(low[...], ea[a])
            acc[a] += dot(low[...], nr[s], TN)

    def sums_over_lanes(s):
        return jnp.sum(cs[s], axis=1, keepdims=True)

    def send_term(s):
        tst[s - 1] = (2.0 * (pul[s] - sums_over_lanes(s) * nr[s].astype(f32))).astype(bf16)
        for j in range(pieces):
            term_copy(s, j).start()

    def term_copy(s, j):
        cut = pl.ds(j * piece, piece)
        return remote(
            tst.at[s - 1, :, cut], trec.at[s - 1, :, cut], t_s.at[s - 1, j], t_r.at[s - 1, j], ((t + nb - s) % nb, r)
        )

    def across_copy(j):
        cut = pl.ds(j * piece, piece)
        return remote(ast1.at[:, cut], arec1.at[:, cut], a1_s.at[j], a1_r.at[j], (t, across))

    def step(i, carry):
        s = lax.shift_right_logical(TILE_CODE, 2 * i) % 4
        a = (r + 0 * i) ^ (lax.shift_right_logical(PEER_CODE, 2 * i) % 4)

        def tile_arrives(s):
            for j in range(wv.shape[0]):
                landed(nr.at[s, :, j * columns : (j + 1) * columns], en_r.at[s - 1, j])
            landed(metan.at[s - 1], mn_r.at[s - 1])
            tile_columns(s, metan[s - 1])

        @pl.when(i == 0)
        def _():
            with scope("tile1"):
                tile_arrives(1)

        @pl.when(i == 2)
        def _():
            with scope("distances"):
                for peer in peers:
                    landed(dpr.at[peer], d_r.at[peer])

        @pl.when(i == 7)
        def _():
            with scope("tile2"):
                tile_arrives(2)

        with scope("chunk"):
            chunk(s, a)

        @pl.when(i == 4)
        def _():
            send_term(1)

        @pl.when(i == 7)
        def _():
            hst[...] = (2.0 * acc[diag]).astype(bf16)
            remote(hst, hrec, h_s, h_r, (t, mate)).start()

        @pl.when(i == 8)
        def _():
            landed(hrec, h_r)
            ast1[...] = (2.0 * acc[across] + hrec[...].astype(f32)).astype(bf16)
            for j in range(FIRST):
                across_copy(j).start()

        @pl.when(i == 10)
        def _():
            send_term(2)

        return carry

    with scope("scores"):
        lax.fori_loop(0, STEPS, step, 0)

    for a in range(4):
        for k in range(4):
            st[a, k : k + 1, :] = jnp.sum(stp[a, k], axis=0, keepdims=True)
        st[a, 4:8, :] = jnp.zeros((4, quarter), f32)
    for n, peer in enumerate(peers):
        push_drained(st, strec.at[r], st_s.at[n], st_r.at[r], (t, peer))
    for j in range(FIRST, pieces):
        across_copy(j).start()
    ast0[...] = (2.0 * acc[mate]).astype(bf16)
    push_drained(ast0, arec0, a0_s, a0_r, (t, mate))

    with scope("features"):
        for n in (q_mate, q_side, q_diag):
            for i in range(4):
                landed(fc.at[n, i], fc_r.at[n, i])
        for n in range(4):
            for i in range(4):
                fct[i * 128 : (i + 1) * 128, n * quarter : (n + 1) * quarter] = jnp.transpose(fc[n, i])

    strec[r] = st[...]
    with scope("statistics"):
        for peer in peers:
            landed(strec.at[peer], st_r.at[peer])
    for a in range(4):
        tot[a] = strec[0, a] + strec[1, a] + strec[2, a] + strec[3, a]
    loss_ref[...] = tot[r, 0:1, :] * (1.0 / (SMOOTHING_SCALE * 3.0 * tile))

    wide_sub = lax.broadcasted_iota(jnp.int32, (quarter, quarter), 0).astype(f32)
    cs[1] = jnp.zeros((quarter, 128), f32)

    def listed(a, first):
        wgt = meta[a, 4:5, :] * (1.0 / (3.0 * tile))
        out = jnp.zeros((quarter, quarter), f32)
        for k in range(3):
            hit = meta[a, 1 + k : 2 + k, :] - first == wide_sub
            out = out + jnp.where(hit, tot[a, 1 + k : 2 + k, :] * wgt, 0.0)
        high = out.astype(bf16)
        return out, high, (out - high.astype(f32)).astype(bf16)

    def pulls(n, carry):
        out, high, rest = listed(n, (r * quarter).astype(f32))
        cs[1] += out[:, :128] + out[:, 128:]
        pushed = dot(high, ea[n]) + dot(rest, ea[n])
        out, high, rest = listed(r, (n * quarter).astype(f32))
        drawn = dot(high, ea[n], TN) + dot(rest, ea[n], TN)
        pul[0] -= pushed + drawn
        return carry

    with scope("pulls"):
        lax.fori_loop(0, 4, pulls, 0)
        acc[r] = 2.0 * (acc[r] + pul[0] + (sums_over_lanes(1) - sums_over_lanes(0)) * ea[r].astype(f32))

    def columns_of(j):
        return pl.ds(pl.multiple_of(j * piece, piece), piece)

    def side_copy(j):
        return remote(ga.at[j, q], ga.at[j, q], g_s.at[j, 1], g_r.at[j, q], (tx, r))

    def mate_copy(j):
        return remote(ga.at[j, q], ga.at[j, q], g_s.at[j, 0], g_r.at[j, q], (t, mate))

    def forward_copy(j):
        return remote(ga.at[j, q_side], ga.at[j, q_side], g_s.at[j, 2], g_r.at[j, q_side], (t, mate))

    def part_copy(j):
        return remote(yst.at[j], yrec.at[j], y_s.at[j], y_r.at[j], (t, across))

    def hop(j, i, h):
        return remote(
            pst.at[j, i, h], prec.at[j, z], p_s.at[j, i, h], p_r.at[j, z], (2 * (2 * c + i) + x, 2 * y + h)
        )

    def away(i, h):
        return jnp.logical_or(2 * c + i != z, c != h)

    def gather(j):
        cut = columns_of(j)
        total = acc[r, :, cut] + arec0[:, cut].astype(f32)
        landed(arec1.at[:, cut], a1_r.at[j])
        total = total + arec1[:, cut].astype(f32)
        for s in (1, 2):
            landed(trec.at[s - 1, :, cut], t_r.at[s - 1, j])
            total = total + trec[s - 1, :, cut].astype(f32)
        ga[j, q] = total.astype(bf16)
        side_copy(j).start()
        mate_copy(j).start()

    def multiply(j):
        landed(ga.at[j, q_side], g_r.at[j, q_side])
        forward_copy(j).start()
        for n in (q_mate, q_diag):
            landed(ga.at[j, n], g_r.at[j, n])
        part = dot(fct[...], ga[j].reshape(tile, piece))
        mine = 1.0 - y.astype(f32)
        top, bottom = part[: 4 * half], part[4 * half :]
        yown[j] = jnp.where(y == 0, top, bottom)
        yst[j] = jnp.where(y == 0, bottom, top).astype(bf16)
        part_copy(j).start()

    def scatter(j):
        landed(yrec.at[j], y_r.at[j])
        total = (yown[j] + yrec[j].astype(f32)).astype(bf16)
        for i in range(2):
            for h in range(2):
                pst[j, i, h] = total[(2 * i + h) * half : (2 * i + h + 1) * half]
        for i in range(2):
            for h in range(2):
                @pl.when(away(i, h))
                def _():
                    hop(j, i, h).start()

                @pl.when(jnp.logical_not(away(i, h)))
                def _():
                    prec[j, z] = pst[j, i, h]

    def finish(j):
        for source in range(nb // 2):
            @pl.when(jnp.logical_or(z // 2 != c, z != source))
            def _():
                landed(prec.at[j, source], p_r.at[j, source])
        result = prec[j, 0].astype(f32)
        for source in range(1, nb // 2):
            result = result + prec[j, source].astype(f32)
        out_ref[:, columns_of(j)] = result

    with scope("mate"):
        landed(arec0, a0_r)

    def stage(i, carry):
        for lag, name, work in ((0, "gather", gather), (LAGS[0], "multiply", multiply), (LAGS[1], "scatter", scatter)):
            @pl.when(jnp.logical_and(i >= lag, i < pieces + lag))
            def _():
                with scope(name):
                    work(i - lag)

        return carry

    lax.fori_loop(0, pieces + LAGS[1], stage, 0)

    def close(j, carry):
        with scope("finish"):
            finish(j)
        return carry

    lax.fori_loop(0, pieces, close, 0)

    def drain(j, carry):
        for copy in (side_copy, mate_copy, forward_copy, part_copy):
            copy(j).wait_send()
        for i in range(2):
            for h in range(2):
                @pl.when(away(i, h))
                def _():
                    hop(j, i, h).wait_send()
        return carry

    lax.fori_loop(0, pieces, drain, 0)
    for j in range(pieces):
        term_copy(1, j).wait_send()
        term_copy(2, j).wait_send()
        across_copy(j).wait_send()
    remote(hst, hrec, h_s, h_r, (t, mate)).wait_send()
    for source, semaphore in drains:
        drained(source, semaphore)


def fused(features, head_weight, labels, pos_index, pair_mask, loss_weight):
    quarter, depth = features.shape
    width = head_weight.shape[1]
    nb = lax.axis_size("blk")
    share = depth // (4 * nb)
    f32, bf16 = jnp.float32, jnp.bfloat16
    dma = pltpu.SemaphoreType.DMA
    vmem = pl.BlockSpec(memory_space=pltpu.VMEM)
    hbm = pl.BlockSpec(memory_space=pl.ANY)
    block = (quarter, width)
    small = (8, quarter)
    piece = width // PIECES
    loss, grad = pl.pallas_call(
        kernel,
        out_shape=(jax.ShapeDtypeStruct((1, quarter), f32), jax.ShapeDtypeStruct((share, width), f32)),
        in_specs=[hbm] * 2 + [vmem] * 4,
        out_specs=(vmem, vmem),
        scratch_shapes=[
            pltpu.VMEM((quarter, depth), bf16),
            pltpu.VMEM((3, depth, width // 3), bf16),
            pltpu.VMEM((4,) + block, bf16),
            pltpu.VMEM((3,) + block, bf16),
            pltpu.VMEM((4,) + small, f32),
            pltpu.VMEM((2,) + small, f32),
            pltpu.VMEM((3,) + small, f32),
            pltpu.VMEM((4, 4, quarter, 128), bf16),
            pltpu.VMEM((512, 4 * quarter), bf16),
            pltpu.VMEM((4,) + block, f32),
            pltpu.VMEM((3,) + block, f32),
            pltpu.VMEM((3, quarter, 128), f32),
            pltpu.VMEM((quarter, quarter), f32),
            pltpu.VMEM((quarter, quarter), bf16),
            pltpu.VMEM((4,) + small, f32),
            pltpu.VMEM((quarter, 128), f32),
            pltpu.VMEM((3, quarter, 128), f32),
            pltpu.VMEM((3, quarter, 128), f32),
            pltpu.VMEM((4, 4) + small, f32),
            pltpu.VMEM((4,) + small, f32),
            pltpu.VMEM((4, 4) + small, f32),
            pltpu.VMEM((4,) + small, f32),
            pltpu.VMEM((2,) + block, bf16),
            pltpu.VMEM((2,) + block, bf16),
            pltpu.VMEM(block, bf16),
            pltpu.VMEM(block, bf16),
            pltpu.VMEM(block, bf16),
            pltpu.VMEM(block, bf16),
            pltpu.VMEM(block, bf16),
            pltpu.VMEM(block, bf16),
            pltpu.VMEM((PIECES, 4, quarter, piece), bf16),
            pltpu.VMEM((PIECES, 4 * share, piece), f32),
            pltpu.VMEM((PIECES, 4 * share, piece), bf16),
            pltpu.VMEM((PIECES, 4 * share, piece), bf16),
            pltpu.VMEM((PIECES, 2, 2, share, piece), bf16),
            pltpu.VMEM((PIECES, nb // 2, share, piece), bf16),
            dma(()), dma((3,)), dma((3, 3)), dma((4, 3)), dma((3,)), dma((4,)), dma((2, 3)), dma((2, 3)), dma((2,)), dma((2,)),
            dma((3, 4)), dma((4, 4)), dma((3,)), dma((4,)), dma((2, PIECES)), dma((2, PIECES)), dma(()), dma(()),
            dma((PIECES,)), dma((PIECES,)), dma(()), dma(()), dma((3,)), dma((4,)),
            dma((PIECES, 3)), dma((PIECES, 4)), dma((PIECES,)), dma((PIECES,)), dma((PIECES, 2, 2)), dma((PIECES, nb // 2)),
        ],
        compiler_params=pltpu.CompilerParams(
            collective_id=0, has_side_effects=True, vmem_limit_bytes=56 * 1024 * 1024
        ),
    )(features, head_weight, labels[None, :], pos_index.T, loss_weight[None, :], pair_mask)
    return loss[0], grad


def solution(mesh):
    body = fused if mesh.shape["blk"] == 8 and mesh.shape["rows"] == 4 else local
    return jax.shard_map(
        body,
        mesh=mesh,
        in_specs=(
            P(("blk", "rows"), None),
            P(),
            P(("blk", "rows")),
            P(("blk", "rows"), None),
            P("blk", None),
            P(("blk", "rows")),
        ),
        out_specs=(P(("blk", "rows")), P(("blk", "rows"), None)),
        check_vma=False,
    )
```

```python
import contextlib
import math

import jax
import jax.numpy as jnp
from jax import lax
from jax.experimental import pallas as pl
from jax.experimental.pallas import tpu as pltpu
from jax.sharding import PartitionSpec as P

SMOOTHING_SCALE = 16.0
SLACK_GAP = 0.1


def passed_along(block, axis, distance):
    devices = range(lax.axis_size(axis))
    route = [((i - distance) % len(devices), i) for i in devices]
    return lax.ppermute(block, axis, route)


def score_tile(
    anchors, anchor_sq, anchor_labels, matching_separation, weights, tile_rows, tile_labels, listed
):
    matching_samples = matching_separation.shape[1]
    block_tally = tile_rows.shape[0]
    anchor_count = anchors.shape[0]

    def compute(unused):
        products = lax.dot_general(
            anchors, tile_rows, (((1,), (1,)), ((), ())), preferred_element_type=jnp.float32
        )
        widened = tile_rows.astype(jnp.float32)
        tile_sq = jnp.sum(widened * widened, axis=1)
        couple_separation = anchor_sq[:, None] + tile_sq[None, :] - 2.0 * products
        valid = (anchor_labels[:, None] != tile_labels[None, :]).astype(jnp.float32)
        weighting = weights / (matching_samples * block_tally)
        objective_accrued = jnp.zeros((anchor_count,), jnp.float32)
        coefficient = jnp.zeros((anchor_count, block_tally), jnp.float32)
        totals = []
        for target_slot in range(matching_samples):
            slack_excess = SMOOTHING_SCALE * (
                matching_separation[:, target_slot : target_slot + 1]
                - couple_separation
                + SLACK_GAP
            )
            objective_accrued = objective_accrued + jnp.sum(
                valid * jax.nn.softplus(slack_excess), axis=1
            )
            sigmoids = valid * jax.nn.sigmoid(slack_excess)
            coefficient = coefficient + sigmoids
            totals.append(jnp.sum(sigmoids, axis=1))
        objective_accrued = objective_accrued / (SMOOTHING_SCALE * matching_samples * block_tally)
        coefficient = coefficient * weighting[:, None]
        pos_coef = jnp.stack(totals, axis=1) * weighting[:, None]
        coef_low = coefficient.astype(jnp.bfloat16)
        anchor_grad = 2.0 * jnp.dot(coef_low, tile_rows, preferred_element_type=jnp.float32)
        pulled = lax.dot_general(
            coef_low, anchors, (((0,), (0,)), ((), ())), preferred_element_type=jnp.float32
        )
        col_sums = jnp.sum(coefficient, axis=0)
        tile_grad = 2.0 * (pulled - col_sums[:, None] * widened)
        return (objective_accrued, pos_coef, anchor_grad, tile_grad, coef_low, col_sums)

    def skip(unused):
        return (
            jnp.zeros((anchor_count,), jnp.float32),
            jnp.zeros((anchor_count, matching_samples), jnp.float32),
            jnp.zeros((anchor_count, anchors.shape[1]), jnp.float32),
            jnp.zeros((block_tally, anchors.shape[1]), jnp.float32),
            jnp.zeros((anchor_count, block_tally), jnp.bfloat16),
            jnp.zeros((block_tally,), jnp.float32),
        )

    return lax.cond(listed, compute, skip, 0)


def local(features, head_weight, labels, pos_index, pair_mask, loss_weight):
    embedded = jnp.dot(features, head_weight, preferred_element_type=jnp.float32).astype(
        jnp.bfloat16
    )
    widened = embedded.astype(jnp.float32)
    anchor_sq = jnp.sum(widened * widened, axis=1)
    tile_rows, tile_labels = (
        lax.all_gather(embedded, "rows", axis=0, tiled=True),
        lax.all_gather(labels, "rows", axis=0, tiled=True),
    )
    pos_rows = tile_rows[pos_index]
    pos_wide = pos_rows.astype(jnp.float32)
    pos_sq = jnp.sum(pos_wide * pos_wide, axis=2)
    matching_separation = (
        anchor_sq[:, None]
        + pos_sq
        - 2.0 * jnp.einsum("ad,akd->ak", embedded, pos_rows, preferred_element_type=jnp.float32)
    )
    offsets = pair_mask.shape[1]
    loss_total, coef_total, grad_total, own_term, first_low, first_sums = score_tile(
        embedded,
        anchor_sq,
        labels,
        matching_separation,
        loss_weight,
        tile_rows,
        tile_labels,
        pair_mask[0, 0] > 0,
    )
    received = jnp.zeros_like(own_term)
    walk_rows, walk_labels = (tile_rows, tile_labels)
    for offset in range(1, offsets):
        walk_rows, walk_labels = passed_along((walk_rows, walk_labels), "blk", 1)
        loss_part, coef_part, grad_part, term_part, low_part, sums_part = score_tile(
            embedded,
            anchor_sq,
            labels,
            matching_separation,
            loss_weight,
            walk_rows,
            walk_labels,
            pair_mask[0, offset] > 0,
        )
        loss_total = loss_total + loss_part
        coef_total = coef_total + coef_part
        grad_total = grad_total + grad_part
        received = received + passed_along(term_part.astype(jnp.bfloat16), "blk", -offset).astype(
            term_part.dtype
        )
    grad_total = grad_total - 2.0 * jnp.sum(coef_total[:, :, None] * pos_wide, axis=1)
    pushed = 2.0 * coef_total[:, :, None] * (pos_wide - widened[:, None, :])
    own_term = own_term.at[pos_index.reshape(-1)].add(pushed.reshape(-1, pushed.shape[2]))
    quarter_sum = lax.psum_scatter(own_term + received, "rows", scatter_dimension=0, tiled=True)
    emb_grad = grad_total + quarter_sum
    grad_low = emb_grad.astype(jnp.bfloat16)
    weight_grad = lax.psum_scatter(
        lax.dot_general(
            features, grad_low, (((0,), (0,)), ((), ())), preferred_element_type=jnp.float32
        ),
        ("blk", "rows"),
        scatter_dimension=0,
        tiled=True,
    )
    return (loss_total, weight_grad)


MESH = pl.DeviceIdType.MESH
NT = (((1,), (1,)), ((), ()))
TN = (((0,), (0,)), ((), ()))


def dot(a, b, dims=(((1,), (0,)), ((), ()))):
    return lax.dot_general(a, b, dims, preferred_element_type=jnp.float32)


LOG2E = math.log2(math.e)
LN2 = math.log(2.0)
CEILING = 40.0
FAR = 1e38
PIECES = 6
SUB = 32
TILES = (0, 2, 0, 1, 1, 2)
SIDES = (0, 1, 1, 1, 0, 0)
FIRST = 0
AHEAD = 2
STEPS = len(TILES)
TILE_CODE = sum(s << (2 * i) for i, s in enumerate(TILES))
SIDE_CODE = sum(p << (2 * i) for i, p in enumerate(SIDES))


def last_of(codes, value):
    return max(i for i, code in enumerate(codes) if code == value)


LAGS = (3, 4, 6)


def scope(name):
    return contextlib.nullcontext()


def spread_rows(row):
    return jnp.transpose(jnp.broadcast_to(row, (128, row.shape[1])))


def twice(block):
    return jnp.concatenate([block, block], axis=1)


def by_eights(block):
    total = block[0:8]
    for i in range(1, block.shape[0] // 8):
        total = total + block[8 * i : 8 * i + 8]
    return total


def kernel(
    f_hbm, w_hbm, lab_ref, pos_ref, wgt_ref, mask_ref, loss_ref, out_ref,
    fv, wv, ea, nr, meta, metan, scored, fc, fct, acc, pul, cs, prod, prod2, gram, low, low2, comb, place, pulled, dpr, sqc, labc, sqn, stp, st, strec, tot,
    tst, trec, relay, ast0, arec0, ast1, arec1, hst, hrec, ga, yown, yst, yrec, pst, prec,
    f_l, w_l, ea_s, ea_r, ma_s, ma_r, en_s, en_r, mn_s, mn_r, fc_s, fc_r, d_s, d_r, t_s, t_r, rl_r, a0_s, a0_r, a1_s, a1_r,
    h_s, h_r, st_s, st_r, g_s, g_r, y_s, y_r, p_s, p_r,
):
    nb = lax.axis_size("blk")
    t = lax.axis_index("blk")
    r = lax.axis_index("rows")
    z, x = t // 2, t % 2
    y, c = r // 2, r % 2
    tx = 2 * z + 1 - x
    mate = 2 * y + 1 - c
    across = 2 * (1 - y) + c
    diag = 2 * (1 - y) + 1 - c
    peers = (mate, across, diag)
    q = 2 * x + c
    q_mate, q_side, q_diag = 2 * x + 1 - c, 2 * (1 - x) + c, 2 * (1 - x) + 1 - c
    quarter, depth = f_hbm.shape
    width = w_hbm.shape[1]
    tile = 4 * quarter
    pieces = ga.shape[0]
    piece = width // pieces
    half = out_ref.shape[0]
    f32, bf16 = jnp.float32, jnp.bfloat16
    scale = SMOOTHING_SCALE * LOG2E

    def remote(src, dst, ss, rs, dev):
        return pltpu.make_async_remote_copy(
            src_ref=src, dst_ref=dst, send_sem=ss, recv_sem=rs, device_id=dev, device_id_type=MESH
        )

    drains = []

    def push(src, dst, ss, rs, dev):
        remote(src, dst, ss, rs, dev).start()

    def push_drained(src, dst, ss, rs, dev):
        push(src, dst, ss, rs, dev)
        drains.append((src, ss))

    def landed(dst, rs):
        remote(dst, dst, ea_s.at[0, 0], rs, (t, mate)).wait_recv()

    def drained(src, ss):
        remote(src, src, ss, ea_r.at[0, 0], (t, mate)).wait_send()

    columns = width // wv.shape[0]
    f_copy = pltpu.make_async_copy(f_hbm, fv, f_l)
    w_copies = [
        pltpu.make_async_copy(w_hbm.at[:, j * columns : (j + 1) * columns], wv.at[j], w_l.at[j])
        for j in range(wv.shape[0])
    ]
    f_copy.start()
    w_copies[0].start()

    barrier = pltpu.get_barrier_semaphore()
    for step in range(nb):
        for row in range(4):
            if step or row:
                pl.semaphore_signal(barrier, inc=1, device_id=((t + step) % nb, (r + row) % 4), device_id_type=MESH)

    meta[r] = jnp.zeros(meta.shape[1:], f32)
    meta[r, 0:1, :] = lab_ref[...].astype(f32)
    meta[r, 1:4, :] = pos_ref[...].astype(f32)
    meta[r, 4:5, :] = wgt_ref[...]
    for s in range(3):
        scored[s] = jnp.broadcast_to((mask_ref[0:1, s : s + 1] > 0).astype(f32), (8, quarter))

    def along_z(j):
        cut = slice(j * columns, (j + 1) * columns)
        return remote(nr.at[0, :, cut], nr.at[2, :, cut], en_s.at[1, j], en_r.at[1, j], ((t + 2) % nb, r))

    def along_x(held, j):
        cut = slice(j * columns, (j + 1) * columns)
        return remote(nr.at[held, :, cut], nr.at[1, :, cut], en_s.at[0, j], en_r.at[0, j], (tx, r))

    def block_column(px, pc, i):
        return pl.multiple_of((4 * (2 * pc + i % 2) + 2 * px + i // 2) * 128, 128)

    def send_features(i):
        for n, (px, pc) in enumerate(((x, 1 - c), (1 - x, c), (1 - x, 1 - c))):
            dev = (2 * z + px, 2 * y + pc)
            push_drained(fv.at[:, pl.ds(block_column(px, pc, i), 128)], fc.at[q, i], fc_s.at[n, i], fc_r.at[q, i], dev)

    f_copy.wait()
    for copy in w_copies[1:]:
        copy.start()
    square = jnp.zeros((quarter, 1), f32)
    for j in range(wv.shape[0]):
        with scope("embed"):
            w_copies[j].wait()
            cut = slice(j * columns, (j + 1) * columns)
            part = dot(fv[...], wv[j]).astype(bf16)
            ea[r, :, cut] = part
            nr[0, :, cut] = part
            wide = part.astype(f32)
            square = square + jnp.sum(wide * wide, axis=1, keepdims=True)
        if j == 0:
            with scope("barrier"):
                pl.semaphore_wait(barrier, 4 * nb - 1)
        for n, peer in ((1, across), (0, mate)):
            push_drained(ea.at[r, :, cut], ea.at[r, :, cut], ea_s.at[n, j], ea_r.at[r, j], (t, peer))
        along_z(j).start()
        if j == 0:
            send_features(0)

        @pl.when(x == 0)
        def _():
            along_x(0, j).start()

    meta[r, 5:6, :] = jnp.transpose(jnp.broadcast_to(square, (quarter, 128)))[0:1, :]
    for n, peer in enumerate(peers):
        push_drained(meta.at[r], meta.at[r], ma_s.at[n], ma_r.at[r], (t, peer))
    for s in (1, 2):
        push_drained(meta.at[r], metan.at[s - 1], mn_s.at[s - 1], mn_r.at[s - 1], ((t + s) % nb, r))
    for i in range(4):
        fc[q, i] = fv[:, pl.ds(block_column(x, c, i), 128)]

    labc[0] = spread_rows(meta[r, 0:1, :])
    for a in range(4):
        stp[a] = jnp.zeros(stp.shape[1:], f32)
        acc[a] = jnp.zeros((quarter, width), f32)
    for s in range(3):
        pul[s] = jnp.zeros((quarter, width), f32)
        cs[s] = jnp.zeros((quarter, 128), f32)

    @pl.when(x == 1)
    def _():
        trec[0] = jnp.zeros((quarter, width), bf16)

    sub = lax.broadcasted_iota(jnp.int32, (SUB, quarter), 0).astype(f32)

    def side_rows(side):
        return ea[pl.ds(2 * side, 2)].reshape(2 * quarter, width)

    def positives(side, found):
        gram[...] = dot(side_rows(side), ea[r], NT)
        places = [meta[r, 1 + k : 2 + k, :] for k in range(3)]
        for h in range(2):
            sqc[h * quarter : (h + 1) * quarter] = spread_rows(meta[2 * side + h, 5:6, :])

        def rows(i, found):
            at = pl.ds(pl.multiple_of(i * SUB, SUB), SUB)
            d = twice(sqc[at]) - 2.0 * gram[at]
            base = (side * 2 * quarter + i * SUB).astype(f32)
            return tuple(found[k] + by_eights(jnp.where(sub == places[k] - base, d, 0.0)) for k in range(3))

        return lax.fori_loop(0, 2 * quarter // SUB, rows, found)

    with scope("own_rows"):
        for j in range(wv.shape[0]):
            landed(ea.at[mate, :, j * columns : (j + 1) * columns], ea_r.at[mate, j])
        landed(meta.at[mate], ma_r.at[mate])
        found = positives(y, tuple(jnp.zeros((8, quarter), f32) for _ in range(3)))
        prod[...] = dot(nr[0], side_rows(y), NT)

    def tile_columns(s, block):
        labc[s] = spread_rows(block[0:1, :])
        sqn[s] = scale * spread_rows(block[5:6, :])

    tile_columns(0, meta[r])
    with scope("rows"):
        for j in range(wv.shape[0]):
            cut = slice(j * columns, (j + 1) * columns)
            landed(ea.at[across, :, cut], ea_r.at[across, j])
            push_drained(ea.at[across, :, cut], ea.at[across, :, cut], ea_s.at[2, j], ea_r.at[across, j], (t, mate))

            @pl.when(x == 1)
            def _():
                landed(nr.at[2, :, cut], en_r.at[1, j])
                along_x(2, j).start()

        for j in range(wv.shape[0]):
            landed(ea.at[diag, :, j * columns : (j + 1) * columns], ea_r.at[diag, j])
        for peer in (across, diag):
            landed(meta.at[peer], ma_r.at[peer])

    for i in range(1, 4):
        send_features(i)
    with scope("positives"):
        found = positives(1 - y, found)
        for k in range(3):
            dpr[r, k : k + 1, :] = scale * (jnp.sum(found[k], axis=0, keepdims=True) + SLACK_GAP)
        dpr[r, 3:8, :] = jnp.zeros((5, quarter), f32)
    for n, peer in enumerate(peers):
        push_drained(dpr.at[r], dpr.at[r], d_s.at[n], d_r.at[r], (t, peer))


    def pairs(s, side, prod, low):
        on = scored[s, 0:1, :] > 0.0
        for g in range(2):
            a = 2 * side + g
            cut = slice(g * quarter, (g + 1) * quarter)
            tops = [jnp.where(on, dpr[a, k : k + 1, :], -FAR) for k in range(3)]
            names = meta[a, 0:1, :]
            weight = meta[a, 4:5, :] * (1.0 / (3.0 * tile))
            sums = [jnp.zeros((8, quarter), f32)] * 4
            for i in range(quarter // SUB):
                at = slice(i * SUB, (i + 1) * SUB)
                spread = twice(sqn[s, at]) - (2.0 * scale) * prod[at, cut]
                spread = jnp.where(twice(labc[s, at]) != names, spread, FAR)
                e, over = [], None
                for k in range(3):
                    h = tops[k] - spread
                    m = jnp.minimum(h, CEILING)
                    e.append(jnp.exp2(m))
                    over = h - m if over is None else over + (h - m)
                p = e[0] + e[1] + e[0] * e[1]
                p = p + e[2] + p * e[2]
                u = 1.0 + p
                inv = 1.0 / u
                logs = LN2 * (jnp.log2(u) + over) + (p - (u - 1.0)) * inv
                one = [1.0 + v for v in e]
                last = inv * one[2]
                sig = (e[0] * (last * one[1]), e[1] * (last * one[0]), e[2] * (inv * (one[0] * one[1])))
                coef = (sig[0] + sig[1] + sig[2]) * weight
                low[at, cut] = coef.astype(bf16)
                cs[s, at] += coef[:, :128] + coef[:, 128:]
                sums = [v + by_eights(w) for v, w in zip(sums, (logs,) + sig)]
            for k in range(4):
                stp[2 * side + g, k] += sums[k]

    def products(s, side, low):
        pul[s] += dot(low[...], side_rows(side))
        acc[pl.ds(2 * side, 2)] += dot(low[...], nr[s], TN).reshape(2, quarter, width)

    def sums_over_lanes(s):
        return jnp.sum(cs[s], axis=1, keepdims=True)

    def term_value(s):
        return 2.0 * (pul[s] - sums_over_lanes(s) * nr[s].astype(f32))

    def columns_of(j):
        return pl.ds(pl.multiple_of(j * piece, piece), piece)

    def term_copy(s, j):
        cut = columns_of(j)
        return remote(
            tst.at[s - 1, :, cut], trec.at[s - 1, :, cut], t_s.at[s - 1, j], t_r.at[s - 1, j], ((t + nb - s) % nb, r)
        )

    def relay_copy(j):
        cut = columns_of(j)
        return remote(tst.at[0, :, cut], relay.at[:, cut], t_s.at[0, j], rl_r.at[j], (tx, r))

    def send_first():
        tst[0] = term_value(1).astype(bf16)
        for j in range(pieces):
            pl.when(x == 0)(lambda: relay_copy(j).start())
            pl.when(x == 1)(lambda: term_copy(1, j).start())

    def send_second():
        pul[2] = term_value(2)

        @pl.when(x == 0)
        def _():
            tst[1] = pul[2].astype(bf16)
            for j in range(pieces):
                term_copy(2, j).start()

    def merge(j):
        cut = columns_of(j)
        landed(relay.at[:, cut], rl_r.at[j])
        tst[1, :, cut] = (pul[2, :, cut] + relay[:, cut].astype(f32)).astype(bf16)
        term_copy(2, j).start()

    def across_copy(j):
        cut = columns_of(j)
        return remote(ast1.at[:, cut], arec1.at[:, cut], a1_s.at[j], a1_r.at[j], (t, across))

    def tile_of(i):
        return lax.shift_right_logical(TILE_CODE, 2 * i) % 4

    def side_of(i):
        return (y + lax.shift_right_logical(SIDE_CODE, 2 * i)) % 2

    def tile_arrives(s):
        for j in range(wv.shape[0]):
            @pl.when(jnp.logical_or(s == 1, x == 0))
            def _():
                landed(nr.at[s, :, j * columns : (j + 1) * columns], en_r.at[s - 1, j])

        landed(metan.at[s - 1], mn_r.at[s - 1])
        tile_columns(s, metan[s - 1])

    def send_hst():
        hst[...] = (2.0 * acc[diag]).astype(bf16)
        remote(hst, hrec, h_s, h_r, (t, mate)).start()

    def send_ast():
        landed(hrec, h_r)
        ast1[...] = (2.0 * acc[across] + hrec[...].astype(f32)).astype(bf16)
        for j in range(FIRST):
            across_copy(j).start()

    events = (
        (last_of(TILES, 1) + 1, send_first),
        (last_of(TILES, 2) + 1, send_second),
        (last_of(SIDES, 1) + 1, send_hst),
        (last_of(SIDES, 1) + 2, send_ast),
    )

    def step(i, held, coming, low, before):
        @pl.when(i == SIDES.index(1))
        def _():
            with scope("distances"):
                for peer in (across, diag):
                    landed(dpr.at[peer], d_r.at[peer])

        @pl.when(i == TILES.index(1) - 1)
        def _():
            with scope("tile1"):
                tile_arrives(1)

        with scope("chunk"):
            later = jnp.minimum(i + 1, STEPS - 1)
            earlier = jnp.maximum(i - 1, 0)
            coming[...] = dot(nr[tile_of(later)], side_rows(side_of(later)), NT)
            products(tile_of(earlier), side_of(earlier), before)
            pairs(tile_of(i), side_of(i), held, low)

        for when, event in events:
            if when < STEPS:
                pl.when(i == when)(event)

    def two_steps(n, carry):
        step(2 * n, prod, prod2, low, low2)
        step(2 * n + 1, prod2, prod, low2, low)
        return carry

    with scope("tile2"):
        tile_arrives(2)
    low2[...] = jnp.zeros(low2.shape, bf16)
    with scope("distance"):
        landed(dpr.at[mate], d_r.at[mate])
    with scope("scores"):
        lax.fori_loop(0, STEPS // 2, two_steps, 0)

    for a in range(4):
        for k in range(4):
            st[a, k : k + 1, :] = jnp.sum(stp[a, k], axis=0, keepdims=True)
        st[a, 4:8, :] = jnp.zeros((4, quarter), f32)
    for n, peer in enumerate(peers):
        push_drained(st, strec.at[r], st_s.at[n], st_r.at[r], (t, peer))
    with scope("last"):
        for j in range(FIRST, pieces):
            across_copy(j).start()
        products(tile_of(STEPS - 1), side_of(STEPS - 1), low2)
        for when, event in events:
            if when == STEPS:
                event()
        ast0[...] = (2.0 * acc[mate]).astype(bf16)
        push_drained(ast0, arec0, a0_s, a0_r, (t, mate))

    with scope("features"):
        for n in (q_mate, q_side, q_diag):
            for i in range(4):
                landed(fc.at[n, i], fc_r.at[n, i])
        for n in range(4):
            for i in range(4):
                fct[i * 128 : (i + 1) * 128, n * quarter : (n + 1) * quarter] = jnp.transpose(fc[n, i])

    strec[r] = st[...]
    with scope("statistics"):
        for peer in peers:
            landed(strec.at[peer], st_r.at[peer])
    with scope("merged"):
        for j in range(AHEAD):
            pl.when(x == 1)(lambda: merge(j))
    for a in range(4):
        tot[a] = strec[0, a] + strec[1, a] + strec[2, a] + strec[3, a]
    loss_ref[...] = tot[r, 0:1, :] * (1.0 / (SMOOTHING_SCALE * 3.0 * tile))

    with scope("pulls"):
        row_sub = lax.broadcasted_iota(jnp.int32, (SUB, quarter), 0).astype(f32)
        lane = lax.broadcasted_iota(jnp.int32, (SUB, quarter), 1).astype(f32)
        share = 1.0 / (3.0 * tile)
        for k in range(3):
            place[k] = spread_rows(meta[r, 1 + k : 2 + k, :])
            pulled[k] = spread_rows(tot[r, 1 + k : 2 + k, :] * meta[r, 4:5, :] * share)

        def listed(i, carry):
            at = pl.ds(pl.multiple_of(i * SUB, SUB), SUB)
            first = (r * quarter + i * SUB).astype(f32)
            gained = jnp.zeros((SUB, 128), f32)
            for n in range(4):
                given = jnp.zeros((SUB, quarter), f32)
                wgt = meta[n, 4:5, :] * share
                for k in range(3):
                    hit = row_sub == meta[n, 1 + k : 2 + k, :] - first
                    given = given + jnp.where(hit, tot[n, 1 + k : 2 + k, :] * wgt, 0.0)
                gained = gained + (given[:, :128] + given[:, 128:])
                for k in range(3):
                    hit = lane == twice(place[k, at]) - float(n * quarter)
                    given = given + jnp.where(hit, twice(pulled[k, at]), 0.0)
                high = given.astype(bf16)
                comb[0, at, n * quarter : (n + 1) * quarter] = high
                comb[1, at, n * quarter : (n + 1) * quarter] = (given - high.astype(f32)).astype(bf16)
            cs[1, at] = gained
            return carry

        lax.fori_loop(0, quarter // SUB, listed, 0)
        rows_all = ea[...].reshape(tile, width)
        net = pul[0] - dot(comb[0], rows_all) - dot(comb[1], rows_all)
        acc[r] = 2.0 * (acc[r] + net + (sums_over_lanes(1) - sums_over_lanes(0)) * ea[r].astype(f32))

    def side_copy(j):
        return remote(ga.at[j, q], ga.at[j, q], g_s.at[j, 1], g_r.at[j, q], (tx, r))

    def mate_copy(j):
        return remote(ga.at[j, q], ga.at[j, q], g_s.at[j, 0], g_r.at[j, q], (t, mate))

    def forward_copy(j):
        return remote(ga.at[j, q_side], ga.at[j, q_side], g_s.at[j, 2], g_r.at[j, q_side], (t, mate))

    def part_copy(j):
        return remote(yst.at[j], yrec.at[j], y_s.at[j], y_r.at[j], (t, across))

    def hop(j, i, h):
        return remote(
            pst.at[j, i, h], prec.at[j, z], p_s.at[j, i, h], p_r.at[j, z], (2 * (2 * c + i) + x, 2 * y + h)
        )

    def away(i, h):
        return jnp.logical_or(2 * c + i != z, c != h)

    def gather(j):
        cut = columns_of(j)
        total = acc[r, :, cut] + arec0[:, cut].astype(f32)
        landed(arec1.at[:, cut], a1_r.at[j])
        total = total + arec1[:, cut].astype(f32)
        @pl.when(x == 0)
        def _():
            landed(trec.at[0, :, cut], t_r.at[0, j])

        landed(trec.at[1, :, cut], t_r.at[1, j])
        total = total + trec[0, :, cut].astype(f32) + trec[1, :, cut].astype(f32)
        ga[j, q] = total.astype(bf16)
        side_copy(j).start()
        mate_copy(j).start()

    def forward(j):
        landed(ga.at[j, q_side], g_r.at[j, q_side])
        forward_copy(j).start()

    def multiply(j):
        for n in (q_mate, q_diag):
            landed(ga.at[j, n], g_r.at[j, n])
        part = dot(fct[...], ga[j].reshape(tile, piece))
        top, bottom = part[: 4 * half], part[4 * half :]
        yown[j] = jnp.where(y == 0, top, bottom)
        yst[j] = jnp.where(y == 0, bottom, top).astype(bf16)
        part_copy(j).start()

    def scatter(j):
        landed(yrec.at[j], y_r.at[j])
        total = (yown[j] + yrec[j].astype(f32)).astype(bf16)
        for i in range(2):
            for h in range(2):
                pst[j, i, h] = total[(2 * i + h) * half : (2 * i + h + 1) * half]
        for i in range(2):
            for h in range(2):
                @pl.when(away(i, h))
                def _():
                    hop(j, i, h).start()

                @pl.when(jnp.logical_not(away(i, h)))
                def _():
                    prec[j, z] = pst[j, i, h]

    def finish(j):
        for source in range(nb // 2):
            @pl.when(jnp.logical_or(z // 2 != c, z != source))
            def _():
                landed(prec.at[j, source], p_r.at[j, source])
        result = prec[j, 0].astype(f32)
        for source in range(1, nb // 2):
            result = result + prec[j, source].astype(f32)
        out_ref[:, columns_of(j)] = result

    with scope("mate"):
        landed(arec0, a0_r)

    def stages(i, carry):
        @pl.when(jnp.logical_and(x == 1, i + AHEAD < pieces))
        def _():
            with scope("merge"):
                merge(i + AHEAD)

        for lag, name, work in zip((0,) + LAGS, ("gather", "forward", "multiply", "scatter"), (gather, forward, multiply, scatter)):
            @pl.when(jnp.logical_and(i >= lag, i < pieces + lag))
            def _():
                with scope(name):
                    work(i - lag)

        return carry

    lax.fori_loop(0, pieces + LAGS[-1], stages, 0)

    def close(j, carry):
        with scope("finish"):
            finish(j)
        return carry

    lax.fori_loop(0, pieces, close, 0)

    def drain(j, carry):
        for copy in (side_copy, mate_copy, forward_copy, part_copy):
            copy(j).wait_send()
        for i in range(2):
            for h in range(2):
                @pl.when(away(i, h))
                def _():
                    hop(j, i, h).wait_send()
        return carry

    lax.fori_loop(0, pieces, drain, 0)
    for j in range(pieces):
        term_copy(1, j).wait_send()
        term_copy(2, j).wait_send()
        across_copy(j).wait_send()
    for j in range(wv.shape[0]):
        along_z(j).wait_send()
        along_x(0, j).wait_send()
    remote(hst, hrec, h_s, h_r, (t, mate)).wait_send()
    for source, semaphore in drains:
        drained(source, semaphore)


def fused(features, head_weight, labels, pos_index, pair_mask, loss_weight):
    quarter, depth = features.shape
    width = head_weight.shape[1]
    nb = lax.axis_size("blk")
    share = depth // (4 * nb)
    f32, bf16 = jnp.float32, jnp.bfloat16
    dma = pltpu.SemaphoreType.DMA
    vmem = pl.BlockSpec(memory_space=pltpu.VMEM)
    hbm = pl.BlockSpec(memory_space=pl.ANY)
    block = (quarter, width)
    small = (8, quarter)
    piece = width // PIECES
    loss, grad = pl.pallas_call(
        kernel,
        out_shape=(jax.ShapeDtypeStruct((1, quarter), f32), jax.ShapeDtypeStruct((share, width), f32)),
        in_specs=[hbm] * 2 + [vmem] * 4,
        out_specs=(vmem, vmem),
        scratch_shapes=[
            pltpu.VMEM((quarter, depth), bf16),
            pltpu.VMEM((3, depth, width // 3), bf16),
            pltpu.VMEM((4,) + block, bf16),
            pltpu.VMEM((3,) + block, bf16),
            pltpu.VMEM((4,) + small, f32),
            pltpu.VMEM((2,) + small, f32),
            pltpu.VMEM((3,) + small, f32),
            pltpu.VMEM((4, 4, quarter, 128), bf16),
            pltpu.VMEM((512, 4 * quarter), bf16),
            pltpu.VMEM((4,) + block, f32),
            pltpu.VMEM((3,) + block, f32),
            pltpu.VMEM((3, quarter, 128), f32),
            pltpu.VMEM((quarter, 2 * quarter), f32),
            pltpu.VMEM((quarter, 2 * quarter), f32),
            pltpu.VMEM((2 * quarter, quarter), f32),
            pltpu.VMEM((quarter, 2 * quarter), bf16),
            pltpu.VMEM((quarter, 2 * quarter), bf16),
            pltpu.VMEM((2, quarter, 4 * quarter), bf16),
            pltpu.VMEM((3, quarter, 128), f32),
            pltpu.VMEM((3, quarter, 128), f32),
            pltpu.VMEM((4,) + small, f32),
            pltpu.VMEM((2 * quarter, 128), f32),
            pltpu.VMEM((3, quarter, 128), f32),
            pltpu.VMEM((3, quarter, 128), f32),
            pltpu.VMEM((4, 4) + small, f32),
            pltpu.VMEM((4,) + small, f32),
            pltpu.VMEM((4, 4) + small, f32),
            pltpu.VMEM((4,) + small, f32),
            pltpu.VMEM((2,) + block, bf16),
            pltpu.VMEM((2,) + block, bf16),
            pltpu.VMEM(block, bf16),
            pltpu.VMEM(block, bf16),
            pltpu.VMEM(block, bf16),
            pltpu.VMEM(block, bf16),
            pltpu.VMEM(block, bf16),
            pltpu.VMEM(block, bf16),
            pltpu.VMEM(block, bf16),
            pltpu.VMEM((PIECES, 4, quarter, piece), bf16),
            pltpu.VMEM((PIECES, 4 * share, piece), f32),
            pltpu.VMEM((PIECES, 4 * share, piece), bf16),
            pltpu.VMEM((PIECES, 4 * share, piece), bf16),
            pltpu.VMEM((PIECES, 2, 2, share, piece), bf16),
            pltpu.VMEM((PIECES, nb // 2, share, piece), bf16),
            dma(()), dma((3,)), dma((3, 3)), dma((4, 3)), dma((3,)), dma((4,)), dma((2, 3)), dma((2, 3)), dma((2,)), dma((2,)),
            dma((3, 4)), dma((4, 4)), dma((3,)), dma((4,)), dma((2, PIECES)), dma((2, PIECES)), dma((PIECES,)), dma(()), dma(()),
            dma((PIECES,)), dma((PIECES,)), dma(()), dma(()), dma((3,)), dma((4,)),
            dma((PIECES, 3)), dma((PIECES, 4)), dma((PIECES,)), dma((PIECES,)), dma((PIECES, 2, 2)), dma((PIECES, nb // 2)),
        ],
        compiler_params=pltpu.CompilerParams(
            collective_id=0, has_side_effects=True, vmem_limit_bytes=56 * 1024 * 1024
        ),
    )(features, head_weight, labels[None, :], pos_index.T, loss_weight[None, :], pair_mask)
    return loss[0], grad


def solution(mesh):
    body = fused if mesh.shape["blk"] == 8 and mesh.shape["rows"] == 4 else local
    return jax.shard_map(
        body,
        mesh=mesh,
        in_specs=(
            P(("blk", "rows"), None),
            P(),
            P(("blk", "rows")),
            P(("blk", "rows"), None),
            P("blk", None),
            P(("blk", "rows")),
        ),
        out_specs=(P(("blk", "rows")), P(("blk", "rows"), None)),
        check_vma=False,
    )
```

```python
import contextlib
import math

import jax
import jax.numpy as jnp
from jax import lax
from jax.experimental import pallas as pl
from jax.experimental.pallas import tpu as pltpu
from jax.sharding import PartitionSpec as P

SMOOTHING_SCALE = 16.0
SLACK_GAP = 0.1


def passed_along(block, axis, distance):
    devices = range(lax.axis_size(axis))
    route = [((i - distance) % len(devices), i) for i in devices]
    return lax.ppermute(block, axis, route)


def score_tile(
    anchors, anchor_sq, anchor_labels, matching_separation, weights, tile_rows, tile_labels, listed
):
    matching_samples = matching_separation.shape[1]
    block_tally = tile_rows.shape[0]
    anchor_count = anchors.shape[0]

    def compute(unused):
        products = lax.dot_general(
            anchors, tile_rows, (((1,), (1,)), ((), ())), preferred_element_type=jnp.float32
        )
        widened = tile_rows.astype(jnp.float32)
        tile_sq = jnp.sum(widened * widened, axis=1)
        couple_separation = anchor_sq[:, None] + tile_sq[None, :] - 2.0 * products
        valid = (anchor_labels[:, None] != tile_labels[None, :]).astype(jnp.float32)
        weighting = weights / (matching_samples * block_tally)
        objective_accrued = jnp.zeros((anchor_count,), jnp.float32)
        coefficient = jnp.zeros((anchor_count, block_tally), jnp.float32)
        totals = []
        for target_slot in range(matching_samples):
            slack_excess = SMOOTHING_SCALE * (
                matching_separation[:, target_slot : target_slot + 1]
                - couple_separation
                + SLACK_GAP
            )
            objective_accrued = objective_accrued + jnp.sum(
                valid * jax.nn.softplus(slack_excess), axis=1
            )
            sigmoids = valid * jax.nn.sigmoid(slack_excess)
            coefficient = coefficient + sigmoids
            totals.append(jnp.sum(sigmoids, axis=1))
        objective_accrued = objective_accrued / (SMOOTHING_SCALE * matching_samples * block_tally)
        coefficient = coefficient * weighting[:, None]
        pos_coef = jnp.stack(totals, axis=1) * weighting[:, None]
        coef_low = coefficient.astype(jnp.bfloat16)
        anchor_grad = 2.0 * jnp.dot(coef_low, tile_rows, preferred_element_type=jnp.float32)
        pulled = lax.dot_general(
            coef_low, anchors, (((0,), (0,)), ((), ())), preferred_element_type=jnp.float32
        )
        col_sums = jnp.sum(coefficient, axis=0)
        tile_grad = 2.0 * (pulled - col_sums[:, None] * widened)
        return (objective_accrued, pos_coef, anchor_grad, tile_grad, coef_low, col_sums)

    def skip(unused):
        return (
            jnp.zeros((anchor_count,), jnp.float32),
            jnp.zeros((anchor_count, matching_samples), jnp.float32),
            jnp.zeros((anchor_count, anchors.shape[1]), jnp.float32),
            jnp.zeros((block_tally, anchors.shape[1]), jnp.float32),
            jnp.zeros((anchor_count, block_tally), jnp.bfloat16),
            jnp.zeros((block_tally,), jnp.float32),
        )

    return lax.cond(listed, compute, skip, 0)


def local(features, head_weight, labels, pos_index, pair_mask, loss_weight):
    embedded = jnp.dot(features, head_weight, preferred_element_type=jnp.float32).astype(
        jnp.bfloat16
    )
    widened = embedded.astype(jnp.float32)
    anchor_sq = jnp.sum(widened * widened, axis=1)
    tile_rows, tile_labels = (
        lax.all_gather(embedded, "rows", axis=0, tiled=True),
        lax.all_gather(labels, "rows", axis=0, tiled=True),
    )
    pos_rows = tile_rows[pos_index]
    pos_wide = pos_rows.astype(jnp.float32)
    pos_sq = jnp.sum(pos_wide * pos_wide, axis=2)
    matching_separation = (
        anchor_sq[:, None]
        + pos_sq
        - 2.0 * jnp.einsum("ad,akd->ak", embedded, pos_rows, preferred_element_type=jnp.float32)
    )
    offsets = pair_mask.shape[1]
    loss_total, coef_total, grad_total, own_term, first_low, first_sums = score_tile(
        embedded,
        anchor_sq,
        labels,
        matching_separation,
        loss_weight,
        tile_rows,
        tile_labels,
        pair_mask[0, 0] > 0,
    )
    received = jnp.zeros_like(own_term)
    walk_rows, walk_labels = (tile_rows, tile_labels)
    for offset in range(1, offsets):
        walk_rows, walk_labels = passed_along((walk_rows, walk_labels), "blk", 1)
        loss_part, coef_part, grad_part, term_part, low_part, sums_part = score_tile(
            embedded,
            anchor_sq,
            labels,
            matching_separation,
            loss_weight,
            walk_rows,
            walk_labels,
            pair_mask[0, offset] > 0,
        )
        loss_total = loss_total + loss_part
        coef_total = coef_total + coef_part
        grad_total = grad_total + grad_part
        received = received + passed_along(term_part.astype(jnp.bfloat16), "blk", -offset).astype(
            term_part.dtype
        )
    grad_total = grad_total - 2.0 * jnp.sum(coef_total[:, :, None] * pos_wide, axis=1)
    pushed = 2.0 * coef_total[:, :, None] * (pos_wide - widened[:, None, :])
    own_term = own_term.at[pos_index.reshape(-1)].add(pushed.reshape(-1, pushed.shape[2]))
    quarter_sum = lax.psum_scatter(own_term + received, "rows", scatter_dimension=0, tiled=True)
    emb_grad = grad_total + quarter_sum
    grad_low = emb_grad.astype(jnp.bfloat16)
    weight_grad = lax.psum_scatter(
        lax.dot_general(
            features, grad_low, (((0,), (0,)), ((), ())), preferred_element_type=jnp.float32
        ),
        ("blk", "rows"),
        scatter_dimension=0,
        tiled=True,
    )
    return (loss_total, weight_grad)


MESH = pl.DeviceIdType.MESH
NT = (((1,), (1,)), ((), ()))
TN = (((0,), (0,)), ((), ()))


def dot(a, b, dims=(((1,), (0,)), ((), ()))):
    return lax.dot_general(a, b, dims, preferred_element_type=jnp.float32)


LOG2E = math.log2(math.e)
LN2 = math.log(2.0)
CEILING = 40.0
FAR = 1e38
PIECES = 6
SUB = 32
TILES = (0, 2, 1, 1, 0, 2)
SIDES = (0, 1, 1, 0, 1, 0)
AHEAD = 4
STEPS = len(TILES)
TILE_CODE = sum(s << (2 * i) for i, s in enumerate(TILES))
SIDE_CODE = sum(p << (2 * i) for i, p in enumerate(SIDES))


def last_of(codes, value):
    return max(i for i, code in enumerate(codes) if code == value)


LAGS = (3, 4, 6)


def scope(name):
    return contextlib.nullcontext()


def spread_rows(row):
    return jnp.transpose(jnp.broadcast_to(row, (128, row.shape[1])))


def twice(block):
    return jnp.concatenate([block, block], axis=1)


def by_eights(block):
    total = block[0:8]
    for i in range(1, block.shape[0] // 8):
        total = total + block[8 * i : 8 * i + 8]
    return total


def kernel(
    f_hbm, w_hbm, lab_hbm, pos_hbm, wgt_hbm, mask_hbm, loss_hbm, out_hbm,
    lab_ref, pos_ref, wgt_ref, mask_ref, loss_ref, out_ref, fv, wv, ea, nr, meta, metan, scored, fc, fct, acc, pul, cs, prod, prod2, gram, low, low2, comb, place, pulled, dpr, sqc, labc, sqn, stp, st, strec, tot,
    tst, trec, relay, ast0, arec0, ast1, arec1, hst, hrec, ga, yown, yst, yrec, pst, prec,
    f_l, w_l, ea_s, ea_r, ma_s, ma_r, en_s, en_r, mn_s, mn_r, fc_s, fc_r, d_s, d_r, t_s, t_r, rl_r, a0_s, a0_r, a1_s, a1_r,
    h_s, h_r, st_s, st_r, g_s, g_r, y_s, y_r, p_s, p_r, l_s, o_s, i_s,
):
    nb = lax.axis_size("blk")
    t = lax.axis_index("blk")
    r = lax.axis_index("rows")
    z, x = t // 2, t % 2
    y, c = r // 2, r % 2
    tx = 2 * z + 1 - x
    mate = 2 * y + 1 - c
    across = 2 * (1 - y) + c
    diag = 2 * (1 - y) + 1 - c
    peers = (mate, across, diag)
    q = 2 * x + c
    q_mate, q_side, q_diag = 2 * x + 1 - c, 2 * (1 - x) + c, 2 * (1 - x) + 1 - c
    quarter, depth = f_hbm.shape
    width = w_hbm.shape[1]
    tile = 4 * quarter
    pieces = ga.shape[0]
    piece = width // pieces
    half = out_hbm.shape[0]
    f32, bf16 = jnp.float32, jnp.bfloat16
    scale = SMOOTHING_SCALE * LOG2E

    def remote(src, dst, ss, rs, dev):
        return pltpu.make_async_remote_copy(
            src_ref=src, dst_ref=dst, send_sem=ss, recv_sem=rs, device_id=dev, device_id_type=MESH
        )

    drains = []

    def push(src, dst, ss, rs, dev):
        remote(src, dst, ss, rs, dev).start()

    def push_drained(src, dst, ss, rs, dev):
        push(src, dst, ss, rs, dev)
        drains.append((src, ss))

    def landed(dst, rs):
        remote(dst, dst, ea_s.at[0, 0], rs, (t, mate)).wait_recv()

    def drained(src, ss):
        remote(src, src, ss, ea_r.at[0, 0], (t, mate)).wait_send()

    columns = width // wv.shape[0]
    f_copy = pltpu.make_async_copy(f_hbm, fv, f_l)
    w_copies = [
        pltpu.make_async_copy(w_hbm.at[:, j * columns : (j + 1) * columns], wv.at[j], w_l.at[j])
        for j in range(wv.shape[0])
    ]
    f_copy.start()
    w_copies[0].start()
    small_copies = [
        pltpu.make_async_copy(source, target, i_s.at[n])
        for n, (source, target) in enumerate(
            ((lab_hbm, lab_ref), (pos_hbm, pos_ref), (wgt_hbm, wgt_ref), (mask_hbm, mask_ref))
        )
    ]
    for copy in small_copies:
        copy.start()

    barrier = pltpu.get_barrier_semaphore()
    for step in range(nb):
        for row in range(4):
            if step or row:
                pl.semaphore_signal(barrier, inc=1, device_id=((t + step) % nb, (r + row) % 4), device_id_type=MESH)

    with scope("small"):
        for copy in small_copies:
            copy.wait()
    meta[r] = jnp.zeros(meta.shape[1:], f32)
    meta[r, 0:1, :] = lab_ref[...].astype(f32)
    meta[r, 1:4, :] = pos_ref[...].astype(f32)
    meta[r, 4:5, :] = wgt_ref[...]
    for s in range(3):
        scored[s] = jnp.broadcast_to((mask_ref[0:1, s : s + 1] > 0).astype(f32), (8, quarter))

    def along_z(j):
        cut = slice(j * columns, (j + 1) * columns)
        return remote(nr.at[0, :, cut], nr.at[2, :, cut], en_s.at[1, j], en_r.at[1, j], ((t + 2) % nb, r))

    def along_x(held, j):
        cut = slice(j * columns, (j + 1) * columns)
        return remote(nr.at[held, :, cut], nr.at[1, :, cut], en_s.at[0, j], en_r.at[0, j], (tx, r))

    def block_column(px, pc, i):
        return pl.multiple_of((4 * (2 * pc + i % 2) + 2 * px + i // 2) * 128, 128)

    def send_features(i):
        for n, (px, pc) in enumerate(((x, 1 - c), (1 - x, c), (1 - x, 1 - c))):
            dev = (2 * z + px, 2 * y + pc)
            push_drained(fv.at[:, pl.ds(block_column(px, pc, i), 128)], fc.at[q, i], fc_s.at[n, i], fc_r.at[q, i], dev)

    f_copy.wait()
    for copy in w_copies[1:]:
        copy.start()
    square = jnp.zeros((quarter, 1), f32)
    for j in range(wv.shape[0]):
        with scope("embed"):
            w_copies[j].wait()
            cut = slice(j * columns, (j + 1) * columns)
            part = dot(fv[...], wv[j]).astype(bf16)
            ea[r, :, cut] = part
            nr[0, :, cut] = part
            wide = part.astype(f32)
            square = square + jnp.sum(wide * wide, axis=1, keepdims=True)
        if j == 0:
            with scope("barrier"):
                pl.semaphore_wait(barrier, 4 * nb - 1)
        for n, peer in ((1, across), (0, mate)):
            push_drained(ea.at[r, :, cut], ea.at[r, :, cut], ea_s.at[n, j], ea_r.at[r, j], (t, peer))
        along_z(j).start()
        if j == 0:
            send_features(0)

        @pl.when(x == 0)
        def _():
            along_x(0, j).start()

    meta[r, 5:6, :] = jnp.transpose(jnp.broadcast_to(square, (quarter, 128)))[0:1, :]
    for n, peer in enumerate(peers):
        push_drained(meta.at[r], meta.at[r], ma_s.at[n], ma_r.at[r], (t, peer))
    for s in (1, 2):
        push_drained(meta.at[r], metan.at[s - 1], mn_s.at[s - 1], mn_r.at[s - 1], ((t + s) % nb, r))
    for i in range(4):
        fc[q, i] = fv[:, pl.ds(block_column(x, c, i), 128)]

    labc[0] = spread_rows(meta[r, 0:1, :])
    for a in range(4):
        stp[a] = jnp.zeros(stp.shape[1:], f32)
        acc[a] = jnp.zeros((quarter, width), f32)
    for s in range(3):
        pul[s] = jnp.zeros((quarter, width), f32)
        cs[s] = jnp.zeros((quarter, 128), f32)

    @pl.when(x == 1)
    def _():
        trec[0] = jnp.zeros((quarter, width), bf16)

    sub = lax.broadcasted_iota(jnp.int32, (SUB, quarter), 0).astype(f32)

    def side_rows(side):
        return ea[pl.ds(2 * side, 2)].reshape(2 * quarter, width)

    def positives(side, found):
        gram[...] = dot(side_rows(side), ea[r], NT)
        places = [meta[r, 1 + k : 2 + k, :] for k in range(3)]
        for h in range(2):
            sqc[h * quarter : (h + 1) * quarter] = spread_rows(meta[2 * side + h, 5:6, :])

        def rows(i, found):
            at = pl.ds(pl.multiple_of(i * SUB, SUB), SUB)
            d = twice(sqc[at]) - 2.0 * gram[at]
            base = (side * 2 * quarter + i * SUB).astype(f32)
            return tuple(found[k] + by_eights(jnp.where(sub == places[k] - base, d, 0.0)) for k in range(3))

        return lax.fori_loop(0, 2 * quarter // SUB, rows, found)

    with scope("own_rows"):
        for j in range(wv.shape[0]):
            landed(ea.at[mate, :, j * columns : (j + 1) * columns], ea_r.at[mate, j])
        landed(meta.at[mate], ma_r.at[mate])
        found = positives(y, tuple(jnp.zeros((8, quarter), f32) for _ in range(3)))
        prod[...] = dot(nr[0], side_rows(y), NT)

    def tile_columns(s, block):
        labc[s] = spread_rows(block[0:1, :])
        sqn[s] = scale * spread_rows(block[5:6, :])

    tile_columns(0, meta[r])
    with scope("rows"):
        for j in range(wv.shape[0]):
            cut = slice(j * columns, (j + 1) * columns)
            landed(ea.at[across, :, cut], ea_r.at[across, j])
            push_drained(ea.at[across, :, cut], ea.at[across, :, cut], ea_s.at[2, j], ea_r.at[across, j], (t, mate))

            @pl.when(x == 1)
            def _():
                landed(nr.at[2, :, cut], en_r.at[1, j])
                along_x(2, j).start()

        for j in range(wv.shape[0]):
            landed(ea.at[diag, :, j * columns : (j + 1) * columns], ea_r.at[diag, j])
        for peer in (across, diag):
            landed(meta.at[peer], ma_r.at[peer])

    for i in range(1, 4):
        send_features(i)
    with scope("positives"):
        found = positives(1 - y, found)
        for k in range(3):
            dpr[r, k : k + 1, :] = scale * (jnp.sum(found[k], axis=0, keepdims=True) + SLACK_GAP)
        dpr[r, 3:8, :] = jnp.zeros((5, quarter), f32)
    for n, peer in enumerate(peers):
        push_drained(dpr.at[r], dpr.at[r], d_s.at[n], d_r.at[r], (t, peer))


    def pairs(s, side, prod, low, beside=()):
        beside = list(beside)
        on = scored[s, 0:1, :] > 0.0
        for g in range(2):
            a = 2 * side + g
            cut = slice(g * quarter, (g + 1) * quarter)
            tops = [jnp.where(on, dpr[a, k : k + 1, :], -FAR) for k in range(3)]
            names = meta[a, 0:1, :]
            weight = meta[a, 4:5, :] * (1.0 / (3.0 * tile))
            sums = [jnp.zeros((8, quarter), f32)] * 4
            for i in range(quarter // SUB):
                at = slice(i * SUB, (i + 1) * SUB)
                spread = twice(sqn[s, at]) - (2.0 * scale) * prod[at, cut]
                spread = jnp.where(twice(labc[s, at]) != names, spread, FAR)
                e, over = [], None
                for k in range(3):
                    h = tops[k] - spread
                    m = jnp.minimum(h, CEILING)
                    e.append(jnp.exp2(m))
                    over = h - m if over is None else over + (h - m)
                one = [1.0 + v for v in e]
                p = (e[0] + one[0] * e[1]) * one[2] + e[2]
                u = 1.0 + p
                inv = 1.0 / u
                logs = LN2 * (jnp.log2(u) + over) + (p - (u - 1.0)) * inv
                last = inv * one[2]
                sig = (e[0] * (last * one[1]), e[1] * (last * one[0]), e[2] * (inv * (one[0] * one[1])))
                coef = (sig[0] + sig[1] + sig[2]) * weight
                low[at, cut] = coef.astype(bf16)
                cs[s, at] += coef[:, :128] + coef[:, 128:]
                sums = [v + by_eights(w) for v, w in zip(sums, (logs,) + sig)]
                if i % 2 == 1 and beside:
                    beside.pop(0)()
            for k in range(4):
                stp[2 * side + g, k] += sums[k]

    def product_parts(s, side, low):
        def pulled_part(n):
            cut = slice(n * quarter, (n + 1) * quarter)
            pul[s, :, cut] += dot(low[...], ea[pl.ds(2 * side, 2), :, cut].reshape(2 * quarter, quarter))

        def gained_part(g):
            acc[2 * side + g] += dot(low[:, g * quarter : (g + 1) * quarter], nr[s], TN)

        return [lambda n=n: pulled_part(n) for n in range(width // quarter)] + [lambda g=g: gained_part(g) for g in range(2)]

    def coming_parts(s, side, coming):
        def part(g):
            coming[:, g * quarter : (g + 1) * quarter] = dot(nr[s], ea[2 * side + g], NT)

        return [lambda g=g: part(g) for g in range(2)]

    def products(s, side, low):
        pul[s] += dot(low[...], side_rows(side))
        acc[pl.ds(2 * side, 2)] += dot(low[...], nr[s], TN).reshape(2, quarter, width)

    def sums_over_lanes(s):
        return jnp.sum(cs[s], axis=1, keepdims=True)

    def term_value(s):
        return 2.0 * (pul[s] - sums_over_lanes(s) * nr[s].astype(f32))

    def columns_of(j):
        return pl.ds(pl.multiple_of(j * piece, piece), piece)

    def term_copy(s, j):
        cut = columns_of(j)
        return remote(
            tst.at[s - 1, :, cut], trec.at[s - 1, :, cut], t_s.at[s - 1, j], t_r.at[s - 1, j], ((t + nb - s) % nb, r)
        )

    def relay_copy(j):
        cut = columns_of(j)
        return remote(tst.at[0, :, cut], relay.at[:, cut], t_s.at[0, j], rl_r.at[j], (tx, r))

    def send_first():
        tst[0] = term_value(1).astype(bf16)
        for j in range(pieces):
            pl.when(x == 0)(lambda: relay_copy(j).start())
            pl.when(x == 1)(lambda: term_copy(1, j).start())

    def send_second():
        pul[2] = term_value(2)

        @pl.when(x == 0)
        def _():
            tst[1] = pul[2].astype(bf16)
            for j in range(pieces):
                term_copy(2, j).start()

    def merge(j):
        cut = columns_of(j)
        landed(relay.at[:, cut], rl_r.at[j])
        tst[1, :, cut] = (pul[2, :, cut] + relay[:, cut].astype(f32)).astype(bf16)
        term_copy(2, j).start()

    def merge_on_x1(j):
        pl.when(x == 1)(lambda: merge(j))

    def across_copy(j):
        cut = columns_of(j)
        return remote(ast1.at[:, cut], arec1.at[:, cut], a1_s.at[j], a1_r.at[j], (t, across))

    def tile_of(i):
        return lax.shift_right_logical(TILE_CODE, 2 * i) % 4

    def side_of(i):
        return (y + lax.shift_right_logical(SIDE_CODE, 2 * i)) % 2

    def tile_arrives(s):
        for j in range(wv.shape[0]):
            @pl.when(jnp.logical_or(s == 1, x == 0))
            def _():
                landed(nr.at[s, :, j * columns : (j + 1) * columns], en_r.at[s - 1, j])

        landed(metan.at[s - 1], mn_r.at[s - 1])
        tile_columns(s, metan[s - 1])

    def send_hst():
        hst[...] = (2.0 * acc[diag]).astype(bf16)
        remote(hst, hrec, h_s, h_r, (t, mate)).start()

    def send_ast():
        landed(hrec, h_r)
        ast1[...] = (2.0 * acc[across] + hrec[...].astype(f32)).astype(bf16)
        for j in range(pieces):
            across_copy(j).start()

    def step(i, held, coming, low, before):
        @pl.when(i == SIDES.index(1))
        def _():
            with scope("distances"):
                for peer in (across, diag):
                    landed(dpr.at[peer], d_r.at[peer])

        @pl.when(i == TILES.index(1) - 1)
        def _():
            with scope("tile1"):
                tile_arrives(1)

        with scope("chunk"):
            later = jnp.minimum(i + 1, STEPS - 1)
            earlier = jnp.maximum(i - 1, 0)
            beside = product_parts(tile_of(earlier), side_of(earlier), before)
            beside += coming_parts(tile_of(later), side_of(later), coming)
            pairs(tile_of(i), side_of(i), held, low, beside)

    def closing_step(i, held, coming, low, before):
        with scope("chunk"):
            if i + 1 < STEPS:
                coming[...] = dot(nr[TILES[i + 1]], side_rows(side_of(i + 1)), NT)
            products(TILES[i - 1], side_of(i - 1), before)
            if i == last_of(TILES, 1) + 1:
                send_first()
            if i == last_of(SIDES, 1) + 1:
                send_hst()
            pairs(TILES[i], side_of(i), held, low)

    def two_steps(n, carry):
        step(2 * n, prod, prod2, low, low2)
        step(2 * n + 1, prod2, prod, low2, low)
        return carry

    with scope("tile2"):
        tile_arrives(2)
    low2[...] = jnp.zeros(low2.shape, bf16)
    with scope("distance"):
        landed(dpr.at[mate], d_r.at[mate])
    with scope("scores"):
        lax.fori_loop(0, STEPS // 2 - 1, two_steps, 0)
        closing_step(STEPS - 2, prod, prod2, low, low2)
        closing_step(STEPS - 1, prod2, prod, low2, low)

    for a in range(4):
        for k in range(4):
            st[a, k : k + 1, :] = jnp.sum(stp[a, k], axis=0, keepdims=True)
        st[a, 4:8, :] = jnp.zeros((4, quarter), f32)
    for n, peer in enumerate(peers):
        push_drained(st, strec.at[r], st_s.at[n], st_r.at[r], (t, peer))
    with scope("last"):
        products(TILES[STEPS - 1], side_of(STEPS - 1), low2)
        send_second()
        merge_on_x1(0)
        send_ast()
        merge_on_x1(1)
        ast0[...] = (2.0 * acc[mate]).astype(bf16)
        push_drained(ast0, arec0, a0_s, a0_r, (t, mate))

    with scope("features"):
        for n in (q_mate, q_side, q_diag):
            for i in range(4):
                landed(fc.at[n, i], fc_r.at[n, i])
        for n in range(4):
            for i in range(4):
                fct[i * 128 : (i + 1) * 128, n * quarter : (n + 1) * quarter] = jnp.transpose(fc[n, i])

    strec[r] = st[...]
    merge_on_x1(2)
    with scope("statistics"):
        for peer in peers:
            landed(strec.at[peer], st_r.at[peer])
    with scope("merged"):
        merge_on_x1(3)
    for a in range(4):
        tot[a] = strec[0, a] + strec[1, a] + strec[2, a] + strec[3, a]
    loss_ref[...] = tot[r, 0:1, :] * (1.0 / (SMOOTHING_SCALE * 3.0 * tile))
    pltpu.make_async_copy(loss_ref, loss_hbm, l_s).start()

    with scope("pulls"):
        row_sub = lax.broadcasted_iota(jnp.int32, (SUB, quarter), 0).astype(f32)
        lane = lax.broadcasted_iota(jnp.int32, (SUB, quarter), 1).astype(f32)
        share = 1.0 / (3.0 * tile)
        for k in range(3):
            place[k] = spread_rows(meta[r, 1 + k : 2 + k, :])
            pulled[k] = spread_rows(tot[r, 1 + k : 2 + k, :] * meta[r, 4:5, :] * share)

        def listed(i, carry):
            at = pl.ds(pl.multiple_of(i * SUB, SUB), SUB)
            first = (r * quarter + i * SUB).astype(f32)
            gained = jnp.zeros((SUB, 128), f32)
            for n in range(4):
                given = jnp.zeros((SUB, quarter), f32)
                wgt = meta[n, 4:5, :] * share
                for k in range(3):
                    hit = row_sub == meta[n, 1 + k : 2 + k, :] - first
                    given = given + jnp.where(hit, tot[n, 1 + k : 2 + k, :] * wgt, 0.0)
                gained = gained + (given[:, :128] + given[:, 128:])
                for k in range(3):
                    hit = lane == twice(place[k, at]) - float(n * quarter)
                    given = given + jnp.where(hit, twice(pulled[k, at]), 0.0)
                high = given.astype(bf16)
                comb[0, at, n * quarter : (n + 1) * quarter] = high
                comb[1, at, n * quarter : (n + 1) * quarter] = (given - high.astype(f32)).astype(bf16)
            cs[1, at] = gained
            return carry

        lax.fori_loop(0, quarter // SUB, listed, 0)
        rows_all = ea[...].reshape(tile, width)
        net = pul[0] - dot(comb[0], rows_all) - dot(comb[1], rows_all)
        acc[r] = 2.0 * (acc[r] + net + (sums_over_lanes(1) - sums_over_lanes(0)) * ea[r].astype(f32))

    def side_copy(j):
        return remote(ga.at[j, q], ga.at[j, q], g_s.at[j, 1], g_r.at[j, q], (tx, r))

    def mate_copy(j):
        return remote(ga.at[j, q], ga.at[j, q], g_s.at[j, 0], g_r.at[j, q], (t, mate))

    def forward_copy(j):
        return remote(ga.at[j, q_side], ga.at[j, q_side], g_s.at[j, 2], g_r.at[j, q_side], (t, mate))

    def part_copy(j):
        return remote(yst.at[j], yrec.at[j], y_s.at[j], y_r.at[j], (t, across))

    def hop(j, i, h):
        return remote(
            pst.at[j, i, h], prec.at[j, z], p_s.at[j, i, h], p_r.at[j, z], (2 * (2 * c + i) + x, 2 * y + h)
        )

    def away(i, h):
        return jnp.logical_or(2 * c + i != z, c != h)

    def gather(j):
        cut = columns_of(j)
        total = acc[r, :, cut] + arec0[:, cut].astype(f32)
        landed(arec1.at[:, cut], a1_r.at[j])
        total = total + arec1[:, cut].astype(f32)
        @pl.when(x == 0)
        def _():
            landed(trec.at[0, :, cut], t_r.at[0, j])

        landed(trec.at[1, :, cut], t_r.at[1, j])
        total = total + trec[0, :, cut].astype(f32) + trec[1, :, cut].astype(f32)
        ga[j, q] = total.astype(bf16)
        side_copy(j).start()
        mate_copy(j).start()

    def forward(j):
        landed(ga.at[j, q_side], g_r.at[j, q_side])
        forward_copy(j).start()

    def multiply(j):
        for n in (q_mate, q_diag):
            landed(ga.at[j, n], g_r.at[j, n])
        part = dot(fct[...], ga[j].reshape(tile, piece))
        top, bottom = part[: 4 * half], part[4 * half :]
        yown[j] = jnp.where(y == 0, top, bottom)
        yst[j] = jnp.where(y == 0, bottom, top).astype(bf16)
        part_copy(j).start()

    def scatter(j):
        landed(yrec.at[j], y_r.at[j])
        total = (yown[j] + yrec[j].astype(f32)).astype(bf16)
        for i in range(2):
            for h in range(2):
                pst[j, i, h] = total[(2 * i + h) * half : (2 * i + h + 1) * half]
        for i in range(2):
            for h in range(2):
                @pl.when(away(i, h))
                def _():
                    hop(j, i, h).start()

                @pl.when(jnp.logical_not(away(i, h)))
                def _():
                    prec[j, z] = pst[j, i, h]

    def result_copy(j):
        return pltpu.make_async_copy(out_ref.at[:, columns_of(j)], out_hbm.at[:, columns_of(j)], o_s.at[j])

    def finish(j):
        for source in range(nb // 2):
            @pl.when(jnp.logical_or(z // 2 != c, z != source))
            def _():
                landed(prec.at[j, source], p_r.at[j, source])
        result = prec[j, 0].astype(f32)
        for source in range(1, nb // 2):
            result = result + prec[j, source].astype(f32)
        out_ref[:, columns_of(j)] = result
        result_copy(j).start()

    with scope("mate"):
        landed(arec0, a0_r)

    def stages(i, carry):
        @pl.when(jnp.logical_and(x == 1, i + AHEAD < pieces))
        def _():
            with scope("merge"):
                merge(i + AHEAD)

        for lag, name, work in zip((0,) + LAGS, ("gather", "forward", "multiply", "scatter"), (gather, forward, multiply, scatter)):
            @pl.when(jnp.logical_and(i >= lag, i < pieces + lag))
            def _():
                with scope(name):
                    work(i - lag)

        return carry

    lax.fori_loop(0, pieces + LAGS[-1], stages, 0)

    def close(j, carry):
        with scope("finish"):
            finish(j)
        return carry

    lax.fori_loop(0, pieces, close, 0)

    def drain(j, carry):
        result_copy(j).wait()
        for copy in (side_copy, mate_copy, forward_copy, part_copy):
            copy(j).wait_send()
        for i in range(2):
            for h in range(2):
                @pl.when(away(i, h))
                def _():
                    hop(j, i, h).wait_send()
        return carry

    with scope("drain"):
        pltpu.make_async_copy(loss_ref, loss_hbm, l_s).wait()
        lax.fori_loop(0, pieces, drain, 0)
        for j in range(pieces):
            term_copy(1, j).wait_send()
            term_copy(2, j).wait_send()
            across_copy(j).wait_send()
        for j in range(wv.shape[0]):
            along_z(j).wait_send()
            along_x(0, j).wait_send()
        remote(hst, hrec, h_s, h_r, (t, mate)).wait_send()
        for source, semaphore in drains:
            drained(source, semaphore)


def results(loss_ref, grad_ref, loss_out, grad_out):
    loss_out[...] = loss_ref[0]
    grad_out[...] = grad_ref[...]


def fused(features, head_weight, labels, pos_index, pair_mask, loss_weight):
    quarter, depth = features.shape
    width = head_weight.shape[1]
    nb = lax.axis_size("blk")
    share = depth // (4 * nb)
    f32, bf16 = jnp.float32, jnp.bfloat16
    dma = pltpu.SemaphoreType.DMA
    vmem = pl.BlockSpec(memory_space=pltpu.VMEM)
    hbm = pl.BlockSpec(memory_space=pl.ANY)
    block = (quarter, width)
    small = (8, quarter)
    piece = width // PIECES
    loss, grad = pl.pallas_call(
        kernel,
        out_shape=(jax.ShapeDtypeStruct((1, quarter), f32), jax.ShapeDtypeStruct((share, width), f32)),
        in_specs=[hbm] * 6,
        out_specs=(hbm, hbm),
        scratch_shapes=[
            pltpu.VMEM((1, quarter), jnp.int32),
            pltpu.VMEM(pos_index.shape[::-1], jnp.int32),
            pltpu.VMEM((1, quarter), f32),
            pltpu.VMEM(pair_mask.shape, jnp.int32),
            pltpu.VMEM((1, quarter), f32),
            pltpu.VMEM((share, width), f32),
            pltpu.VMEM((quarter, depth), bf16),
            pltpu.VMEM((3, depth, width // 3), bf16),
            pltpu.VMEM((4,) + block, bf16),
            pltpu.VMEM((3,) + block, bf16),
            pltpu.VMEM((4,) + small, f32),
            pltpu.VMEM((2,) + small, f32),
            pltpu.VMEM((3,) + small, f32),
            pltpu.VMEM((4, 4, quarter, 128), bf16),
            pltpu.VMEM((512, 4 * quarter), bf16),
            pltpu.VMEM((4,) + block, f32),
            pltpu.VMEM((3,) + block, f32),
            pltpu.VMEM((3, quarter, 128), f32),
            pltpu.VMEM((quarter, 2 * quarter), f32),
            pltpu.VMEM((quarter, 2 * quarter), f32),
            pltpu.VMEM((2 * quarter, quarter), f32),
            pltpu.VMEM((quarter, 2 * quarter), bf16),
            pltpu.VMEM((quarter, 2 * quarter), bf16),
            pltpu.VMEM((2, quarter, 4 * quarter), bf16),
            pltpu.VMEM((3, quarter, 128), f32),
            pltpu.VMEM((3, quarter, 128), f32),
            pltpu.VMEM((4,) + small, f32),
            pltpu.VMEM((2 * quarter, 128), f32),
            pltpu.VMEM((3, quarter, 128), f32),
            pltpu.VMEM((3, quarter, 128), f32),
            pltpu.VMEM((4, 4) + small, f32),
            pltpu.VMEM((4,) + small, f32),
            pltpu.VMEM((4, 4) + small, f32),
            pltpu.VMEM((4,) + small, f32),
            pltpu.VMEM((2,) + block, bf16),
            pltpu.VMEM((2,) + block, bf16),
            pltpu.VMEM(block, bf16),
            pltpu.VMEM(block, bf16),
            pltpu.VMEM(block, bf16),
            pltpu.VMEM(block, bf16),
            pltpu.VMEM(block, bf16),
            pltpu.VMEM(block, bf16),
            pltpu.VMEM(block, bf16),
            pltpu.VMEM((PIECES, 4, quarter, piece), bf16),
            pltpu.VMEM((PIECES, 4 * share, piece), f32),
            pltpu.VMEM((PIECES, 4 * share, piece), bf16),
            pltpu.VMEM((PIECES, 4 * share, piece), bf16),
            pltpu.VMEM((PIECES, 2, 2, share, piece), bf16),
            pltpu.VMEM((PIECES, nb // 2, share, piece), bf16),
            dma(()), dma((3,)), dma((3, 3)), dma((4, 3)), dma((3,)), dma((4,)), dma((2, 3)), dma((2, 3)), dma((2,)), dma((2,)),
            dma((3, 4)), dma((4, 4)), dma((3,)), dma((4,)), dma((2, PIECES)), dma((2, PIECES)), dma((PIECES,)), dma(()), dma(()),
            dma((PIECES,)), dma((PIECES,)), dma(()), dma(()), dma((3,)), dma((4,)),
            dma((PIECES, 3)), dma((PIECES, 4)), dma((PIECES,)), dma((PIECES,)), dma((PIECES, 2, 2)), dma((PIECES, nb // 2)), dma(()), dma((PIECES,)), dma((4,)),
        ],
        compiler_params=pltpu.CompilerParams(
            collective_id=0, has_side_effects=True, vmem_limit_bytes=56 * 1024 * 1024
        ),
    )(features, head_weight, labels[None, :], pos_index.T, loss_weight[None, :], pair_mask)
    return pl.pallas_call(
        results,
        out_shape=(jax.ShapeDtypeStruct((quarter,), f32), jax.ShapeDtypeStruct((share, width), f32)),
        in_specs=[vmem] * 2,
        out_specs=(vmem, vmem),
    )(loss, grad)


def solution(mesh):
    body = fused if mesh.shape["blk"] == 8 and mesh.shape["rows"] == 4 else local
    return jax.shard_map(
        body,
        mesh=mesh,
        in_specs=(
            P(("blk", "rows"), None),
            P(),
            P(("blk", "rows")),
            P(("blk", "rows"), None),
            P("blk", None),
            P(("blk", "rows")),
        ),
        out_specs=(P(("blk", "rows")), P(("blk", "rows"), None)),
        check_vma=False,
    )
```

```python
import contextlib
import math

import jax
import jax.numpy as jnp
from jax import lax
from jax.experimental import pallas as pl
from jax.experimental.pallas import tpu as pltpu
from jax.sharding import PartitionSpec as P

SMOOTHING_SCALE = 16.0
SLACK_GAP = 0.1


def passed_along(block, axis, distance):
    devices = range(lax.axis_size(axis))
    route = [((i - distance) % len(devices), i) for i in devices]
    return lax.ppermute(block, axis, route)


def score_tile(
    anchors, anchor_sq, anchor_labels, matching_separation, weights, tile_rows, tile_labels, listed
):
    matching_samples = matching_separation.shape[1]
    block_tally = tile_rows.shape[0]
    anchor_count = anchors.shape[0]

    def compute(unused):
        products = lax.dot_general(
            anchors, tile_rows, (((1,), (1,)), ((), ())), preferred_element_type=jnp.float32
        )
        widened = tile_rows.astype(jnp.float32)
        tile_sq = jnp.sum(widened * widened, axis=1)
        couple_separation = anchor_sq[:, None] + tile_sq[None, :] - 2.0 * products
        valid = (anchor_labels[:, None] != tile_labels[None, :]).astype(jnp.float32)
        weighting = weights / (matching_samples * block_tally)
        objective_accrued = jnp.zeros((anchor_count,), jnp.float32)
        coefficient = jnp.zeros((anchor_count, block_tally), jnp.float32)
        totals = []
        for target_slot in range(matching_samples):
            slack_excess = SMOOTHING_SCALE * (
                matching_separation[:, target_slot : target_slot + 1]
                - couple_separation
                + SLACK_GAP
            )
            objective_accrued = objective_accrued + jnp.sum(
                valid * jax.nn.softplus(slack_excess), axis=1
            )
            sigmoids = valid * jax.nn.sigmoid(slack_excess)
            coefficient = coefficient + sigmoids
            totals.append(jnp.sum(sigmoids, axis=1))
        objective_accrued = objective_accrued / (SMOOTHING_SCALE * matching_samples * block_tally)
        coefficient = coefficient * weighting[:, None]
        pos_coef = jnp.stack(totals, axis=1) * weighting[:, None]
        coef_low = coefficient.astype(jnp.bfloat16)
        anchor_grad = 2.0 * jnp.dot(coef_low, tile_rows, preferred_element_type=jnp.float32)
        pulled = lax.dot_general(
            coef_low, anchors, (((0,), (0,)), ((), ())), preferred_element_type=jnp.float32
        )
        col_sums = jnp.sum(coefficient, axis=0)
        tile_grad = 2.0 * (pulled - col_sums[:, None] * widened)
        return (objective_accrued, pos_coef, anchor_grad, tile_grad, coef_low, col_sums)

    def skip(unused):
        return (
            jnp.zeros((anchor_count,), jnp.float32),
            jnp.zeros((anchor_count, matching_samples), jnp.float32),
            jnp.zeros((anchor_count, anchors.shape[1]), jnp.float32),
            jnp.zeros((block_tally, anchors.shape[1]), jnp.float32),
            jnp.zeros((anchor_count, block_tally), jnp.bfloat16),
            jnp.zeros((block_tally,), jnp.float32),
        )

    return lax.cond(listed, compute, skip, 0)


def local(features, head_weight, labels, pos_index, pair_mask, loss_weight):
    embedded = jnp.dot(features, head_weight, preferred_element_type=jnp.float32).astype(
        jnp.bfloat16
    )
    widened = embedded.astype(jnp.float32)
    anchor_sq = jnp.sum(widened * widened, axis=1)
    tile_rows, tile_labels = (
        lax.all_gather(embedded, "rows", axis=0, tiled=True),
        lax.all_gather(labels, "rows", axis=0, tiled=True),
    )
    pos_rows = tile_rows[pos_index]
    pos_wide = pos_rows.astype(jnp.float32)
    pos_sq = jnp.sum(pos_wide * pos_wide, axis=2)
    matching_separation = (
        anchor_sq[:, None]
        + pos_sq
        - 2.0 * jnp.einsum("ad,akd->ak", embedded, pos_rows, preferred_element_type=jnp.float32)
    )
    offsets = pair_mask.shape[1]
    loss_total, coef_total, grad_total, own_term, first_low, first_sums = score_tile(
        embedded,
        anchor_sq,
        labels,
        matching_separation,
        loss_weight,
        tile_rows,
        tile_labels,
        pair_mask[0, 0] > 0,
    )
    received = jnp.zeros_like(own_term)
    walk_rows, walk_labels = (tile_rows, tile_labels)
    for offset in range(1, offsets):
        walk_rows, walk_labels = passed_along((walk_rows, walk_labels), "blk", 1)
        loss_part, coef_part, grad_part, term_part, low_part, sums_part = score_tile(
            embedded,
            anchor_sq,
            labels,
            matching_separation,
            loss_weight,
            walk_rows,
            walk_labels,
            pair_mask[0, offset] > 0,
        )
        loss_total = loss_total + loss_part
        coef_total = coef_total + coef_part
        grad_total = grad_total + grad_part
        received = received + passed_along(term_part.astype(jnp.bfloat16), "blk", -offset).astype(
            term_part.dtype
        )
    grad_total = grad_total - 2.0 * jnp.sum(coef_total[:, :, None] * pos_wide, axis=1)
    pushed = 2.0 * coef_total[:, :, None] * (pos_wide - widened[:, None, :])
    own_term = own_term.at[pos_index.reshape(-1)].add(pushed.reshape(-1, pushed.shape[2]))
    quarter_sum = lax.psum_scatter(own_term + received, "rows", scatter_dimension=0, tiled=True)
    emb_grad = grad_total + quarter_sum
    grad_low = emb_grad.astype(jnp.bfloat16)
    weight_grad = lax.psum_scatter(
        lax.dot_general(
            features, grad_low, (((0,), (0,)), ((), ())), preferred_element_type=jnp.float32
        ),
        ("blk", "rows"),
        scatter_dimension=0,
        tiled=True,
    )
    return (loss_total, weight_grad)


MESH = pl.DeviceIdType.MESH
NT = (((1,), (1,)), ((), ()))
TN = (((0,), (0,)), ((), ()))


def dot(a, b, dims=(((1,), (0,)), ((), ()))):
    return lax.dot_general(a, b, dims, preferred_element_type=jnp.float32)


LOG2E = math.log2(math.e)
LN2 = math.log(2.0)
CEILING = 40.0
FAR = 1e38
PIECES = 6
SUB = 32
TILES = (0, 2, 1, 1, 0, 2)
SIDES = (0, 1, 1, 0, 1, 0)
AHEAD = 3
STEPS = len(TILES)


def last_of(codes, value):
    return max(i for i, code in enumerate(codes) if code == value)


LAGS = (3, 4, 6)


def scope(name):
    return contextlib.nullcontext()


def spread_rows(row):
    return jnp.transpose(jnp.broadcast_to(row, (128, row.shape[1])))


def twice(block):
    return jnp.concatenate([block, block], axis=1)


def by_eights(block):
    total = block[0:8]
    for i in range(1, block.shape[0] // 8):
        total = total + block[8 * i : 8 * i + 8]
    return total


def kernel(
    f_hbm, w_hbm, lab_hbm, pos_hbm, wgt_hbm, mask_hbm, loss_hbm, out_hbm,
    lab_ref, pos_ref, wgt_ref, mask_ref, loss_ref, out_ref, fv, wv, ea, nr, meta, metan, scored, fc, fct, acc, pul, cs, prod, prod2, gram, low, low2, comb, place, pulled, dpr, sqc, labc, sqn, stp, st, strec, tot,
    tst, trec, relay, ast0, arec0, ast1, arec1, hst, hrec, ga, yown, yst, yrec, pst, prec,
    f_l, w_l, ea_s, ea_r, ma_s, ma_r, en_s, en_r, mn_s, mn_r, fc_s, fc_r, d_s, d_r, t_s, t_r, rl_r, a0_s, a0_r, a1_s, a1_r,
    h_s, h_r, st_s, st_r, g_s, g_r, y_s, y_r, p_s, p_r, l_s, o_s, i_s,
):
    nb = lax.axis_size("blk")
    t = lax.axis_index("blk")
    r = lax.axis_index("rows")
    z, x = t // 2, t % 2
    y, c = r // 2, r % 2
    tx = 2 * z + 1 - x
    mate = 2 * y + 1 - c
    across = 2 * (1 - y) + c
    diag = 2 * (1 - y) + 1 - c
    peers = (mate, across, diag)
    q = 2 * x + c
    q_mate, q_side, q_diag = 2 * x + 1 - c, 2 * (1 - x) + c, 2 * (1 - x) + 1 - c
    quarter, depth = f_hbm.shape
    width = w_hbm.shape[1]
    tile = 4 * quarter
    pieces = ga.shape[0]
    piece = width // pieces
    half = out_hbm.shape[0]
    f32, bf16 = jnp.float32, jnp.bfloat16
    scale = SMOOTHING_SCALE * LOG2E

    def remote(src, dst, ss, rs, dev):
        return pltpu.make_async_remote_copy(
            src_ref=src, dst_ref=dst, send_sem=ss, recv_sem=rs, device_id=dev, device_id_type=MESH
        )

    drains = []

    def push(src, dst, ss, rs, dev):
        remote(src, dst, ss, rs, dev).start()

    def push_drained(src, dst, ss, rs, dev):
        push(src, dst, ss, rs, dev)
        drains.append((src, ss))

    def landed(dst, rs):
        remote(dst, dst, ea_s.at[0, 0], rs, (t, mate)).wait_recv()

    def drained(src, ss):
        remote(src, src, ss, ea_r.at[0, 0], (t, mate)).wait_send()

    columns = width // wv.shape[0]
    f_copy = pltpu.make_async_copy(f_hbm, fv, f_l)
    w_copies = [
        pltpu.make_async_copy(w_hbm.at[:, j * columns : (j + 1) * columns], wv.at[j], w_l.at[j])
        for j in range(wv.shape[0])
    ]
    f_copy.start()
    w_copies[0].start()
    small_copies = [
        pltpu.make_async_copy(source, target, i_s.at[n])
        for n, (source, target) in enumerate(
            ((lab_hbm, lab_ref), (pos_hbm, pos_ref), (wgt_hbm, wgt_ref), (mask_hbm, mask_ref))
        )
    ]
    for copy in small_copies:
        copy.start()

    barrier = pltpu.get_barrier_semaphore()
    for step in range(nb):
        for row in range(4):
            if step or row:
                pl.semaphore_signal(barrier, inc=1, device_id=((t + step) % nb, (r + row) % 4), device_id_type=MESH)

    with scope("small"):
        for copy in small_copies:
            copy.wait()
    meta[r] = jnp.zeros(meta.shape[1:], f32)
    meta[r, 0:1, :] = lab_ref[...].astype(f32)
    meta[r, 1:4, :] = pos_ref[...].astype(f32)
    meta[r, 4:5, :] = wgt_ref[...]
    for s in range(3):
        scored[s] = jnp.broadcast_to((mask_ref[0:1, s : s + 1] > 0).astype(f32), (8, quarter))

    def along_z(j):
        cut = slice(j * columns, (j + 1) * columns)
        return remote(nr.at[0, :, cut], nr.at[2, :, cut], en_s.at[1, j], en_r.at[1, j], ((t + 2) % nb, r))

    def along_x(held, j):
        cut = slice(j * columns, (j + 1) * columns)
        return remote(nr.at[held, :, cut], nr.at[1, :, cut], en_s.at[0, j], en_r.at[0, j], (tx, r))

    def block_column(px, pc, i):
        return pl.multiple_of((4 * (2 * pc + i % 2) + 2 * px + i // 2) * 128, 128)

    def send_features(i):
        for n, (px, pc) in enumerate(((x, 1 - c), (1 - x, c), (1 - x, 1 - c))):
            dev = (2 * z + px, 2 * y + pc)
            push_drained(fv.at[:, pl.ds(block_column(px, pc, i), 128)], fc.at[q, i], fc_s.at[n, i], fc_r.at[q, i], dev)

    f_copy.wait()
    for copy in w_copies[1:]:
        copy.start()
    square = jnp.zeros((quarter, 1), f32)
    for j in range(wv.shape[0]):
        with scope("embed"):
            w_copies[j].wait()
            cut = slice(j * columns, (j + 1) * columns)
            part = dot(fv[...], wv[j]).astype(bf16)
            ea[r, :, cut] = part
            nr[0, :, cut] = part
            wide = part.astype(f32)
            square = square + jnp.sum(wide * wide, axis=1, keepdims=True)
        if j == 0:
            with scope("barrier"):
                pl.semaphore_wait(barrier, 4 * nb - 1)
        for n, peer in ((1, across), (0, mate)):
            push_drained(ea.at[r, :, cut], ea.at[r, :, cut], ea_s.at[n, j], ea_r.at[r, j], (t, peer))
        along_z(j).start()
        if j == 0:
            send_features(0)

        @pl.when(x == 0)
        def _():
            along_x(0, j).start()

    meta[r, 5:6, :] = jnp.transpose(jnp.broadcast_to(square, (quarter, 128)))[0:1, :]
    for n, peer in enumerate(peers):
        push_drained(meta.at[r], meta.at[r], ma_s.at[n], ma_r.at[r], (t, peer))
    for s in (1, 2):
        push_drained(meta.at[r], metan.at[s - 1], mn_s.at[s - 1], mn_r.at[s - 1], ((t + s) % nb, r))
    for i in range(4):
        fc[q, i] = fv[:, pl.ds(block_column(x, c, i), 128)]

    labc[0] = spread_rows(meta[r, 0:1, :])
    for a in range(4):
        stp[a] = jnp.zeros(stp.shape[1:], f32)
    for s in range(3):
        cs[s] = jnp.zeros((quarter, 128), f32)

    @pl.when(x == 1)
    def _():
        trec[0] = jnp.zeros((quarter, width), bf16)

    sub = lax.broadcasted_iota(jnp.int32, (SUB, quarter), 0).astype(f32)

    def side_rows(side):
        return ea[pl.ds(2 * side, 2)].reshape(2 * quarter, width)

    def positives(first, count, found):
        rows_here = ea[pl.ds(first, count)].reshape(count * quarter, width)
        gram[0 : count * quarter] = dot(rows_here, ea[r], NT)
        places = [meta[r, 1 + k : 2 + k, :] for k in range(3)]
        for h in range(count):
            sqc[h * quarter : (h + 1) * quarter] = spread_rows(meta[first + h, 5:6, :])

        def rows(i, found):
            at = pl.ds(pl.multiple_of(i * SUB, SUB), SUB)
            d = twice(sqc[at]) - 2.0 * gram[at]
            base = (first * quarter + i * SUB).astype(f32)
            return tuple(found[k] + by_eights(jnp.where(sub == places[k] - base, d, 0.0)) for k in range(3))

        return lax.fori_loop(0, count * quarter // SUB, rows, found)

    with scope("own_rows"):
        for j in range(wv.shape[0]):
            landed(ea.at[mate, :, j * columns : (j + 1) * columns], ea_r.at[mate, j])
        landed(meta.at[mate], ma_r.at[mate])
        found = positives(2 * y, 2, tuple(jnp.zeros((8, quarter), f32) for _ in range(3)))
        prod[...] = dot(nr[0], side_rows(y), NT)

    def tile_columns(s, block):
        labc[s] = spread_rows(block[0:1, :])
        sqn[s] = scale * spread_rows(block[5:6, :])

    tile_columns(0, meta[r])
    with scope("rows"):
        for j in range(wv.shape[0]):
            cut = slice(j * columns, (j + 1) * columns)
            landed(ea.at[across, :, cut], ea_r.at[across, j])
            push_drained(ea.at[across, :, cut], ea.at[across, :, cut], ea_s.at[2, j], ea_r.at[across, j], (t, mate))

            @pl.when(x == 1)
            def _():
                landed(nr.at[2, :, cut], en_r.at[1, j])
                along_x(2, j).start()

        landed(meta.at[across], ma_r.at[across])

    for i in range(1, 4):
        send_features(i)
    with scope("positives"):
        found = positives(across, 1, found)
        for j in range(wv.shape[0]):
            landed(ea.at[diag, :, j * columns : (j + 1) * columns], ea_r.at[diag, j])
        landed(meta.at[diag], ma_r.at[diag])
        found = positives(diag, 1, found)
        for k in range(3):
            dpr[r, k : k + 1, :] = scale * (jnp.sum(found[k], axis=0, keepdims=True) + SLACK_GAP)
        dpr[r, 3:8, :] = jnp.zeros((5, quarter), f32)
    for n, peer in enumerate(peers):
        push_drained(dpr.at[r], dpr.at[r], d_s.at[n], d_r.at[r], (t, peer))


    def pairs(s, side, prod, low):
        on = scored[s, 0:1, :] > 0.0
        for g in range(2):
            a = 2 * side + g
            cut = slice(g * quarter, (g + 1) * quarter)
            tops = [jnp.where(on, dpr[a, k : k + 1, :], -FAR) for k in range(3)]
            names = meta[a, 0:1, :]
            weight = meta[a, 4:5, :] * (1.0 / (3.0 * tile))
            sums = [jnp.zeros((8, quarter), f32)] * 4
            for i in range(quarter // SUB):
                at = slice(i * SUB, (i + 1) * SUB)
                spread = twice(sqn[s, at]) - (2.0 * scale) * prod[at, cut]
                spread = jnp.where(twice(labc[s, at]) != names, spread, FAR)
                e, over = [], None
                for k in range(3):
                    h = tops[k] - spread
                    m = jnp.minimum(h, CEILING)
                    e.append(jnp.exp2(m))
                    over = h - m if over is None else over + (h - m)
                one = [1.0 + v for v in e]
                p = (e[0] + one[0] * e[1]) * one[2] + e[2]
                u = 1.0 + p
                inv = 1.0 / u
                logs = LN2 * (jnp.log2(u) + over) + (p - (u - 1.0)) * inv
                last = inv * one[2]
                sig = (e[0] * (last * one[1]), e[1] * (last * one[0]), e[2] * (inv * (one[0] * one[1])))
                coef = (sig[0] + sig[1] + sig[2]) * weight
                low[at, cut] = coef.astype(bf16)
                cs[s, at] += coef[:, :128] + coef[:, 128:]
                sums = [v + by_eights(w) for v, w in zip(sums, (logs,) + sig)]
            for k in range(4):
                stp[2 * side + g, k] += sums[k]

    def products(i, low):
        s, side = TILES[i], side_of(i)
        pulled_here = dot(low[...], side_rows(side))
        gained_here = dot(low[...], nr[s], TN).reshape(2, quarter, width)
        if TILES.index(s) == i:
            pul[s] = pulled_here
        else:
            pul[s] += pulled_here
        if SIDES.index(SIDES[i]) == i:
            acc[pl.ds(2 * side, 2)] = gained_here
        else:
            acc[pl.ds(2 * side, 2)] += gained_here

    def sums_over_lanes(s):
        return jnp.sum(cs[s], axis=1, keepdims=True)

    def term_value(s):
        return 2.0 * (pul[s] - sums_over_lanes(s) * nr[s].astype(f32))

    def columns_of(j):
        return pl.ds(pl.multiple_of(j * piece, piece), piece)

    def term_copy(s, j):
        cut = columns_of(j)
        return remote(
            tst.at[s - 1, :, cut], trec.at[s - 1, :, cut], t_s.at[s - 1, j], t_r.at[s - 1, j], ((t + nb - s) % nb, r)
        )

    def relay_copy(j):
        cut = columns_of(j)
        return remote(tst.at[0, :, cut], relay.at[:, cut], t_s.at[0, j], rl_r.at[j], (tx, r))

    def send_first():
        tst[0] = term_value(1).astype(bf16)
        for j in range(pieces):
            pl.when(x == 0)(lambda: relay_copy(j).start())
            pl.when(x == 1)(lambda: term_copy(1, j).start())

    def send_second():
        pul[2] = term_value(2)

        @pl.when(x == 0)
        def _():
            tst[1] = pul[2].astype(bf16)
            for j in range(pieces):
                term_copy(2, j).start()

    def merge(j):
        cut = columns_of(j)
        landed(relay.at[:, cut], rl_r.at[j])
        tst[1, :, cut] = (pul[2, :, cut] + relay[:, cut].astype(f32)).astype(bf16)
        term_copy(2, j).start()

    def merge_on_x1(j):
        pl.when(x == 1)(lambda: merge(j))

    def across_copy(j):
        cut = columns_of(j)
        return remote(ast1.at[:, cut], arec1.at[:, cut], a1_s.at[j], a1_r.at[j], (t, across))

    def side_of(i):
        return 1 - y if SIDES[i] else y

    def tile_arrives(s):
        for j in range(wv.shape[0]):
            @pl.when(jnp.logical_or(s == 1, x == 0))
            def _():
                landed(nr.at[s, :, j * columns : (j + 1) * columns], en_r.at[s - 1, j])

        landed(metan.at[s - 1], mn_r.at[s - 1])
        tile_columns(s, metan[s - 1])

    def send_hst():
        hst[...] = (2.0 * acc[diag]).astype(bf16)
        remote(hst, hrec, h_s, h_r, (t, mate)).start()

    def send_ast():
        landed(hrec, h_r)
        ast1[...] = (2.0 * acc[across] + hrec[...].astype(f32)).astype(bf16)
        for j in range(pieces):
            across_copy(j).start()

    def step(i, held, coming, low, before):
        arriving = i == TILES.index(1) - 1

        def next_product():
            if i + 1 < STEPS:
                coming[...] = dot(nr[TILES[i + 1]], side_rows(side_of(i + 1)), NT)

        if i == SIDES.index(1):
            with scope("distances"):
                for peer in (across, diag):
                    landed(dpr.at[peer], d_r.at[peer])
        with scope("chunk"):
            if not arriving:
                next_product()
            if i:
                products(i - 1, before)
            if i == last_of(TILES, 1) + 1:
                send_first()
            if i == last_of(SIDES, 1) + 1:
                send_hst()
            pairs(TILES[i], side_of(i), held, low)
        if arriving:
            with scope("tile1"):
                tile_arrives(1)
            next_product()

    with scope("tile2"):
        tile_arrives(2)
    with scope("distance"):
        landed(dpr.at[mate], d_r.at[mate])
    with scope("scores"):
        for i in range(0, STEPS, 2):
            step(i, prod, prod2, low, low2)
            step(i + 1, prod2, prod, low2, low)

    for a in range(4):
        for k in range(4):
            row = 4 * (a % 2) + k
            st[a // 2, row : row + 1, :] = jnp.sum(stp[a, k], axis=0, keepdims=True)
    for n, peer in enumerate(peers):
        push_drained(st, strec.at[r], st_s.at[n], st_r.at[r], (t, peer))
    with scope("last"):
        products(STEPS - 1, low2)
        send_second()
        merge_on_x1(0)
        send_ast()
        merge_on_x1(1)
        ast0[...] = (2.0 * acc[mate]).astype(bf16)
        push_drained(ast0, arec0, a0_s, a0_r, (t, mate))

    def features():
        with scope("features"):
            for n in (q_mate, q_side, q_diag):
                for i in range(4):
                    landed(fc.at[n, i], fc_r.at[n, i])
            for n in range(4):
                for i in range(4):
                    fct[i * 128 : (i + 1) * 128, n * quarter : (n + 1) * quarter] = jnp.transpose(fc[n, i])

    strec[r] = st[...]
    features()
    merge_on_x1(2)
    with scope("statistics"):
        for peer in peers:
            landed(strec.at[peer], st_r.at[peer])
    for a in range(4):
        part = slice(4 * (a % 2), 4 * (a % 2) + 4)
        tot[a, 0:4, :] = (
            strec[0, a // 2, part] + strec[1, a // 2, part] + strec[2, a // 2, part] + strec[3, a // 2, part]
        )
    loss_ref[...] = tot[r, 0:1, :] * (1.0 / (SMOOTHING_SCALE * 3.0 * tile))
    pltpu.make_async_copy(loss_ref, loss_hbm, l_s).start()

    with scope("pulls"):
        row_sub = lax.broadcasted_iota(jnp.int32, (SUB, quarter), 0).astype(f32)
        lane = lax.broadcasted_iota(jnp.int32, (SUB, quarter), 1).astype(f32)
        share = 1.0 / (3.0 * tile)
        for k in range(3):
            place[k] = spread_rows(meta[r, 1 + k : 2 + k, :])
            pulled[k] = spread_rows(tot[r, 1 + k : 2 + k, :] * meta[r, 4:5, :] * share)

        def listed(i, carry):
            at = pl.ds(pl.multiple_of(i * SUB, SUB), SUB)
            first = (r * quarter + i * SUB).astype(f32)
            gained = jnp.zeros((SUB, 128), f32)
            for n in range(4):
                given = jnp.zeros((SUB, quarter), f32)
                wgt = meta[n, 4:5, :] * share
                for k in range(3):
                    hit = row_sub == meta[n, 1 + k : 2 + k, :] - first
                    given = given + jnp.where(hit, tot[n, 1 + k : 2 + k, :] * wgt, 0.0)
                gained = gained + (given[:, :128] + given[:, 128:])
                for k in range(3):
                    hit = lane == twice(place[k, at]) - float(n * quarter)
                    given = given + jnp.where(hit, twice(pulled[k, at]), 0.0)
                high = given.astype(bf16)
                comb[0, at, n * quarter : (n + 1) * quarter] = high
                comb[1, at, n * quarter : (n + 1) * quarter] = (given - high.astype(f32)).astype(bf16)
            cs[1, at] = gained
            return carry

        lax.fori_loop(0, quarter // SUB, listed, 0)
        cs[2] = jnp.broadcast_to(sums_over_lanes(1) - sums_over_lanes(0), (quarter, 128))

    def side_copy(j):
        return remote(ga.at[j, q], ga.at[j, q], g_s.at[j, 1], g_r.at[j, q], (tx, r))

    def mate_copy(j):
        return remote(ga.at[j, q], ga.at[j, q], g_s.at[j, 0], g_r.at[j, q], (t, mate))

    def forward_copy(j):
        return remote(ga.at[j, q_side], ga.at[j, q_side], g_s.at[j, 2], g_r.at[j, q_side], (t, mate))

    def part_copy(j):
        return remote(yst.at[j], yrec.at[j], y_s.at[j], y_r.at[j], (t, across))

    def hop(j, i, h):
        return remote(
            pst.at[j, i, h], prec.at[j, z], p_s.at[j, i, h], p_r.at[j, z], (2 * (2 * c + i) + x, 2 * y + h)
        )

    def away(i, h):
        return jnp.logical_or(2 * c + i != z, c != h)

    def gather(j):
        cut = columns_of(j)
        rows_cut = ea[:, :, cut].reshape(tile, piece)
        net = acc[r, :, cut] + pul[0, :, cut] + cs[2, :, :piece] * ea[r, :, cut].astype(f32)
        net = net - dot(comb[0], rows_cut) - dot(comb[1], rows_cut)
        total = 2.0 * net + arec0[:, cut].astype(f32)
        landed(arec1.at[:, cut], a1_r.at[j])
        total = total + arec1[:, cut].astype(f32)
        @pl.when(x == 0)
        def _():
            landed(trec.at[0, :, cut], t_r.at[0, j])

        landed(trec.at[1, :, cut], t_r.at[1, j])
        total = total + trec[0, :, cut].astype(f32) + trec[1, :, cut].astype(f32)
        ga[j, q] = total.astype(bf16)
        side_copy(j).start()
        mate_copy(j).start()

    def forward(j):
        landed(ga.at[j, q_side], g_r.at[j, q_side])
        forward_copy(j).start()

    def multiply(j):
        for n in (q_mate, q_diag):
            landed(ga.at[j, n], g_r.at[j, n])
        part = dot(fct[...], ga[j].reshape(tile, piece))
        top, bottom = part[: 4 * half], part[4 * half :]
        yown[j] = jnp.where(y == 0, top, bottom)
        yst[j] = jnp.where(y == 0, bottom, top).astype(bf16)
        part_copy(j).start()

    def scatter(j):
        landed(yrec.at[j], y_r.at[j])
        total = (yown[j] + yrec[j].astype(f32)).astype(bf16)
        for i in range(2):
            for h in range(2):
                pst[j, i, h] = total[(2 * i + h) * half : (2 * i + h + 1) * half]
        for i in range(2):
            for h in range(2):
                @pl.when(away(i, h))
                def _():
                    hop(j, i, h).start()

                @pl.when(jnp.logical_not(away(i, h)))
                def _():
                    prec[j, z] = pst[j, i, h]

    def result_copy(j):
        return pltpu.make_async_copy(out_ref.at[:, columns_of(j)], out_hbm.at[:, columns_of(j)], o_s.at[j])

    def finish(j):
        for source in range(nb // 2):
            @pl.when(jnp.logical_or(z // 2 != c, z != source))
            def _():
                landed(prec.at[j, source], p_r.at[j, source])
        result = prec[j, 0].astype(f32)
        for source in range(1, nb // 2):
            result = result + prec[j, source].astype(f32)
        out_ref[:, columns_of(j)] = result
        result_copy(j).start()

    with scope("mate"):
        landed(arec0, a0_r)

    def stages(i, carry):
        @pl.when(i < pieces)
        def _():
            with scope("gather"):
                gather(i)

        @pl.when(jnp.logical_and(x == 1, i + AHEAD < pieces))
        def _():
            with scope("merge"):
                merge(i + AHEAD)

        for lag, name, work in zip(LAGS, ("forward", "multiply", "scatter"), (forward, multiply, scatter)):
            @pl.when(jnp.logical_and(i >= lag, i < pieces + lag))
            def _():
                with scope(name):
                    work(i - lag)

        return carry

    lax.fori_loop(0, pieces + LAGS[-1], stages, 0)

    def close(j, carry):
        with scope("finish"):
            finish(j)
        return carry

    lax.fori_loop(0, pieces, close, 0)

    def drain(j, carry):
        result_copy(j).wait()
        for copy in (side_copy, mate_copy, forward_copy, part_copy):
            copy(j).wait_send()
        for i in range(2):
            for h in range(2):
                @pl.when(away(i, h))
                def _():
                    hop(j, i, h).wait_send()
        return carry

    with scope("drain"):
        pltpu.make_async_copy(loss_ref, loss_hbm, l_s).wait()
        lax.fori_loop(0, pieces, drain, 0)
        for j in range(pieces):
            term_copy(1, j).wait_send()
            term_copy(2, j).wait_send()
            across_copy(j).wait_send()
        for j in range(wv.shape[0]):
            along_z(j).wait_send()
            along_x(0, j).wait_send()
        remote(hst, hrec, h_s, h_r, (t, mate)).wait_send()
        for source, semaphore in drains:
            drained(source, semaphore)


def results(loss_ref, grad_ref, loss_out, grad_out):
    loss_out[...] = loss_ref[0]
    grad_out[...] = grad_ref[...]


def fused(features, head_weight, labels, pos_index, pair_mask, loss_weight):
    quarter, depth = features.shape
    width = head_weight.shape[1]
    nb = lax.axis_size("blk")
    share = depth // (4 * nb)
    f32, bf16 = jnp.float32, jnp.bfloat16
    dma = pltpu.SemaphoreType.DMA
    vmem = pl.BlockSpec(memory_space=pltpu.VMEM)
    hbm = pl.BlockSpec(memory_space=pl.ANY)
    block = (quarter, width)
    small = (8, quarter)
    piece = width // PIECES
    loss, grad = pl.pallas_call(
        kernel,
        out_shape=(jax.ShapeDtypeStruct((1, quarter), f32), jax.ShapeDtypeStruct((share, width), f32)),
        in_specs=[hbm] * 6,
        out_specs=(hbm, hbm),
        scratch_shapes=[
            pltpu.VMEM((1, quarter), jnp.int32),
            pltpu.VMEM(pos_index.shape[::-1], jnp.int32),
            pltpu.VMEM((1, quarter), f32),
            pltpu.VMEM(pair_mask.shape, jnp.int32),
            pltpu.VMEM((1, quarter), f32),
            pltpu.VMEM((share, width), f32),
            pltpu.VMEM((quarter, depth), bf16),
            pltpu.VMEM((3, depth, width // 3), bf16),
            pltpu.VMEM((4,) + block, bf16),
            pltpu.VMEM((3,) + block, bf16),
            pltpu.VMEM((4,) + small, f32),
            pltpu.VMEM((2,) + small, f32),
            pltpu.VMEM((3,) + small, f32),
            pltpu.VMEM((4, 4, quarter, 128), bf16),
            pltpu.VMEM((512, 4 * quarter), bf16),
            pltpu.VMEM((4,) + block, f32),
            pltpu.VMEM((3,) + block, f32),
            pltpu.VMEM((3, quarter, 128), f32),
            pltpu.VMEM((quarter, 2 * quarter), f32),
            pltpu.VMEM((quarter, 2 * quarter), f32),
            pltpu.VMEM((2 * quarter, quarter), f32),
            pltpu.VMEM((quarter, 2 * quarter), bf16),
            pltpu.VMEM((quarter, 2 * quarter), bf16),
            pltpu.VMEM((2, quarter, 4 * quarter), bf16),
            pltpu.VMEM((3, quarter, 128), f32),
            pltpu.VMEM((3, quarter, 128), f32),
            pltpu.VMEM((4,) + small, f32),
            pltpu.VMEM((2 * quarter, 128), f32),
            pltpu.VMEM((3, quarter, 128), f32),
            pltpu.VMEM((3, quarter, 128), f32),
            pltpu.VMEM((4, 4) + small, f32),
            pltpu.VMEM((2,) + small, f32),
            pltpu.VMEM((4, 2) + small, f32),
            pltpu.VMEM((4,) + small, f32),
            pltpu.VMEM((2,) + block, bf16),
            pltpu.VMEM((2,) + block, bf16),
            pltpu.VMEM(block, bf16),
            pltpu.VMEM(block, bf16),
            pltpu.VMEM(block, bf16),
            pltpu.VMEM(block, bf16),
            pltpu.VMEM(block, bf16),
            pltpu.VMEM(block, bf16),
            pltpu.VMEM(block, bf16),
            pltpu.VMEM((PIECES, 4, quarter, piece), bf16),
            pltpu.VMEM((PIECES, 4 * share, piece), f32),
            pltpu.VMEM((PIECES, 4 * share, piece), bf16),
            pltpu.VMEM((PIECES, 4 * share, piece), bf16),
            pltpu.VMEM((PIECES, 2, 2, share, piece), bf16),
            pltpu.VMEM((PIECES, nb // 2, share, piece), bf16),
            dma(()), dma((3,)), dma((3, 3)), dma((4, 3)), dma((3,)), dma((4,)), dma((2, 3)), dma((2, 3)), dma((2,)), dma((2,)),
            dma((3, 4)), dma((4, 4)), dma((3,)), dma((4,)), dma((2, PIECES)), dma((2, PIECES)), dma((PIECES,)), dma(()), dma(()),
            dma((PIECES,)), dma((PIECES,)), dma(()), dma(()), dma((3,)), dma((4,)),
            dma((PIECES, 3)), dma((PIECES, 4)), dma((PIECES,)), dma((PIECES,)), dma((PIECES, 2, 2)), dma((PIECES, nb // 2)), dma(()), dma((PIECES,)), dma((4,)),
        ],
        compiler_params=pltpu.CompilerParams(
            collective_id=0, has_side_effects=True, vmem_limit_bytes=56 * 1024 * 1024
        ),
    )(features, head_weight, labels[None, :], pos_index.T, loss_weight[None, :], pair_mask)
    return pl.pallas_call(
        results,
        out_shape=(jax.ShapeDtypeStruct((quarter,), f32), jax.ShapeDtypeStruct((share, width), f32)),
        in_specs=[vmem] * 2,
        out_specs=(vmem, vmem),
    )(loss, grad)


def solution(mesh):
    body = fused if mesh.shape["blk"] == 8 and mesh.shape["rows"] == 4 else local
    return jax.shard_map(
        body,
        mesh=mesh,
        in_specs=(
            P(("blk", "rows"), None),
            P(),
            P(("blk", "rows")),
            P(("blk", "rows"), None),
            P("blk", None),
            P(("blk", "rows")),
        ),
        out_specs=(P(("blk", "rows")), P(("blk", "rows"), None)),
        check_vma=False,
    )
```

```python
import contextlib
import math

import jax
import jax.numpy as jnp
from jax import lax
from jax.experimental import pallas as pl
from jax.experimental.pallas import tpu as pltpu
from jax.sharding import PartitionSpec as P

SMOOTHING_SCALE = 16.0
SLACK_GAP = 0.1


def passed_along(block, axis, distance):
    devices = range(lax.axis_size(axis))
    route = [((i - distance) % len(devices), i) for i in devices]
    return lax.ppermute(block, axis, route)


def score_tile(
    anchors, anchor_sq, anchor_labels, matching_separation, weights, tile_rows, tile_labels, listed
):
    matching_samples = matching_separation.shape[1]
    block_tally = tile_rows.shape[0]
    anchor_count = anchors.shape[0]

    def compute(unused):
        products = lax.dot_general(
            anchors, tile_rows, (((1,), (1,)), ((), ())), preferred_element_type=jnp.float32
        )
        widened = tile_rows.astype(jnp.float32)
        tile_sq = jnp.sum(widened * widened, axis=1)
        couple_separation = anchor_sq[:, None] + tile_sq[None, :] - 2.0 * products
        valid = (anchor_labels[:, None] != tile_labels[None, :]).astype(jnp.float32)
        weighting = weights / (matching_samples * block_tally)
        objective_accrued = jnp.zeros((anchor_count,), jnp.float32)
        coefficient = jnp.zeros((anchor_count, block_tally), jnp.float32)
        totals = []
        for target_slot in range(matching_samples):
            slack_excess = SMOOTHING_SCALE * (
                matching_separation[:, target_slot : target_slot + 1]
                - couple_separation
                + SLACK_GAP
            )
            objective_accrued = objective_accrued + jnp.sum(
                valid * jax.nn.softplus(slack_excess), axis=1
            )
            sigmoids = valid * jax.nn.sigmoid(slack_excess)
            coefficient = coefficient + sigmoids
            totals.append(jnp.sum(sigmoids, axis=1))
        objective_accrued = objective_accrued / (SMOOTHING_SCALE * matching_samples * block_tally)
        coefficient = coefficient * weighting[:, None]
        pos_coef = jnp.stack(totals, axis=1) * weighting[:, None]
        coef_low = coefficient.astype(jnp.bfloat16)
        anchor_grad = 2.0 * jnp.dot(coef_low, tile_rows, preferred_element_type=jnp.float32)
        pulled = lax.dot_general(
            coef_low, anchors, (((0,), (0,)), ((), ())), preferred_element_type=jnp.float32
        )
        col_sums = jnp.sum(coefficient, axis=0)
        tile_grad = 2.0 * (pulled - col_sums[:, None] * widened)
        return (objective_accrued, pos_coef, anchor_grad, tile_grad, coef_low, col_sums)

    def skip(unused):
        return (
            jnp.zeros((anchor_count,), jnp.float32),
            jnp.zeros((anchor_count, matching_samples), jnp.float32),
            jnp.zeros((anchor_count, anchors.shape[1]), jnp.float32),
            jnp.zeros((block_tally, anchors.shape[1]), jnp.float32),
            jnp.zeros((anchor_count, block_tally), jnp.bfloat16),
            jnp.zeros((block_tally,), jnp.float32),
        )

    return lax.cond(listed, compute, skip, 0)


def local(features, head_weight, labels, pos_index, pair_mask, loss_weight):
    embedded = jnp.dot(features, head_weight, preferred_element_type=jnp.float32).astype(
        jnp.bfloat16
    )
    widened = embedded.astype(jnp.float32)
    anchor_sq = jnp.sum(widened * widened, axis=1)
    tile_rows, tile_labels = (
        lax.all_gather(embedded, "rows", axis=0, tiled=True),
        lax.all_gather(labels, "rows", axis=0, tiled=True),
    )
    pos_rows = tile_rows[pos_index]
    pos_wide = pos_rows.astype(jnp.float32)
    pos_sq = jnp.sum(pos_wide * pos_wide, axis=2)
    matching_separation = (
        anchor_sq[:, None]
        + pos_sq
        - 2.0 * jnp.einsum("ad,akd->ak", embedded, pos_rows, preferred_element_type=jnp.float32)
    )
    offsets = pair_mask.shape[1]
    loss_total, coef_total, grad_total, own_term, first_low, first_sums = score_tile(
        embedded,
        anchor_sq,
        labels,
        matching_separation,
        loss_weight,
        tile_rows,
        tile_labels,
        pair_mask[0, 0] > 0,
    )
    received = jnp.zeros_like(own_term)
    walk_rows, walk_labels = (tile_rows, tile_labels)
    for offset in range(1, offsets):
        walk_rows, walk_labels = passed_along((walk_rows, walk_labels), "blk", 1)
        loss_part, coef_part, grad_part, term_part, low_part, sums_part = score_tile(
            embedded,
            anchor_sq,
            labels,
            matching_separation,
            loss_weight,
            walk_rows,
            walk_labels,
            pair_mask[0, offset] > 0,
        )
        loss_total = loss_total + loss_part
        coef_total = coef_total + coef_part
        grad_total = grad_total + grad_part
        received = received + passed_along(term_part.astype(jnp.bfloat16), "blk", -offset).astype(
            term_part.dtype
        )
    grad_total = grad_total - 2.0 * jnp.sum(coef_total[:, :, None] * pos_wide, axis=1)
    pushed = 2.0 * coef_total[:, :, None] * (pos_wide - widened[:, None, :])
    own_term = own_term.at[pos_index.reshape(-1)].add(pushed.reshape(-1, pushed.shape[2]))
    quarter_sum = lax.psum_scatter(own_term + received, "rows", scatter_dimension=0, tiled=True)
    emb_grad = grad_total + quarter_sum
    grad_low = emb_grad.astype(jnp.bfloat16)
    weight_grad = lax.psum_scatter(
        lax.dot_general(
            features, grad_low, (((0,), (0,)), ((), ())), preferred_element_type=jnp.float32
        ),
        ("blk", "rows"),
        scatter_dimension=0,
        tiled=True,
    )
    return (loss_total, weight_grad)


MESH = pl.DeviceIdType.MESH
NT = (((1,), (1,)), ((), ()))
TN = (((0,), (0,)), ((), ()))


def dot(a, b, dims=(((1,), (0,)), ((), ()))):
    return lax.dot_general(a, b, dims, preferred_element_type=jnp.float32)


LOG2E = math.log2(math.e)
LN2 = math.log(2.0)
CEILING = 40.0
FAR = 1e38
PIECES = 6
SUB = 32
TILES = (0, 2, 1, 1, 0, 2)
SIDES = (0, 1, 1, 0, 1, 0)
AHEAD = 3
STEPS = len(TILES)


def last_of(codes, value):
    return max(i for i, code in enumerate(codes) if code == value)


LAGS = (3, 4, 6)


def scope(name):
    return contextlib.nullcontext()


def spread_rows(row):
    return jnp.transpose(jnp.broadcast_to(row, (128, row.shape[1])))


def twice(block):
    return jnp.concatenate([block, block], axis=1)


def by_eights(block):
    total = block[0:8]
    for i in range(1, block.shape[0] // 8):
        total = total + block[8 * i : 8 * i + 8]
    return total


def kernel(
    f_hbm, w_hbm, lab_hbm, pos_hbm, wgt_hbm, mask_hbm, loss_ref, out_ref,
    lab_ref, pos_ref, wgt_ref, mask_ref, fv, wv, ea, nr, meta, metan, scored, fc, fct, acc, pul, cs, prod, prod2, gram, low, low2, comb, place, pulled, dpr, sqc, labc, sqn, stp, st, strec, tot,
    tst, trec, relay, ast0, arec0, ast1, arec1, hst, hrec, ga, yown, yst, yrec, pst, prec,
    f_l, w_l, ea_s, ea_r, ma_s, ma_r, en_s, en_r, mn_s, mn_r, fc_s, fc_r, d_s, d_r, t_s, t_r, rl_r, a0_s, a0_r, a1_s, a1_r,
    h_s, h_r, st_s, st_r, g_s, g_r, y_s, y_r, p_s, p_r, i_s,
):
    nb = lax.axis_size("blk")
    t = lax.axis_index("blk")
    r = lax.axis_index("rows")
    z, x = t // 2, t % 2
    y, c = r // 2, r % 2
    tx = 2 * z + 1 - x
    mate = 2 * y + 1 - c
    across = 2 * (1 - y) + c
    diag = 2 * (1 - y) + 1 - c
    peers = (mate, across, diag)
    q = 2 * x + c
    q_mate, q_side, q_diag = 2 * x + 1 - c, 2 * (1 - x) + c, 2 * (1 - x) + 1 - c
    quarter, depth = f_hbm.shape
    width = w_hbm.shape[1]
    tile = 4 * quarter
    pieces = ga.shape[0]
    piece = width // pieces
    half = out_ref.shape[0]
    f32, bf16 = jnp.float32, jnp.bfloat16
    scale = SMOOTHING_SCALE * LOG2E

    def remote(src, dst, ss, rs, dev):
        return pltpu.make_async_remote_copy(
            src_ref=src, dst_ref=dst, send_sem=ss, recv_sem=rs, device_id=dev, device_id_type=MESH
        )

    drains = []

    def push(src, dst, ss, rs, dev):
        remote(src, dst, ss, rs, dev).start()

    def push_drained(src, dst, ss, rs, dev):
        push(src, dst, ss, rs, dev)
        drains.append((src, ss))

    def landed(dst, rs):
        remote(dst, dst, ea_s.at[0, 0], rs, (t, mate)).wait_recv()

    def drained(src, ss):
        remote(src, src, ss, ea_r.at[0, 0], (t, mate)).wait_send()

    columns = width // wv.shape[0]
    f_copy = pltpu.make_async_copy(f_hbm, fv, f_l)
    w_copies = [
        pltpu.make_async_copy(w_hbm.at[:, j * columns : (j + 1) * columns], wv.at[j], w_l.at[j])
        for j in range(wv.shape[0])
    ]
    f_copy.start()
    w_copies[0].start()
    small_copies = [
        pltpu.make_async_copy(source, target, i_s.at[n])
        for n, (source, target) in enumerate(
            ((lab_hbm, lab_ref), (pos_hbm, pos_ref), (wgt_hbm, wgt_ref), (mask_hbm, mask_ref))
        )
    ]
    for copy in small_copies:
        copy.start()

    barrier = pltpu.get_barrier_semaphore()
    for step in range(nb):
        for row in range(4):
            if step or row:
                pl.semaphore_signal(barrier, inc=1, device_id=((t + step) % nb, (r + row) % 4), device_id_type=MESH)

    with scope("small"):
        for copy in small_copies:
            copy.wait()
    meta[r] = jnp.zeros(meta.shape[1:], f32)
    meta[r, 0:1, :] = lab_ref[...].astype(f32)
    meta[r, 1:4, :] = pos_ref[...].astype(f32)
    meta[r, 4:5, :] = wgt_ref[...]
    for s in range(3):
        scored[s] = jnp.broadcast_to((mask_ref[0:1, s : s + 1] > 0).astype(f32), (8, quarter))

    def along_z(j):
        cut = slice(j * columns, (j + 1) * columns)
        return remote(nr.at[0, :, cut], nr.at[2, :, cut], en_s.at[1, j], en_r.at[1, j], ((t + 2) % nb, r))

    def along_x(held, j):
        cut = slice(j * columns, (j + 1) * columns)
        return remote(nr.at[held, :, cut], nr.at[1, :, cut], en_s.at[0, j], en_r.at[0, j], (tx, r))

    def block_column(px, pc, i):
        return pl.multiple_of((4 * (2 * pc + i % 2) + 2 * px + i // 2) * 128, 128)

    def send_features(i):
        for n, (px, pc) in enumerate(((x, 1 - c), (1 - x, c), (1 - x, 1 - c))):
            dev = (2 * z + px, 2 * y + pc)
            push_drained(fv.at[:, pl.ds(block_column(px, pc, i), 128)], fc.at[q, i], fc_s.at[n, i], fc_r.at[q, i], dev)

    f_copy.wait()
    for copy in w_copies[1:]:
        copy.start()
    square = jnp.zeros((quarter, 1), f32)
    for j in range(wv.shape[0]):
        with scope("embed"):
            w_copies[j].wait()
            cut = slice(j * columns, (j + 1) * columns)
            part = dot(fv[...], wv[j]).astype(bf16)
            ea[r, :, cut] = part
            nr[0, :, cut] = part
            wide = part.astype(f32)
            square = square + jnp.sum(wide * wide, axis=1, keepdims=True)
        if j == 0:
            with scope("barrier"):
                pl.semaphore_wait(barrier, 4 * nb - 1)
        for n, peer in ((1, across), (0, mate)):
            push_drained(ea.at[r, :, cut], ea.at[r, :, cut], ea_s.at[n, j], ea_r.at[r, j], (t, peer))
        along_z(j).start()
        if j == 0:
            send_features(0)

        @pl.when(x == 0)
        def _():
            along_x(0, j).start()

    meta[r, 5:6, :] = jnp.transpose(jnp.broadcast_to(square, (quarter, 128)))[0:1, :]
    for n, peer in enumerate(peers):
        push_drained(meta.at[r], meta.at[r], ma_s.at[n], ma_r.at[r], (t, peer))
    for s in (1, 2):
        push_drained(meta.at[r], metan.at[s - 1], mn_s.at[s - 1], mn_r.at[s - 1], ((t + s) % nb, r))
    for i in range(4):
        fc[q, i] = fv[:, pl.ds(block_column(x, c, i), 128)]

    labc[0] = spread_rows(meta[r, 0:1, :])
    for a in range(4):
        stp[a] = jnp.zeros(stp.shape[1:], f32)
    for s in range(3):
        cs[s] = jnp.zeros((quarter, 128), f32)

    @pl.when(x == 1)
    def _():
        trec[0] = jnp.zeros((quarter, width), bf16)

    sub = lax.broadcasted_iota(jnp.int32, (SUB, quarter), 0).astype(f32)

    def side_rows(side):
        return ea[pl.ds(2 * side, 2)].reshape(2 * quarter, width)

    def positives(first, count, found):
        rows_here = ea[pl.ds(first, count)].reshape(count * quarter, width)
        gram[0 : count * quarter] = dot(rows_here, ea[r], NT)
        places = [meta[r, 1 + k : 2 + k, :] for k in range(3)]
        for h in range(count):
            sqc[h * quarter : (h + 1) * quarter] = spread_rows(meta[first + h, 5:6, :])

        def rows(i, found):
            at = pl.ds(pl.multiple_of(i * SUB, SUB), SUB)
            d = twice(sqc[at]) - 2.0 * gram[at]
            base = (first * quarter + i * SUB).astype(f32)
            return tuple(found[k] + by_eights(jnp.where(sub == places[k] - base, d, 0.0)) for k in range(3))

        return lax.fori_loop(0, count * quarter // SUB, rows, found)

    with scope("own_rows"):
        for j in range(wv.shape[0]):
            landed(ea.at[mate, :, j * columns : (j + 1) * columns], ea_r.at[mate, j])
        landed(meta.at[mate], ma_r.at[mate])
        found = positives(2 * y, 2, tuple(jnp.zeros((8, quarter), f32) for _ in range(3)))
        prod[...] = dot(nr[0], side_rows(y), NT)

    def tile_columns(s, block):
        labc[s] = spread_rows(block[0:1, :])
        sqn[s] = scale * spread_rows(block[5:6, :])

    tile_columns(0, meta[r])
    with scope("rows"):
        for j in range(wv.shape[0]):
            cut = slice(j * columns, (j + 1) * columns)
            landed(ea.at[across, :, cut], ea_r.at[across, j])
            push_drained(ea.at[across, :, cut], ea.at[across, :, cut], ea_s.at[2, j], ea_r.at[across, j], (t, mate))

            @pl.when(x == 1)
            def _():
                landed(nr.at[2, :, cut], en_r.at[1, j])
                along_x(2, j).start()

        landed(meta.at[across], ma_r.at[across])

    for i in range(1, 4):
        send_features(i)
    with scope("positives"):
        found = positives(across, 1, found)
        for j in range(wv.shape[0]):
            landed(ea.at[diag, :, j * columns : (j + 1) * columns], ea_r.at[diag, j])
        landed(meta.at[diag], ma_r.at[diag])
        found = positives(diag, 1, found)
        for k in range(3):
            dpr[r, k : k + 1, :] = scale * (jnp.sum(found[k], axis=0, keepdims=True) + SLACK_GAP)
        dpr[r, 3:8, :] = jnp.zeros((5, quarter), f32)
    for n, peer in enumerate(peers):
        push_drained(dpr.at[r], dpr.at[r], d_s.at[n], d_r.at[r], (t, peer))


    def pairs(s, side, prod, low):
        on = scored[s, 0:1, :] > 0.0
        for g in range(2):
            a = 2 * side + g
            cut = slice(g * quarter, (g + 1) * quarter)
            tops = [jnp.where(on, dpr[a, k : k + 1, :], -FAR) for k in range(3)]
            names = meta[a, 0:1, :]
            weight = meta[a, 4:5, :] * (1.0 / (3.0 * tile))
            sums = [jnp.zeros((8, quarter), f32)] * 4
            for i in range(quarter // SUB):
                at = slice(i * SUB, (i + 1) * SUB)
                spread = twice(sqn[s, at]) - (2.0 * scale) * prod[at, cut]
                spread = jnp.where(twice(labc[s, at]) != names, spread, FAR)
                e, over = [], None
                for k in range(3):
                    h = tops[k] - spread
                    m = jnp.minimum(h, CEILING)
                    e.append(jnp.exp2(m))
                    over = h - m if over is None else over + (h - m)
                one = [1.0 + v for v in e]
                p = (e[0] + one[0] * e[1]) * one[2] + e[2]
                u = 1.0 + p
                inv = 1.0 / u
                logs = LN2 * (jnp.log2(u) + over) + (p - (u - 1.0)) * inv
                last = inv * one[2]
                sig = (e[0] * (last * one[1]), e[1] * (last * one[0]), e[2] * (inv * (one[0] * one[1])))
                coef = (sig[0] + sig[1] + sig[2]) * weight
                low[at, cut] = coef.astype(bf16)
                cs[s, at] += coef[:, :128] + coef[:, 128:]
                sums = [v + by_eights(w) for v, w in zip(sums, (logs,) + sig)]
            for k in range(4):
                stp[2 * side + g, k] += sums[k]

    def products(i, low):
        s, side = TILES[i], side_of(i)
        pulled_here = dot(low[...], side_rows(side))
        gained_here = dot(low[...], nr[s], TN).reshape(2, quarter, width)
        if TILES.index(s) == i:
            pul[s] = pulled_here
        else:
            pul[s] += pulled_here
        if SIDES.index(SIDES[i]) == i:
            acc[pl.ds(2 * side, 2)] = gained_here
        else:
            acc[pl.ds(2 * side, 2)] += gained_here

    def sums_over_lanes(s):
        return jnp.sum(cs[s], axis=1, keepdims=True)

    def term_value(s):
        return 2.0 * (pul[s] - sums_over_lanes(s) * nr[s].astype(f32))

    def columns_of(j):
        return pl.ds(pl.multiple_of(j * piece, piece), piece)

    def term_copy(s, j):
        cut = columns_of(j)
        return remote(
            tst.at[s - 1, :, cut], trec.at[s - 1, :, cut], t_s.at[s - 1, j], t_r.at[s - 1, j], ((t + nb - s) % nb, r)
        )

    def relay_copy(j):
        cut = columns_of(j)
        return remote(tst.at[0, :, cut], relay.at[:, cut], t_s.at[0, j], rl_r.at[j], (tx, r))

    def send_first():
        tst[0] = term_value(1).astype(bf16)
        for j in range(pieces):
            pl.when(x == 0)(lambda: relay_copy(j).start())
            pl.when(x == 1)(lambda: term_copy(1, j).start())

    def send_second():
        pul[2] = term_value(2)

        @pl.when(x == 0)
        def _():
            tst[1] = pul[2].astype(bf16)
            for j in range(pieces):
                term_copy(2, j).start()

    def merge(j):
        cut = columns_of(j)
        landed(relay.at[:, cut], rl_r.at[j])
        tst[1, :, cut] = (pul[2, :, cut] + relay[:, cut].astype(f32)).astype(bf16)
        term_copy(2, j).start()

    def merge_on_x1(j):
        pl.when(x == 1)(lambda: merge(j))

    def across_copy(j):
        cut = columns_of(j)
        return remote(ast1.at[:, cut], arec1.at[:, cut], a1_s.at[j], a1_r.at[j], (t, across))

    def side_of(i):
        return 1 - y if SIDES[i] else y

    def tile_arrives(s):
        for j in range(wv.shape[0]):
            @pl.when(jnp.logical_or(s == 1, x == 0))
            def _():
                landed(nr.at[s, :, j * columns : (j + 1) * columns], en_r.at[s - 1, j])

        landed(metan.at[s - 1], mn_r.at[s - 1])
        tile_columns(s, metan[s - 1])

    def send_hst():
        hst[...] = (2.0 * acc[diag]).astype(bf16)
        remote(hst, hrec, h_s, h_r, (t, mate)).start()

    def send_ast():
        landed(hrec, h_r)
        ast1[...] = (2.0 * acc[across] + hrec[...].astype(f32)).astype(bf16)
        for j in range(pieces):
            across_copy(j).start()

    def step(i, held, coming, low, before):
        arriving = i == TILES.index(1) - 1

        def next_product():
            if i + 1 < STEPS:
                coming[...] = dot(nr[TILES[i + 1]], side_rows(side_of(i + 1)), NT)

        if i == SIDES.index(1):
            with scope("distances"):
                for peer in (across, diag):
                    landed(dpr.at[peer], d_r.at[peer])
        with scope("chunk"):
            if not arriving:
                next_product()
            if i:
                products(i - 1, before)
            if i == last_of(TILES, 1) + 1:
                send_first()
            if i == last_of(SIDES, 1) + 1:
                send_hst()
            pairs(TILES[i], side_of(i), held, low)
        if arriving:
            with scope("tile1"):
                tile_arrives(1)
            next_product()

    with scope("tile2"):
        tile_arrives(2)
    with scope("distance"):
        landed(dpr.at[mate], d_r.at[mate])
    with scope("scores"):
        for i in range(0, STEPS, 2):
            step(i, prod, prod2, low, low2)
            step(i + 1, prod2, prod, low2, low)

    for a in range(4):
        for k in range(4):
            row = 4 * (a % 2) + k
            st[a // 2, row : row + 1, :] = jnp.sum(stp[a, k], axis=0, keepdims=True)
    for n, peer in enumerate(peers):
        push_drained(st, strec.at[r], st_s.at[n], st_r.at[r], (t, peer))
    with scope("last"):
        products(STEPS - 1, low2)
        send_second()
        merge_on_x1(0)
        send_ast()
        merge_on_x1(1)
        ast0[...] = (2.0 * acc[mate]).astype(bf16)
        push_drained(ast0, arec0, a0_s, a0_r, (t, mate))

    def features():
        with scope("features"):
            for n in (q_mate, q_side, q_diag):
                for i in range(4):
                    landed(fc.at[n, i], fc_r.at[n, i])
            for n in range(4):
                for i in range(4):
                    fct[i * 128 : (i + 1) * 128, n * quarter : (n + 1) * quarter] = jnp.transpose(fc[n, i])

    strec[r] = st[...]
    features()
    merge_on_x1(2)
    with scope("statistics"):
        for peer in peers:
            landed(strec.at[peer], st_r.at[peer])
    for a in range(4):
        part = slice(4 * (a % 2), 4 * (a % 2) + 4)
        tot[a, 0:4, :] = (
            strec[0, a // 2, part] + strec[1, a // 2, part] + strec[2, a // 2, part] + strec[3, a // 2, part]
        )
    loss_ref[...] = tot[r, 0:1, :] * (1.0 / (SMOOTHING_SCALE * 3.0 * tile))

    with scope("pulls"):
        row_sub = lax.broadcasted_iota(jnp.int32, (SUB, quarter), 0).astype(f32)
        lane = lax.broadcasted_iota(jnp.int32, (SUB, quarter), 1).astype(f32)
        share = 1.0 / (3.0 * tile)
        for k in range(3):
            place[k] = spread_rows(meta[r, 1 + k : 2 + k, :])
            pulled[k] = spread_rows(tot[r, 1 + k : 2 + k, :] * meta[r, 4:5, :] * share)

        def listed(i, carry):
            at = pl.ds(pl.multiple_of(i * SUB, SUB), SUB)
            first = (r * quarter + i * SUB).astype(f32)
            gained = jnp.zeros((SUB, 128), f32)
            for n in range(4):
                given = jnp.zeros((SUB, quarter), f32)
                wgt = meta[n, 4:5, :] * share
                for k in range(3):
                    hit = row_sub == meta[n, 1 + k : 2 + k, :] - first
                    given = given + jnp.where(hit, tot[n, 1 + k : 2 + k, :] * wgt, 0.0)
                gained = gained + (given[:, :128] + given[:, 128:])
                for k in range(3):
                    hit = lane == twice(place[k, at]) - float(n * quarter)
                    given = given + jnp.where(hit, twice(pulled[k, at]), 0.0)
                high = given.astype(bf16)
                comb[0, at, n * quarter : (n + 1) * quarter] = high
                comb[1, at, n * quarter : (n + 1) * quarter] = (given - high.astype(f32)).astype(bf16)
            cs[1, at] = gained
            return carry

        lax.fori_loop(0, quarter // SUB, listed, 0)
        cs[2] = jnp.broadcast_to(sums_over_lanes(1) - sums_over_lanes(0), (quarter, 128))

    def side_copy(j):
        return remote(ga.at[j, q], ga.at[j, q], g_s.at[j, 1], g_r.at[j, q], (tx, r))

    def mate_copy(j):
        return remote(ga.at[j, q], ga.at[j, q], g_s.at[j, 0], g_r.at[j, q], (t, mate))

    def forward_copy(j):
        return remote(ga.at[j, q_side], ga.at[j, q_side], g_s.at[j, 2], g_r.at[j, q_side], (t, mate))

    def part_copy(j):
        return remote(yst.at[j], yrec.at[j], y_s.at[j], y_r.at[j], (t, across))

    def hop(j, i, h):
        return remote(
            pst.at[j, i, h], prec.at[j, z], p_s.at[j, i, h], p_r.at[j, z], (2 * (2 * c + i) + x, 2 * y + h)
        )

    def away(i, h):
        return jnp.logical_or(2 * c + i != z, c != h)

    def gather(j):
        cut = columns_of(j)
        rows_cut = ea[:, :, cut].reshape(tile, piece)
        net = acc[r, :, cut] + pul[0, :, cut] + cs[2, :, :piece] * ea[r, :, cut].astype(f32)
        net = net - dot(comb[0], rows_cut) - dot(comb[1], rows_cut)
        total = 2.0 * net + arec0[:, cut].astype(f32)
        landed(arec1.at[:, cut], a1_r.at[j])
        total = total + arec1[:, cut].astype(f32)
        @pl.when(x == 0)
        def _():
            landed(trec.at[0, :, cut], t_r.at[0, j])

        landed(trec.at[1, :, cut], t_r.at[1, j])
        total = total + trec[0, :, cut].astype(f32) + trec[1, :, cut].astype(f32)
        ga[j, q] = total.astype(bf16)
        side_copy(j).start()
        mate_copy(j).start()

    def forward(j):
        landed(ga.at[j, q_side], g_r.at[j, q_side])
        forward_copy(j).start()

    def multiply(j):
        for n in (q_mate, q_diag):
            landed(ga.at[j, n], g_r.at[j, n])
        part = dot(fct[...], ga[j].reshape(tile, piece))
        top, bottom = part[: 4 * half], part[4 * half :]
        yown[j] = jnp.where(y == 0, top, bottom)
        yst[j] = jnp.where(y == 0, bottom, top).astype(bf16)
        part_copy(j).start()

    def scatter(j):
        landed(yrec.at[j], y_r.at[j])
        total = (yown[j] + yrec[j].astype(f32)).astype(bf16)
        for i in range(2):
            for h in range(2):
                pst[j, i, h] = total[(2 * i + h) * half : (2 * i + h + 1) * half]
        for i in range(2):
            for h in range(2):
                @pl.when(away(i, h))
                def _():
                    hop(j, i, h).start()

                @pl.when(jnp.logical_not(away(i, h)))
                def _():
                    prec[j, z] = pst[j, i, h]

    def finish(j):
        for source in range(nb // 2):
            @pl.when(jnp.logical_or(z // 2 != c, z != source))
            def _():
                landed(prec.at[j, source], p_r.at[j, source])
        result = prec[j, 0].astype(f32)
        for source in range(1, nb // 2):
            result = result + prec[j, source].astype(f32)
        out_ref[:, columns_of(j)] = result

    with scope("mate"):
        landed(arec0, a0_r)

    def stages(i, carry):
        @pl.when(i < pieces)
        def _():
            with scope("gather"):
                gather(i)

        @pl.when(jnp.logical_and(x == 1, i + AHEAD < pieces))
        def _():
            with scope("merge"):
                merge(i + AHEAD)

        for lag, name, work in zip(LAGS, ("forward", "multiply", "scatter"), (forward, multiply, scatter)):
            @pl.when(jnp.logical_and(i >= lag, i < pieces + lag))
            def _():
                with scope(name):
                    work(i - lag)

        return carry

    lax.fori_loop(0, pieces + LAGS[-1], stages, 0)

    def close(j, carry):
        with scope("finish"):
            finish(j)
        return carry

    lax.fori_loop(0, pieces, close, 0)

    def drain(j, carry):
        for copy in (side_copy, mate_copy, forward_copy, part_copy):
            copy(j).wait_send()
        for i in range(2):
            for h in range(2):
                @pl.when(away(i, h))
                def _():
                    hop(j, i, h).wait_send()
        return carry

    with scope("drain"):
        lax.fori_loop(0, pieces, drain, 0)
        for j in range(pieces):
            term_copy(1, j).wait_send()
            term_copy(2, j).wait_send()
            across_copy(j).wait_send()
        for j in range(wv.shape[0]):
            along_z(j).wait_send()
            along_x(0, j).wait_send()
        remote(hst, hrec, h_s, h_r, (t, mate)).wait_send()
        for source, semaphore in drains:
            drained(source, semaphore)


def results(loss_ref, grad_ref, loss_out, grad_out):
    loss_out[...] = loss_ref[0]
    grad_out[...] = grad_ref[...]


def fused(features, head_weight, labels, pos_index, pair_mask, loss_weight):
    quarter, depth = features.shape
    width = head_weight.shape[1]
    nb = lax.axis_size("blk")
    share = depth // (4 * nb)
    f32, bf16 = jnp.float32, jnp.bfloat16
    dma = pltpu.SemaphoreType.DMA
    vmem = pl.BlockSpec(memory_space=pltpu.VMEM)
    hbm = pl.BlockSpec(memory_space=pl.ANY)
    block = (quarter, width)
    small = (8, quarter)
    piece = width // PIECES
    loss, grad = pl.pallas_call(
        kernel,
        out_shape=(pltpu.VMEM((1, quarter), f32), pltpu.VMEM((share, width), f32)),
        in_specs=[hbm] * 6,
        out_specs=(vmem, vmem),
        scratch_shapes=[
            pltpu.VMEM((1, quarter), jnp.int32),
            pltpu.VMEM(pos_index.shape[::-1], jnp.int32),
            pltpu.VMEM((1, quarter), f32),
            pltpu.VMEM(pair_mask.shape, jnp.int32),
            pltpu.VMEM((quarter, depth), bf16),
            pltpu.VMEM((3, depth, width // 3), bf16),
            pltpu.VMEM((4,) + block, bf16),
            pltpu.VMEM((3,) + block, bf16),
            pltpu.VMEM((4,) + small, f32),
            pltpu.VMEM((2,) + small, f32),
            pltpu.VMEM((3,) + small, f32),
            pltpu.VMEM((4, 4, quarter, 128), bf16),
            pltpu.VMEM((512, 4 * quarter), bf16),
            pltpu.VMEM((4,) + block, f32),
            pltpu.VMEM((3,) + block, f32),
            pltpu.VMEM((3, quarter, 128), f32),
            pltpu.VMEM((quarter, 2 * quarter), f32),
            pltpu.VMEM((quarter, 2 * quarter), f32),
            pltpu.VMEM((2 * quarter, quarter), f32),
            pltpu.VMEM((quarter, 2 * quarter), bf16),
            pltpu.VMEM((quarter, 2 * quarter), bf16),
            pltpu.VMEM((2, quarter, 4 * quarter), bf16),
            pltpu.VMEM((3, quarter, 128), f32),
            pltpu.VMEM((3, quarter, 128), f32),
            pltpu.VMEM((4,) + small, f32),
            pltpu.VMEM((2 * quarter, 128), f32),
            pltpu.VMEM((3, quarter, 128), f32),
            pltpu.VMEM((3, quarter, 128), f32),
            pltpu.VMEM((4, 4) + small, f32),
            pltpu.VMEM((2,) + small, f32),
            pltpu.VMEM((4, 2) + small, f32),
            pltpu.VMEM((4,) + small, f32),
            pltpu.VMEM((2,) + block, bf16),
            pltpu.VMEM((2,) + block, bf16),
            pltpu.VMEM(block, bf16),
            pltpu.VMEM(block, bf16),
            pltpu.VMEM(block, bf16),
            pltpu.VMEM(block, bf16),
            pltpu.VMEM(block, bf16),
            pltpu.VMEM(block, bf16),
            pltpu.VMEM(block, bf16),
            pltpu.VMEM((PIECES, 4, quarter, piece), bf16),
            pltpu.VMEM((PIECES, 4 * share, piece), f32),
            pltpu.VMEM((PIECES, 4 * share, piece), bf16),
            pltpu.VMEM((PIECES, 4 * share, piece), bf16),
            pltpu.VMEM((PIECES, 2, 2, share, piece), bf16),
            pltpu.VMEM((PIECES, nb // 2, share, piece), bf16),
            dma(()), dma((3,)), dma((3, 3)), dma((4, 3)), dma((3,)), dma((4,)), dma((2, 3)), dma((2, 3)), dma((2,)), dma((2,)),
            dma((3, 4)), dma((4, 4)), dma((3,)), dma((4,)), dma((2, PIECES)), dma((2, PIECES)), dma((PIECES,)), dma(()), dma(()),
            dma((PIECES,)), dma((PIECES,)), dma(()), dma(()), dma((3,)), dma((4,)),
            dma((PIECES, 3)), dma((PIECES, 4)), dma((PIECES,)), dma((PIECES,)), dma((PIECES, 2, 2)), dma((PIECES, nb // 2)), dma((4,)),
        ],
        compiler_params=pltpu.CompilerParams(
            collective_id=0, has_side_effects=True, vmem_limit_bytes=56 * 1024 * 1024
        ),
    )(features, head_weight, labels[None, :], pos_index.T, loss_weight[None, :], pair_mask)
    return pl.pallas_call(
        results,
        out_shape=(jax.ShapeDtypeStruct((quarter,), f32), jax.ShapeDtypeStruct((share, width), f32)),
        in_specs=[vmem] * 2,
        out_specs=(vmem, vmem),
    )(*(pltpu.with_memory_space_constraint(part, pltpu.VMEM) for part in (loss, grad)))


def solution(mesh):
    body = fused if mesh.shape["blk"] == 8 and mesh.shape["rows"] == 4 else local
    return jax.shard_map(
        body,
        mesh=mesh,
        in_specs=(
            P(("blk", "rows"), None),
            P(),
            P(("blk", "rows")),
            P(("blk", "rows"), None),
            P("blk", None),
            P(("blk", "rows")),
        ),
        out_specs=(P(("blk", "rows")), P(("blk", "rows"), None)),
        check_vma=False,
    )
```

```python
import contextlib
import math

import jax
import jax.numpy as jnp
from jax import lax
from jax.experimental import pallas as pl
from jax.experimental.pallas import tpu as pltpu
from jax.sharding import PartitionSpec as P

SMOOTHING_SCALE = 16.0
SLACK_GAP = 0.1


def passed_along(block, axis, distance):
    devices = range(lax.axis_size(axis))
    route = [((i - distance) % len(devices), i) for i in devices]
    return lax.ppermute(block, axis, route)


def score_tile(
    anchors, anchor_sq, anchor_labels, matching_separation, weights, tile_rows, tile_labels, listed
):
    matching_samples = matching_separation.shape[1]
    block_tally = tile_rows.shape[0]
    anchor_count = anchors.shape[0]

    def compute(unused):
        products = lax.dot_general(
            anchors, tile_rows, (((1,), (1,)), ((), ())), preferred_element_type=jnp.float32
        )
        widened = tile_rows.astype(jnp.float32)
        tile_sq = jnp.sum(widened * widened, axis=1)
        couple_separation = anchor_sq[:, None] + tile_sq[None, :] - 2.0 * products
        valid = (anchor_labels[:, None] != tile_labels[None, :]).astype(jnp.float32)
        weighting = weights / (matching_samples * block_tally)
        objective_accrued = jnp.zeros((anchor_count,), jnp.float32)
        coefficient = jnp.zeros((anchor_count, block_tally), jnp.float32)
        totals = []
        for target_slot in range(matching_samples):
            slack_excess = SMOOTHING_SCALE * (
                matching_separation[:, target_slot : target_slot + 1]
                - couple_separation
                + SLACK_GAP
            )
            objective_accrued = objective_accrued + jnp.sum(
                valid * jax.nn.softplus(slack_excess), axis=1
            )
            sigmoids = valid * jax.nn.sigmoid(slack_excess)
            coefficient = coefficient + sigmoids
            totals.append(jnp.sum(sigmoids, axis=1))
        objective_accrued = objective_accrued / (SMOOTHING_SCALE * matching_samples * block_tally)
        coefficient = coefficient * weighting[:, None]
        pos_coef = jnp.stack(totals, axis=1) * weighting[:, None]
        coef_low = coefficient.astype(jnp.bfloat16)
        anchor_grad = 2.0 * jnp.dot(coef_low, tile_rows, preferred_element_type=jnp.float32)
        pulled = lax.dot_general(
            coef_low, anchors, (((0,), (0,)), ((), ())), preferred_element_type=jnp.float32
        )
        col_sums = jnp.sum(coefficient, axis=0)
        tile_grad = 2.0 * (pulled - col_sums[:, None] * widened)
        return (objective_accrued, pos_coef, anchor_grad, tile_grad, coef_low, col_sums)

    def skip(unused):
        return (
            jnp.zeros((anchor_count,), jnp.float32),
            jnp.zeros((anchor_count, matching_samples), jnp.float32),
            jnp.zeros((anchor_count, anchors.shape[1]), jnp.float32),
            jnp.zeros((block_tally, anchors.shape[1]), jnp.float32),
            jnp.zeros((anchor_count, block_tally), jnp.bfloat16),
            jnp.zeros((block_tally,), jnp.float32),
        )

    return lax.cond(listed, compute, skip, 0)


def local(features, head_weight, labels, pos_index, pair_mask, loss_weight):
    embedded = jnp.dot(features, head_weight, preferred_element_type=jnp.float32).astype(
        jnp.bfloat16
    )
    widened = embedded.astype(jnp.float32)
    anchor_sq = jnp.sum(widened * widened, axis=1)
    tile_rows, tile_labels = (
        lax.all_gather(embedded, "rows", axis=0, tiled=True),
        lax.all_gather(labels, "rows", axis=0, tiled=True),
    )
    pos_rows = tile_rows[pos_index]
    pos_wide = pos_rows.astype(jnp.float32)
    pos_sq = jnp.sum(pos_wide * pos_wide, axis=2)
    matching_separation = (
        anchor_sq[:, None]
        + pos_sq
        - 2.0 * jnp.einsum("ad,akd->ak", embedded, pos_rows, preferred_element_type=jnp.float32)
    )
    offsets = pair_mask.shape[1]
    loss_total, coef_total, grad_total, own_term, first_low, first_sums = score_tile(
        embedded,
        anchor_sq,
        labels,
        matching_separation,
        loss_weight,
        tile_rows,
        tile_labels,
        pair_mask[0, 0] > 0,
    )
    received = jnp.zeros_like(own_term)
    walk_rows, walk_labels = (tile_rows, tile_labels)
    for offset in range(1, offsets):
        walk_rows, walk_labels = passed_along((walk_rows, walk_labels), "blk", 1)
        loss_part, coef_part, grad_part, term_part, low_part, sums_part = score_tile(
            embedded,
            anchor_sq,
            labels,
            matching_separation,
            loss_weight,
            walk_rows,
            walk_labels,
            pair_mask[0, offset] > 0,
        )
        loss_total = loss_total + loss_part
        coef_total = coef_total + coef_part
        grad_total = grad_total + grad_part
        received = received + passed_along(term_part.astype(jnp.bfloat16), "blk", -offset).astype(
            term_part.dtype
        )
    grad_total = grad_total - 2.0 * jnp.sum(coef_total[:, :, None] * pos_wide, axis=1)
    pushed = 2.0 * coef_total[:, :, None] * (pos_wide - widened[:, None, :])
    own_term = own_term.at[pos_index.reshape(-1)].add(pushed.reshape(-1, pushed.shape[2]))
    quarter_sum = lax.psum_scatter(own_term + received, "rows", scatter_dimension=0, tiled=True)
    emb_grad = grad_total + quarter_sum
    grad_low = emb_grad.astype(jnp.bfloat16)
    weight_grad = lax.psum_scatter(
        lax.dot_general(
            features, grad_low, (((0,), (0,)), ((), ())), preferred_element_type=jnp.float32
        ),
        ("blk", "rows"),
        scatter_dimension=0,
        tiled=True,
    )
    return (loss_total, weight_grad)


MESH = pl.DeviceIdType.MESH
NT = (((1,), (1,)), ((), ()))
TN = (((0,), (0,)), ((), ()))


def dot(a, b, dims=(((1,), (0,)), ((), ()))):
    return lax.dot_general(a, b, dims, preferred_element_type=jnp.float32)


LOG2E = math.log2(math.e)
LN2 = math.log(2.0)
CEILING = 40.0
FAR = 1e38
PIECES = 6
SUB = 32
TILES = (0, 2, 1, 1, 0, 2)
SIDES = (0, 1, 1, 0, 1, 0)
AHEAD = 3
STEPS = len(TILES)


def last_of(codes, value):
    return max(i for i, code in enumerate(codes) if code == value)


LAGS = (3, 4, 6)


def scope(name):
    return contextlib.nullcontext()


def spread_rows(row):
    return jnp.transpose(jnp.broadcast_to(row, (128, row.shape[1])))


def twice(block):
    return jnp.concatenate([block, block], axis=1)


def by_eights(block):
    total = block[0:8]
    for i in range(1, block.shape[0] // 8):
        total = total + block[8 * i : 8 * i + 8]
    return total


def kernel(
    f_hbm, w_hbm, lab_hbm, pos_hbm, wgt_hbm, mask_hbm, loss_ref, out_ref,
    lab_ref, pos_ref, wgt_ref, mask_ref, fv, wv, ea, nr, meta, metan, scored, fc, fct, acc, pul, cs, prod, prod2, gram, low, low2, comb, place, pulled, dpr, sqc, labc, sqn, stp, st, strec, tot,
    tst, trec, relay, ast0, arec0, ast1, arec1, hst, hrec, ga, yown, yst, yrec, pst, prec,
    f_l, w_l, ea_s, ea_r, ma_s, ma_r, en_s, en_r, mn_s, mn_r, fc_s, fc_r, d_s, d_r, t_s, t_r, rl_r, a0_s, a0_r, a1_s, a1_r,
    h_s, h_r, st_s, st_r, g_s, g_r, y_s, y_r, p_s, p_r, i_s,
):
    nb = lax.axis_size("blk")
    t = lax.axis_index("blk")
    r = lax.axis_index("rows")
    z, x = t // 2, t % 2
    y, c = r // 2, r % 2
    tx = 2 * z + 1 - x
    mate = 2 * y + 1 - c
    across = 2 * (1 - y) + c
    diag = 2 * (1 - y) + 1 - c
    peers = (mate, across, diag)
    q = 2 * x + c
    q_mate, q_side, q_diag = 2 * x + 1 - c, 2 * (1 - x) + c, 2 * (1 - x) + 1 - c
    quarter, depth = f_hbm.shape
    width = w_hbm.shape[1]
    tile = 4 * quarter
    pieces = ga.shape[0]
    piece = width // pieces
    half = out_ref.shape[0]
    f32, bf16 = jnp.float32, jnp.bfloat16
    scale = SMOOTHING_SCALE * LOG2E

    def remote(src, dst, ss, rs, dev):
        return pltpu.make_async_remote_copy(
            src_ref=src, dst_ref=dst, send_sem=ss, recv_sem=rs, device_id=dev, device_id_type=MESH
        )

    drains = []

    def push(src, dst, ss, rs, dev):
        remote(src, dst, ss, rs, dev).start()

    def push_drained(src, dst, ss, rs, dev):
        push(src, dst, ss, rs, dev)
        drains.append((src, ss))

    def landed(dst, rs):
        remote(dst, dst, ea_s.at[0], rs, (t, mate)).wait_recv()

    def drained(src, ss):
        remote(src, src, ss, ea_r.at[0, 0], (t, mate)).wait_send()

    columns = width // wv.shape[0]
    f_copy = pltpu.make_async_copy(f_hbm, fv, f_l)
    w_copies = [
        pltpu.make_async_copy(w_hbm.at[:, j * columns : (j + 1) * columns], wv.at[j], w_l.at[j])
        for j in range(wv.shape[0])
    ]
    f_copy.start()
    w_copies[0].start()
    small_copies = [
        pltpu.make_async_copy(source, target, i_s.at[n])
        for n, (source, target) in enumerate(
            ((lab_hbm, lab_ref), (pos_hbm, pos_ref), (wgt_hbm, wgt_ref), (mask_hbm, mask_ref))
        )
    ]
    for copy in small_copies:
        copy.start()

    barrier = pltpu.get_barrier_semaphore()
    for step in range(nb):
        for row in range(4):
            if step or row:
                pl.semaphore_signal(barrier, inc=1, device_id=((t + step) % nb, (r + row) % 4), device_id_type=MESH)

    with scope("small"):
        for copy in small_copies:
            copy.wait()
    meta[r] = jnp.zeros(meta.shape[1:], f32)
    meta[r, 0:1, :] = lab_ref[...].astype(f32)
    meta[r, 1:4, :] = pos_ref[...].astype(f32)
    meta[r, 4:5, :] = wgt_ref[...]
    for s in range(3):
        scored[s] = jnp.broadcast_to((mask_ref[0:1, s : s + 1] > 0).astype(f32), (8, quarter))

    def along_z(j):
        cut = slice(j * columns, (j + 1) * columns)
        return remote(nr.at[0, :, cut], nr.at[2, :, cut], en_s.at[1], en_r.at[1, j], ((t + 2) % nb, r))

    def along_x(held, j):
        cut = slice(j * columns, (j + 1) * columns)
        return remote(nr.at[held, :, cut], nr.at[1, :, cut], en_s.at[0], en_r.at[0, j], (tx, r))

    def block_column(px, pc, i):
        return pl.multiple_of((4 * (2 * pc + i % 2) + 2 * px + i // 2) * 128, 128)

    def send_features(i):
        for n, (px, pc) in enumerate(((x, 1 - c), (1 - x, c), (1 - x, 1 - c))):
            dev = (2 * z + px, 2 * y + pc)
            push(fv.at[:, pl.ds(block_column(px, pc, i), 128)], fc.at[q, i], fc_s.at[n], fc_r.at[q], dev)

    f_copy.wait()
    for copy in w_copies[1:]:
        copy.start()
    square = jnp.zeros((quarter, 1), f32)
    for j in range(wv.shape[0]):
        with scope("embed"):
            w_copies[j].wait()
            cut = slice(j * columns, (j + 1) * columns)
            part = dot(fv[...], wv[j]).astype(bf16)
            ea[r, :, cut] = part
            nr[0, :, cut] = part
            wide = part.astype(f32)
            square = square + jnp.sum(wide * wide, axis=1, keepdims=True)
        if j == 0:
            with scope("barrier"):
                pl.semaphore_wait(barrier, 4 * nb - 1)
        for n, peer in ((1, across), (0, mate)):
            push(ea.at[r, :, cut], ea.at[r, :, cut], ea_s.at[n], ea_r.at[r, j], (t, peer))
        along_z(j).start()
        if j == 0:
            send_features(0)

        @pl.when(x == 0)
        def _():
            along_x(0, j).start()

    meta[r, 5:6, :] = jnp.transpose(jnp.broadcast_to(square, (quarter, 128)))[0:1, :]
    for n, peer in enumerate(peers):
        push_drained(meta.at[r], meta.at[r], ma_s.at[n], ma_r.at[r], (t, peer))
    for s in (1, 2):
        push_drained(meta.at[r], metan.at[s - 1], mn_s.at[s - 1], mn_r.at[s - 1], ((t + s) % nb, r))
    for i in range(4):
        fc[q, i] = fv[:, pl.ds(block_column(x, c, i), 128)]

    labc[0] = spread_rows(meta[r, 0:1, :])
    for a in range(4):
        stp[a] = jnp.zeros(stp.shape[1:], f32)
    for s in range(3):
        cs[s] = jnp.zeros((quarter, 128), f32)

    @pl.when(x == 1)
    def _():
        trec[0] = jnp.zeros((quarter, width), bf16)

    sub = lax.broadcasted_iota(jnp.int32, (SUB, quarter), 0).astype(f32)

    def side_rows(side):
        return ea[pl.ds(2 * side, 2)].reshape(2 * quarter, width)

    def positives(first, count, found):
        rows_here = ea[pl.ds(first, count)].reshape(count * quarter, width)
        gram[0 : count * quarter] = dot(rows_here, ea[r], NT)
        places = [meta[r, 1 + k : 2 + k, :] for k in range(3)]
        for h in range(count):
            sqc[h * quarter : (h + 1) * quarter] = spread_rows(meta[first + h, 5:6, :])

        def rows(i, found):
            at = pl.ds(pl.multiple_of(i * SUB, SUB), SUB)
            d = twice(sqc[at]) - 2.0 * gram[at]
            base = (first * quarter + i * SUB).astype(f32)
            return tuple(found[k] + by_eights(jnp.where(sub == places[k] - base, d, 0.0)) for k in range(3))

        return lax.fori_loop(0, count * quarter // SUB, rows, found)

    with scope("own_rows"):
        for j in range(wv.shape[0]):
            landed(ea.at[mate, :, j * columns : (j + 1) * columns], ea_r.at[mate, j])
        landed(meta.at[mate], ma_r.at[mate])
        found = positives(2 * y, 2, tuple(jnp.zeros((8, quarter), f32) for _ in range(3)))
        prod[...] = dot(nr[0], side_rows(y), NT)

    def tile_columns(s, block):
        labc[s] = spread_rows(block[0:1, :])
        sqn[s] = scale * spread_rows(block[5:6, :])

    tile_columns(0, meta[r])
    with scope("rows"):
        for j in range(wv.shape[0]):
            cut = slice(j * columns, (j + 1) * columns)
            landed(ea.at[across, :, cut], ea_r.at[across, j])
            push(ea.at[across, :, cut], ea.at[across, :, cut], ea_s.at[2], ea_r.at[across, j], (t, mate))

            @pl.when(x == 1)
            def _():
                landed(nr.at[2, :, cut], en_r.at[1, j])
                along_x(2, j).start()

        landed(meta.at[across], ma_r.at[across])

    for i in range(1, 4):
        send_features(i)
    with scope("positives"):
        found = positives(across, 1, found)
        for j in range(wv.shape[0]):
            landed(ea.at[diag, :, j * columns : (j + 1) * columns], ea_r.at[diag, j])
        landed(meta.at[diag], ma_r.at[diag])
        found = positives(diag, 1, found)
        for k in range(3):
            dpr[r, k : k + 1, :] = scale * (jnp.sum(found[k], axis=0, keepdims=True) + SLACK_GAP)
        dpr[r, 3:8, :] = jnp.zeros((5, quarter), f32)
    for n, peer in enumerate(peers):
        push_drained(dpr.at[r], dpr.at[r], d_s.at[n], d_r.at[r], (t, peer))


    def pairs(s, side, prod, low):
        on = scored[s, 0:1, :] > 0.0
        for g in range(2):
            a = 2 * side + g
            cut = slice(g * quarter, (g + 1) * quarter)
            tops = [jnp.where(on, dpr[a, k : k + 1, :], -FAR) for k in range(3)]
            names = meta[a, 0:1, :]
            weight = meta[a, 4:5, :] * (1.0 / (3.0 * tile))
            sums = [jnp.zeros((8, quarter), f32)] * 4
            for i in range(quarter // SUB):
                at = slice(i * SUB, (i + 1) * SUB)
                spread = twice(sqn[s, at]) - (2.0 * scale) * prod[at, cut]
                spread = jnp.where(twice(labc[s, at]) != names, spread, FAR)
                e, over = [], None
                for k in range(3):
                    h = tops[k] - spread
                    m = jnp.minimum(h, CEILING)
                    e.append(jnp.exp2(m))
                    over = h - m if over is None else over + (h - m)
                one = [1.0 + v for v in e]
                p = (e[0] + one[0] * e[1]) * one[2] + e[2]
                u = 1.0 + p
                inv = 1.0 / u
                logs = LN2 * (jnp.log2(u) + over) + (p - (u - 1.0)) * inv
                last = inv * one[2]
                sig = (e[0] * (last * one[1]), e[1] * (last * one[0]), e[2] * (inv * (one[0] * one[1])))
                coef = (sig[0] + sig[1] + sig[2]) * weight
                low[at, cut] = coef.astype(bf16)
                cs[s, at] += coef[:, :128] + coef[:, 128:]
                sums = [v + by_eights(w) for v, w in zip(sums, (logs,) + sig)]
            for k in range(4):
                stp[2 * side + g, k] += sums[k]

    def products(i, low):
        s, side = TILES[i], side_of(i)
        pulled_here = dot(low[...], side_rows(side))
        gained_here = dot(low[...], nr[s], TN).reshape(2, quarter, width)
        if TILES.index(s) == i:
            pul[s] = pulled_here
        else:
            pul[s] += pulled_here
        if SIDES.index(SIDES[i]) == i:
            acc[pl.ds(2 * side, 2)] = gained_here
        else:
            acc[pl.ds(2 * side, 2)] += gained_here

    def sums_over_lanes(s):
        return jnp.sum(cs[s], axis=1, keepdims=True)

    def term_value(s):
        return 2.0 * (pul[s] - sums_over_lanes(s) * nr[s].astype(f32))

    def columns_of(j):
        return pl.ds(pl.multiple_of(j * piece, piece), piece)

    def term_copy(s, j):
        cut = columns_of(j)
        return remote(
            tst.at[s - 1, :, cut], trec.at[s - 1, :, cut], t_s.at[s - 1], t_r.at[s - 1, j], ((t + nb - s) % nb, r)
        )

    def relay_copy(j):
        cut = columns_of(j)
        return remote(tst.at[0, :, cut], relay.at[:, cut], t_s.at[0], rl_r.at[j], (tx, r))

    def send_first():
        tst[0] = term_value(1).astype(bf16)
        for j in range(pieces):
            pl.when(x == 0)(lambda: relay_copy(j).start())
            pl.when(x == 1)(lambda: term_copy(1, j).start())

    def send_second():
        pul[2] = term_value(2)

        @pl.when(x == 0)
        def _():
            tst[1] = pul[2].astype(bf16)
            for j in range(pieces):
                term_copy(2, j).start()

    def merge(j):
        cut = columns_of(j)
        landed(relay.at[:, cut], rl_r.at[j])
        tst[1, :, cut] = (pul[2, :, cut] + relay[:, cut].astype(f32)).astype(bf16)
        term_copy(2, j).start()

    def merge_on_x1(j):
        pl.when(x == 1)(lambda: merge(j))

    def across_copy(j):
        cut = columns_of(j)
        return remote(ast1.at[:, cut], arec1.at[:, cut], a1_s, a1_r.at[j], (t, across))

    def side_of(i):
        return 1 - y if SIDES[i] else y

    def tile_arrives(s):
        for j in range(wv.shape[0]):
            @pl.when(jnp.logical_or(s == 1, x == 0))
            def _():
                landed(nr.at[s, :, j * columns : (j + 1) * columns], en_r.at[s - 1, j])

        landed(metan.at[s - 1], mn_r.at[s - 1])
        tile_columns(s, metan[s - 1])

    def send_hst():
        hst[...] = (2.0 * acc[diag]).astype(bf16)
        remote(hst, hrec, h_s, h_r, (t, mate)).start()

    def send_ast():
        landed(hrec, h_r)
        ast1[...] = (2.0 * acc[across] + hrec[...].astype(f32)).astype(bf16)
        for j in range(pieces):
            across_copy(j).start()

    def step(i, held, coming, low, before):
        arriving = i == TILES.index(1) - 1

        def next_product():
            if i + 1 < STEPS:
                coming[...] = dot(nr[TILES[i + 1]], side_rows(side_of(i + 1)), NT)

        if i == SIDES.index(1):
            with scope("distances"):
                for peer in (across, diag):
                    landed(dpr.at[peer], d_r.at[peer])
        with scope("chunk"):
            if not arriving:
                next_product()
            if i:
                products(i - 1, before)
            if i == last_of(TILES, 1) + 1:
                send_first()
            if i == last_of(SIDES, 1) + 1:
                send_hst()
            pairs(TILES[i], side_of(i), held, low)
        if arriving:
            with scope("tile1"):
                tile_arrives(1)
            next_product()

    with scope("tile2"):
        tile_arrives(2)
    with scope("distance"):
        landed(dpr.at[mate], d_r.at[mate])
    with scope("scores"):
        for i in range(0, STEPS, 2):
            step(i, prod, prod2, low, low2)
            step(i + 1, prod2, prod, low2, low)

    for a in range(4):
        for k in range(4):
            row = 4 * (a % 2) + k
            st[a // 2, row : row + 1, :] = jnp.sum(stp[a, k], axis=0, keepdims=True)
    for n, peer in enumerate(peers):
        push_drained(st, strec.at[r], st_s.at[n], st_r.at[r], (t, peer))
    with scope("last"):
        products(STEPS - 1, low2)
        send_second()
        merge_on_x1(0)
        send_ast()
        merge_on_x1(1)
        ast0[...] = (2.0 * acc[mate]).astype(bf16)
        push_drained(ast0, arec0, a0_s, a0_r, (t, mate))

    def features():
        with scope("features"):
            for n in (q_mate, q_side, q_diag):
                landed(fc.at[n], fc_r.at[n])
            for n in range(4):
                for i in range(4):
                    fct[i * 128 : (i + 1) * 128, n * quarter : (n + 1) * quarter] = jnp.transpose(fc[n, i])

    strec[r] = st[...]
    features()
    merge_on_x1(2)
    with scope("statistics"):
        for peer in peers:
            landed(strec.at[peer], st_r.at[peer])
    for a in range(4):
        part = slice(4 * (a % 2), 4 * (a % 2) + 4)
        tot[a, 0:4, :] = (
            strec[0, a // 2, part] + strec[1, a // 2, part] + strec[2, a // 2, part] + strec[3, a // 2, part]
        )
    loss_ref[...] = tot[r, 0:1, :] * (1.0 / (SMOOTHING_SCALE * 3.0 * tile))

    with scope("pulls"):
        row_sub = lax.broadcasted_iota(jnp.int32, (SUB, quarter), 0).astype(f32)
        lane = lax.broadcasted_iota(jnp.int32, (SUB, quarter), 1).astype(f32)
        share = 1.0 / (3.0 * tile)
        for k in range(3):
            place[k] = spread_rows(meta[r, 1 + k : 2 + k, :])
            pulled[k] = spread_rows(tot[r, 1 + k : 2 + k, :] * meta[r, 4:5, :] * share)

        def listed(i, carry):
            at = pl.ds(pl.multiple_of(i * SUB, SUB), SUB)
            first = (r * quarter + i * SUB).astype(f32)
            gained = jnp.zeros((SUB, 128), f32)
            for n in range(4):
                given = jnp.zeros((SUB, quarter), f32)
                wgt = meta[n, 4:5, :] * share
                for k in range(3):
                    hit = row_sub == meta[n, 1 + k : 2 + k, :] - first
                    given = given + jnp.where(hit, tot[n, 1 + k : 2 + k, :] * wgt, 0.0)
                gained = gained + (given[:, :128] + given[:, 128:])
                for k in range(3):
                    hit = lane == twice(place[k, at]) - float(n * quarter)
                    given = given + jnp.where(hit, twice(pulled[k, at]), 0.0)
                high = given.astype(bf16)
                comb[0, at, n * quarter : (n + 1) * quarter] = high
                comb[1, at, n * quarter : (n + 1) * quarter] = (given - high.astype(f32)).astype(bf16)
            cs[1, at] = gained
            return carry

        lax.fori_loop(0, quarter // SUB, listed, 0)
        cs[2] = jnp.broadcast_to(sums_over_lanes(1) - sums_over_lanes(0), (quarter, 128))

    def side_copy(j):
        return remote(ga.at[j, q], ga.at[j, q], g_s.at[1], g_r.at[j, q], (tx, r))

    def mate_copy(j):
        return remote(ga.at[j, q], ga.at[j, q], g_s.at[0], g_r.at[j, q], (t, mate))

    def forward_copy(j):
        return remote(ga.at[j, q_side], ga.at[j, q_side], g_s.at[2], g_r.at[j, q_side], (t, mate))

    def part_copy(j):
        return remote(yst.at[j], yrec.at[j], y_s, y_r.at[j], (t, across))

    def hop(j, i, h):
        return remote(
            pst.at[j, i, h], prec.at[j, z], p_s.at[i, h], p_r.at[j, z], (2 * (2 * c + i) + x, 2 * y + h)
        )

    def away(i, h):
        return jnp.logical_or(2 * c + i != z, c != h)

    def gather(j):
        cut = columns_of(j)
        rows_cut = ea[:, :, cut].reshape(tile, piece)
        net = acc[r, :, cut] + pul[0, :, cut] + cs[2, :, :piece] * ea[r, :, cut].astype(f32)
        net = net - dot(comb[0], rows_cut) - dot(comb[1], rows_cut)
        total = 2.0 * net + arec0[:, cut].astype(f32)
        landed(arec1.at[:, cut], a1_r.at[j])
        total = total + arec1[:, cut].astype(f32)
        @pl.when(x == 0)
        def _():
            landed(trec.at[0, :, cut], t_r.at[0, j])

        landed(trec.at[1, :, cut], t_r.at[1, j])
        total = total + trec[0, :, cut].astype(f32) + trec[1, :, cut].astype(f32)
        ga[j, q] = total.astype(bf16)
        side_copy(j).start()
        mate_copy(j).start()

    def forward(j):
        landed(ga.at[j, q_side], g_r.at[j, q_side])
        forward_copy(j).start()

    def multiply(j):
        for n in (q_mate, q_diag):
            landed(ga.at[j, n], g_r.at[j, n])
        part = dot(fct[...], ga[j].reshape(tile, piece))
        top, bottom = part[: 4 * half], part[4 * half :]
        yown[j] = jnp.where(y == 0, top, bottom)
        yst[j] = jnp.where(y == 0, bottom, top).astype(bf16)
        part_copy(j).start()

    def scatter(j):
        landed(yrec.at[j], y_r.at[j])
        total = (yown[j] + yrec[j].astype(f32)).astype(bf16)
        for i in range(2):
            for h in range(2):
                pst[j, i, h] = total[(2 * i + h) * half : (2 * i + h + 1) * half]
        for i in range(2):
            for h in range(2):
                @pl.when(away(i, h))
                def _():
                    hop(j, i, h).start()

                @pl.when(jnp.logical_not(away(i, h)))
                def _():
                    prec[j, z] = pst[j, i, h]

    def finish(j):
        for source in range(nb // 2):
            @pl.when(jnp.logical_or(z // 2 != c, z != source))
            def _():
                landed(prec.at[j, source], p_r.at[j, source])
        result = prec[j, 0].astype(f32)
        for source in range(1, nb // 2):
            result = result + prec[j, source].astype(f32)
        out_ref[:, columns_of(j)] = result

    with scope("mate"):
        landed(arec0, a0_r)

    def stages(i, carry):
        @pl.when(i < pieces)
        def _():
            with scope("gather"):
                gather(i)

        @pl.when(jnp.logical_and(x == 1, i + AHEAD < pieces))
        def _():
            with scope("merge"):
                merge(i + AHEAD)

        for lag, name, work in zip(LAGS, ("forward", "multiply", "scatter"), (forward, multiply, scatter)):
            @pl.when(jnp.logical_and(i >= lag, i < pieces + lag))
            def _():
                with scope(name):
                    work(i - lag)

        return carry

    lax.fori_loop(0, pieces + LAGS[-1], stages, 0)

    def close(j, carry):
        with scope("finish"):
            finish(j)
        return carry

    lax.fori_loop(0, pieces, close, 0)

    with scope("drain"):
        for n, source in enumerate((q, q, q_side)):
            drained(ga.at[:, source], g_s.at[n])
        drained(yst, y_s)
        for i in range(2):
            for h in range(2):
                @pl.when(away(i, h))
                def _():
                    drained(pst.at[:, i, h], p_s.at[i, h])
        for n, source in enumerate((mate, r, across)):
            drained(ea.at[source], ea_s.at[n])
        for n in range(2):
            drained(nr.at[n], en_s.at[n])
            drained(tst.at[n], t_s.at[n])
        for n in range(3):
            drained(fc.at[q], fc_s.at[n])
        drained(ast1, a1_s)
        drained(hst, h_s)
        for source, semaphore in drains:
            drained(source, semaphore)


def results(loss_ref, grad_ref, loss_out, grad_out):
    loss_out[...] = loss_ref[0]
    grad_out[...] = grad_ref[...]


def fused(features, head_weight, labels, pos_index, pair_mask, loss_weight):
    quarter, depth = features.shape
    width = head_weight.shape[1]
    nb = lax.axis_size("blk")
    share = depth // (4 * nb)
    f32, bf16 = jnp.float32, jnp.bfloat16
    dma = pltpu.SemaphoreType.DMA
    vmem = pl.BlockSpec(memory_space=pltpu.VMEM)
    hbm = pl.BlockSpec(memory_space=pl.ANY)
    block = (quarter, width)
    small = (8, quarter)
    piece = width // PIECES
    loss, grad = pl.pallas_call(
        kernel,
        out_shape=(pltpu.VMEM((1, quarter), f32), pltpu.VMEM((share, width), f32)),
        in_specs=[hbm] * 6,
        out_specs=(vmem, vmem),
        scratch_shapes=[
            pltpu.VMEM((1, quarter), jnp.int32),
            pltpu.VMEM(pos_index.shape[::-1], jnp.int32),
            pltpu.VMEM((1, quarter), f32),
            pltpu.VMEM(pair_mask.shape, jnp.int32),
            pltpu.VMEM((quarter, depth), bf16),
            pltpu.VMEM((3, depth, width // 3), bf16),
            pltpu.VMEM((4,) + block, bf16),
            pltpu.VMEM((3,) + block, bf16),
            pltpu.VMEM((4,) + small, f32),
            pltpu.VMEM((2,) + small, f32),
            pltpu.VMEM((3,) + small, f32),
            pltpu.VMEM((4, 4, quarter, 128), bf16),
            pltpu.VMEM((512, 4 * quarter), bf16),
            pltpu.VMEM((4,) + block, f32),
            pltpu.VMEM((3,) + block, f32),
            pltpu.VMEM((3, quarter, 128), f32),
            pltpu.VMEM((quarter, 2 * quarter), f32),
            pltpu.VMEM((quarter, 2 * quarter), f32),
            pltpu.VMEM((2 * quarter, quarter), f32),
            pltpu.VMEM((quarter, 2 * quarter), bf16),
            pltpu.VMEM((quarter, 2 * quarter), bf16),
            pltpu.VMEM((2, quarter, 4 * quarter), bf16),
            pltpu.VMEM((3, quarter, 128), f32),
            pltpu.VMEM((3, quarter, 128), f32),
            pltpu.VMEM((4,) + small, f32),
            pltpu.VMEM((2 * quarter, 128), f32),
            pltpu.VMEM((3, quarter, 128), f32),
            pltpu.VMEM((3, quarter, 128), f32),
            pltpu.VMEM((4, 4) + small, f32),
            pltpu.VMEM((2,) + small, f32),
            pltpu.VMEM((4, 2) + small, f32),
            pltpu.VMEM((4,) + small, f32),
            pltpu.VMEM((2,) + block, bf16),
            pltpu.VMEM((2,) + block, bf16),
            pltpu.VMEM(block, bf16),
            pltpu.VMEM(block, bf16),
            pltpu.VMEM(block, bf16),
            pltpu.VMEM(block, bf16),
            pltpu.VMEM(block, bf16),
            pltpu.VMEM(block, bf16),
            pltpu.VMEM(block, bf16),
            pltpu.VMEM((PIECES, 4, quarter, piece), bf16),
            pltpu.VMEM((PIECES, 4 * share, piece), f32),
            pltpu.VMEM((PIECES, 4 * share, piece), bf16),
            pltpu.VMEM((PIECES, 4 * share, piece), bf16),
            pltpu.VMEM((PIECES, 2, 2, share, piece), bf16),
            pltpu.VMEM((PIECES, nb // 2, share, piece), bf16),
            dma(()), dma((3,)), dma((3,)), dma((4, 3)), dma((3,)), dma((4,)), dma((2,)), dma((2, 3)), dma((2,)), dma((2,)),
            dma((3,)), dma((4,)), dma((3,)), dma((4,)), dma((2,)), dma((2, PIECES)), dma((PIECES,)), dma(()), dma(()),
            dma(()), dma((PIECES,)), dma(()), dma(()), dma((3,)), dma((4,)),
            dma((3,)), dma((PIECES, 4)), dma(()), dma((PIECES,)), dma((2, 2)), dma((PIECES, nb // 2)), dma((4,)),
        ],
        compiler_params=pltpu.CompilerParams(
            collective_id=0, has_side_effects=True, vmem_limit_bytes=56 * 1024 * 1024
        ),
    )(features, head_weight, labels[None, :], pos_index.T, loss_weight[None, :], pair_mask)
    return pl.pallas_call(
        results,
        out_shape=(jax.ShapeDtypeStruct((quarter,), f32), jax.ShapeDtypeStruct((share, width), f32)),
        in_specs=[vmem] * 2,
        out_specs=(vmem, vmem),
    )(*(pltpu.with_memory_space_constraint(part, pltpu.VMEM) for part in (loss, grad)))


def solution(mesh):
    body = fused if mesh.shape["blk"] == 8 and mesh.shape["rows"] == 4 else local
    return jax.shard_map(
        body,
        mesh=mesh,
        in_specs=(
            P(("blk", "rows"), None),
            P(),
            P(("blk", "rows")),
            P(("blk", "rows"), None),
            P("blk", None),
            P(("blk", "rows")),
        ),
        out_specs=(P(("blk", "rows")), P(("blk", "rows"), None)),
        check_vma=False,
    )
```

```python
import contextlib
import math

import jax
import jax.numpy as jnp
from jax import lax
from jax.experimental import pallas as pl
from jax.experimental.pallas import tpu as pltpu
from jax.sharding import PartitionSpec as P

SMOOTHING_SCALE = 16.0
SLACK_GAP = 0.1


def passed_along(block, axis, distance):
    devices = range(lax.axis_size(axis))
    route = [((i - distance) % len(devices), i) for i in devices]
    return lax.ppermute(block, axis, route)


def score_tile(
    anchors, anchor_sq, anchor_labels, matching_separation, weights, tile_rows, tile_labels, listed
):
    matching_samples = matching_separation.shape[1]
    block_tally = tile_rows.shape[0]
    anchor_count = anchors.shape[0]

    def compute(unused):
        products = lax.dot_general(
            anchors, tile_rows, (((1,), (1,)), ((), ())), preferred_element_type=jnp.float32
        )
        widened = tile_rows.astype(jnp.float32)
        tile_sq = jnp.sum(widened * widened, axis=1)
        couple_separation = anchor_sq[:, None] + tile_sq[None, :] - 2.0 * products
        valid = (anchor_labels[:, None] != tile_labels[None, :]).astype(jnp.float32)
        weighting = weights / (matching_samples * block_tally)
        objective_accrued = jnp.zeros((anchor_count,), jnp.float32)
        coefficient = jnp.zeros((anchor_count, block_tally), jnp.float32)
        totals = []
        for target_slot in range(matching_samples):
            slack_excess = SMOOTHING_SCALE * (
                matching_separation[:, target_slot : target_slot + 1]
                - couple_separation
                + SLACK_GAP
            )
            objective_accrued = objective_accrued + jnp.sum(
                valid * jax.nn.softplus(slack_excess), axis=1
            )
            sigmoids = valid * jax.nn.sigmoid(slack_excess)
            coefficient = coefficient + sigmoids
            totals.append(jnp.sum(sigmoids, axis=1))
        objective_accrued = objective_accrued / (SMOOTHING_SCALE * matching_samples * block_tally)
        coefficient = coefficient * weighting[:, None]
        pos_coef = jnp.stack(totals, axis=1) * weighting[:, None]
        coef_low = coefficient.astype(jnp.bfloat16)
        anchor_grad = 2.0 * jnp.dot(coef_low, tile_rows, preferred_element_type=jnp.float32)
        pulled = lax.dot_general(
            coef_low, anchors, (((0,), (0,)), ((), ())), preferred_element_type=jnp.float32
        )
        col_sums = jnp.sum(coefficient, axis=0)
        tile_grad = 2.0 * (pulled - col_sums[:, None] * widened)
        return (objective_accrued, pos_coef, anchor_grad, tile_grad, coef_low, col_sums)

    def skip(unused):
        return (
            jnp.zeros((anchor_count,), jnp.float32),
            jnp.zeros((anchor_count, matching_samples), jnp.float32),
            jnp.zeros((anchor_count, anchors.shape[1]), jnp.float32),
            jnp.zeros((block_tally, anchors.shape[1]), jnp.float32),
            jnp.zeros((anchor_count, block_tally), jnp.bfloat16),
            jnp.zeros((block_tally,), jnp.float32),
        )

    return lax.cond(listed, compute, skip, 0)


def local(features, head_weight, labels, pos_index, pair_mask, loss_weight):
    embedded = jnp.dot(features, head_weight, preferred_element_type=jnp.float32).astype(
        jnp.bfloat16
    )
    widened = embedded.astype(jnp.float32)
    anchor_sq = jnp.sum(widened * widened, axis=1)
    tile_rows, tile_labels = (
        lax.all_gather(embedded, "rows", axis=0, tiled=True),
        lax.all_gather(labels, "rows", axis=0, tiled=True),
    )
    pos_rows = tile_rows[pos_index]
    pos_wide = pos_rows.astype(jnp.float32)
    pos_sq = jnp.sum(pos_wide * pos_wide, axis=2)
    matching_separation = (
        anchor_sq[:, None]
        + pos_sq
        - 2.0 * jnp.einsum("ad,akd->ak", embedded, pos_rows, preferred_element_type=jnp.float32)
    )
    offsets = pair_mask.shape[1]
    loss_total, coef_total, grad_total, own_term, first_low, first_sums = score_tile(
        embedded,
        anchor_sq,
        labels,
        matching_separation,
        loss_weight,
        tile_rows,
        tile_labels,
        pair_mask[0, 0] > 0,
    )
    received = jnp.zeros_like(own_term)
    walk_rows, walk_labels = (tile_rows, tile_labels)
    for offset in range(1, offsets):
        walk_rows, walk_labels = passed_along((walk_rows, walk_labels), "blk", 1)
        loss_part, coef_part, grad_part, term_part, low_part, sums_part = score_tile(
            embedded,
            anchor_sq,
            labels,
            matching_separation,
            loss_weight,
            walk_rows,
            walk_labels,
            pair_mask[0, offset] > 0,
        )
        loss_total = loss_total + loss_part
        coef_total = coef_total + coef_part
        grad_total = grad_total + grad_part
        received = received + passed_along(term_part.astype(jnp.bfloat16), "blk", -offset).astype(
            term_part.dtype
        )
    grad_total = grad_total - 2.0 * jnp.sum(coef_total[:, :, None] * pos_wide, axis=1)
    pushed = 2.0 * coef_total[:, :, None] * (pos_wide - widened[:, None, :])
    own_term = own_term.at[pos_index.reshape(-1)].add(pushed.reshape(-1, pushed.shape[2]))
    quarter_sum = lax.psum_scatter(own_term + received, "rows", scatter_dimension=0, tiled=True)
    emb_grad = grad_total + quarter_sum
    grad_low = emb_grad.astype(jnp.bfloat16)
    weight_grad = lax.psum_scatter(
        lax.dot_general(
            features, grad_low, (((0,), (0,)), ((), ())), preferred_element_type=jnp.float32
        ),
        ("blk", "rows"),
        scatter_dimension=0,
        tiled=True,
    )
    return (loss_total, weight_grad)


MESH = pl.DeviceIdType.MESH
NT = (((1,), (1,)), ((), ()))
TN = (((0,), (0,)), ((), ()))


def dot(a, b, dims=(((1,), (0,)), ((), ()))):
    return lax.dot_general(a, b, dims, preferred_element_type=jnp.float32)


LOG2E = math.log2(math.e)
LN2 = math.log(2.0)
CEILING = 40.0
FAR = 1e38
PIECES = 6
SUB = 32
TILES = (0, 2, 1, 1, 0, 2)
SIDES = (0, 1, 1, 0, 1, 0)
AHEAD = 3
STEPS = len(TILES)


def last_of(codes, value):
    return max(i for i, code in enumerate(codes) if code == value)


LAGS = (3, 4, 6)


def scope(name):
    return contextlib.nullcontext()


def spread_rows(row):
    return jnp.transpose(jnp.broadcast_to(row, (128, row.shape[1])))


def twice(block):
    return jnp.concatenate([block, block], axis=1)


def by_eights(block):
    total = block[0:8]
    for i in range(1, block.shape[0] // 8):
        total = total + block[8 * i : 8 * i + 8]
    return total


def kernel(
    f_hbm, w_hbm, lab_hbm, pos_hbm, wgt_hbm, mask_hbm, loss_ref, out_ref,
    lab_ref, pos_ref, wgt_ref, mask_ref, fv, wv, ea, nr, meta, metan, scored, fc, fct, acc, pul, cs, prod, prod2, gram, low, low2, comb, place, pulled, dpr, sqc, labc, sqn, stp, st, strec, tot,
    tst, trec, relay, ast0, arec0, ast1, arec1, hst, hrec, ga, yown, yst, yrec, pst, prec,
    f_l, w_l, ea_s, ea_r, ma_s, ma_r, en_s, en_r, mn_s, mn_r, fc_s, fc_r, d_s, d_r, t_s, t_r, rl_r, a0_s, a0_r, a1_s, a1_r,
    h_s, h_r, st_s, st_r, g_s, g_r, y_s, y_r, p_s, p_r, i_s,
):
    nb = lax.axis_size("blk")
    t = lax.axis_index("blk")
    r = lax.axis_index("rows")
    z, x = t // 2, t % 2
    y, c = r // 2, r % 2
    tx = 2 * z + 1 - x
    mate = 2 * y + 1 - c
    across = 2 * (1 - y) + c
    diag = 2 * (1 - y) + 1 - c
    peers = (mate, across, diag)
    q = 2 * x + c
    q_mate, q_side, q_diag = 2 * x + 1 - c, 2 * (1 - x) + c, 2 * (1 - x) + 1 - c
    quarter, depth = f_hbm.shape
    width = w_hbm.shape[1]
    tile = 4 * quarter
    pieces = ga.shape[0]
    piece = width // pieces
    half = out_ref.shape[0]
    f32, bf16 = jnp.float32, jnp.bfloat16
    scale = SMOOTHING_SCALE * LOG2E

    def remote(src, dst, ss, rs, dev):
        return pltpu.make_async_remote_copy(
            src_ref=src, dst_ref=dst, send_sem=ss, recv_sem=rs, device_id=dev, device_id_type=MESH
        )

    drains = []

    def push(src, dst, ss, rs, dev):
        remote(src, dst, ss, rs, dev).start()

    def push_drained(src, dst, ss, rs, dev):
        push(src, dst, ss, rs, dev)
        drains.append((src, ss))

    def landed(dst, rs):
        remote(dst, dst, ea_s.at[0], rs, (t, mate)).wait_recv()

    def drained(src, ss):
        remote(src, src, ss, ea_r.at[0, 0], (t, mate)).wait_send()

    columns = width // wv.shape[0]
    f_copy = pltpu.make_async_copy(f_hbm, fv, f_l)
    w_copies = [
        pltpu.make_async_copy(w_hbm.at[:, j * columns : (j + 1) * columns], wv.at[j], w_l.at[j])
        for j in range(wv.shape[0])
    ]
    f_copy.start()
    w_copies[0].start()
    small_copies = [
        pltpu.make_async_copy(source, target, i_s.at[n])
        for n, (source, target) in enumerate(
            ((lab_hbm, lab_ref), (pos_hbm, pos_ref), (wgt_hbm, wgt_ref), (mask_hbm, mask_ref))
        )
    ]
    for copy in small_copies:
        copy.start()

    barrier = pltpu.get_barrier_semaphore()
    for step in range(nb):
        for row in range(4):
            if step or row:
                pl.semaphore_signal(barrier, inc=1, device_id=((t + step) % nb, (r + row) % 4), device_id_type=MESH)

    with scope("small"):
        for copy in small_copies:
            copy.wait()
    meta[r] = jnp.zeros(meta.shape[1:], f32)
    meta[r, 0:1, :] = lab_ref[...].astype(f32)
    meta[r, 1:4, :] = pos_ref[...].astype(f32)
    meta[r, 4:5, :] = wgt_ref[...]
    for s in range(3):
        scored[s] = jnp.broadcast_to((mask_ref[0:1, s : s + 1] > 0).astype(f32), (8, quarter))

    def along_z(j):
        cut = slice(j * columns, (j + 1) * columns)
        return remote(nr.at[0, :, cut], nr.at[2, :, cut], en_s.at[1], en_r.at[1, j], ((t + 2) % nb, r))

    def along_x(held, j):
        cut = slice(j * columns, (j + 1) * columns)
        return remote(nr.at[held, :, cut], nr.at[1, :, cut], en_s.at[0], en_r.at[0, j], (tx, r))

    def block_column(px, pc, i):
        return pl.multiple_of((4 * (2 * pc + i % 2) + 2 * px + i // 2) * 128, 128)

    def send_features(i):
        for n, (px, pc) in enumerate(((x, 1 - c), (1 - x, c), (1 - x, 1 - c))):
            dev = (2 * z + px, 2 * y + pc)
            push(fv.at[:, pl.ds(block_column(px, pc, i), 128)], fc.at[q, i], fc_s.at[n], fc_r.at[q], dev)

    f_copy.wait()
    for copy in w_copies[1:]:
        copy.start()
    square = jnp.zeros((quarter, 1), f32)
    for j in range(wv.shape[0]):
        with scope("embed"):
            w_copies[j].wait()
            cut = slice(j * columns, (j + 1) * columns)
            part = dot(fv[...], wv[j]).astype(bf16)
            ea[r, :, cut] = part
            nr[0, :, cut] = part
            wide = part.astype(f32)
            square = square + jnp.sum(wide * wide, axis=1, keepdims=True)
        if j == 0:
            with scope("barrier"):
                pl.semaphore_wait(barrier, 4 * nb - 1)
        for n, peer in ((1, across), (0, mate)):
            push(ea.at[r, :, cut], ea.at[r, :, cut], ea_s.at[n], ea_r.at[r, j], (t, peer))
        along_z(j).start()
        if j == 0:
            send_features(0)

        @pl.when(x == 0)
        def _():
            along_x(0, j).start()

    meta[r, 5:6, :] = jnp.transpose(jnp.broadcast_to(square, (quarter, 128)))[0:1, :]
    for n, peer in enumerate(peers):
        push_drained(meta.at[r], meta.at[r], ma_s.at[n], ma_r.at[r], (t, peer))
    for s in (1, 2):
        push_drained(meta.at[r], metan.at[s - 1], mn_s.at[s - 1], mn_r.at[s - 1], ((t + s) % nb, r))
    for i in range(4):
        fc[q, i] = fv[:, pl.ds(block_column(x, c, i), 128)]

    labc[0] = spread_rows(meta[r, 0:1, :])
    for a in range(4):
        stp[a] = jnp.zeros(stp.shape[1:], f32)
    for s in range(3):
        cs[s] = jnp.zeros((quarter, 128), f32)

    @pl.when(x == 1)
    def _():
        trec[0] = jnp.zeros((quarter, width), bf16)

    sub = lax.broadcasted_iota(jnp.int32, (SUB, quarter), 0).astype(f32)

    def side_rows(side):
        return ea[pl.ds(2 * side, 2)].reshape(2 * quarter, width)

    def positives(first, count, found):
        rows_here = ea[pl.ds(first, count)].reshape(count * quarter, width)
        gram[0 : count * quarter] = dot(rows_here, ea[r], NT)
        places = [meta[r, 1 + k : 2 + k, :] for k in range(3)]
        for h in range(count):
            sqc[h * quarter : (h + 1) * quarter] = spread_rows(meta[first + h, 5:6, :])

        def rows(i, found):
            at = pl.ds(pl.multiple_of(i * SUB, SUB), SUB)
            d = twice(sqc[at]) - 2.0 * gram[at]
            base = (first * quarter + i * SUB).astype(f32)
            return tuple(found[k] + by_eights(jnp.where(sub == places[k] - base, d, 0.0)) for k in range(3))

        return lax.fori_loop(0, count * quarter // SUB, rows, found)

    with scope("own_rows"):
        for j in range(wv.shape[0]):
            landed(ea.at[mate, :, j * columns : (j + 1) * columns], ea_r.at[mate, j])
        landed(meta.at[mate], ma_r.at[mate])
        found = positives(2 * y, 2, tuple(jnp.zeros((8, quarter), f32) for _ in range(3)))
        prod[...] = dot(nr[0], side_rows(y), NT)

    def tile_columns(s, block):
        labc[s] = spread_rows(block[0:1, :])
        sqn[s] = scale * spread_rows(block[5:6, :])

    tile_columns(0, meta[r])
    with scope("rows"):
        for j in range(wv.shape[0]):
            cut = slice(j * columns, (j + 1) * columns)
            landed(ea.at[across, :, cut], ea_r.at[across, j])
            push(ea.at[across, :, cut], ea.at[across, :, cut], ea_s.at[2], ea_r.at[across, j], (t, mate))

            @pl.when(x == 1)
            def _():
                landed(nr.at[2, :, cut], en_r.at[1, j])
                along_x(2, j).start()

        landed(meta.at[across], ma_r.at[across])

    for i in range(1, 4):
        send_features(i)
    with scope("positives"):
        found = positives(across, 1, found)
        for j in range(wv.shape[0]):
            landed(ea.at[diag, :, j * columns : (j + 1) * columns], ea_r.at[diag, j])
        landed(meta.at[diag], ma_r.at[diag])
        found = positives(diag, 1, found)
        for k in range(3):
            dpr[r, k : k + 1, :] = scale * (jnp.sum(found[k], axis=0, keepdims=True) + SLACK_GAP)
        dpr[r, 3:8, :] = jnp.zeros((5, quarter), f32)
    for n, peer in enumerate(peers):
        push_drained(dpr.at[r], dpr.at[r], d_s.at[n], d_r.at[r], (t, peer))


    def pairs(s, side, prod, low):
        on = scored[s, 0:1, :] > 0.0
        for g in range(2):
            a = 2 * side + g
            cut = slice(g * quarter, (g + 1) * quarter)
            tops = [jnp.where(on, dpr[a, k : k + 1, :], -FAR) for k in range(3)]
            names = meta[a, 0:1, :]
            weight = meta[a, 4:5, :] * (1.0 / (3.0 * tile))
            sums = [jnp.zeros((8, quarter), f32)] * 4
            for i in range(quarter // SUB):
                at = slice(i * SUB, (i + 1) * SUB)
                spread = twice(sqn[s, at]) - (2.0 * scale) * prod[at, cut]
                spread = jnp.where(twice(labc[s, at]) != names, spread, FAR)
                e, over = [], None
                for k in range(3):
                    h = tops[k] - spread
                    m = jnp.minimum(h, CEILING)
                    e.append(jnp.exp2(m))
                    over = h - m if over is None else over + (h - m)
                one = [1.0 + v for v in e]
                p = (e[0] + one[0] * e[1]) * one[2] + e[2]
                u = 1.0 + p
                inv = 1.0 / u
                logs = LN2 * (jnp.log2(u) + over) + (p - (u - 1.0)) * inv
                last = inv * one[2]
                sig = (e[0] * (last * one[1]), e[1] * (last * one[0]), e[2] * (inv * (one[0] * one[1])))
                coef = (sig[0] + sig[1] + sig[2]) * weight
                low[at, cut] = coef.astype(bf16)
                cs[s, at] += coef[:, :128] + coef[:, 128:]
                sums = [v + by_eights(w) for v, w in zip(sums, (logs,) + sig)]
            for k in range(4):
                stp[2 * side + g, k] += sums[k]

    def products(i, low):
        s, side = TILES[i], side_of(i)
        pulled_here = dot(low[...], side_rows(side))
        gained_here = dot(low[...], nr[s], TN).reshape(2, quarter, width)
        if TILES.index(s) == i:
            pul[s] = pulled_here
        else:
            pul[s] += pulled_here
        if SIDES.index(SIDES[i]) == i:
            acc[pl.ds(2 * side, 2)] = gained_here
        else:
            acc[pl.ds(2 * side, 2)] += gained_here

    def sums_over_lanes(s):
        return jnp.sum(cs[s], axis=1, keepdims=True)

    def term_value(s):
        return 2.0 * (pul[s] - sums_over_lanes(s) * nr[s].astype(f32))

    def columns_of(j):
        return pl.ds(pl.multiple_of(j * piece, piece), piece)

    def term_copy(s, j):
        cut = columns_of(j)
        return remote(
            tst.at[s - 1, :, cut], trec.at[s - 1, :, cut], t_s.at[s - 1], t_r.at[s - 1, j], ((t + nb - s) % nb, r)
        )

    def relay_copy(j):
        cut = columns_of(j)
        return remote(tst.at[0, :, cut], relay.at[:, cut], t_s.at[0], rl_r.at[j], (tx, r))

    def send_first():
        tst[0] = term_value(1).astype(bf16)
        for j in range(pieces):
            pl.when(x == 0)(lambda: relay_copy(j).start())
            pl.when(x == 1)(lambda: term_copy(1, j).start())

    def send_second():
        pul[2] = term_value(2)

        @pl.when(x == 0)
        def _():
            tst[1] = pul[2].astype(bf16)
            for j in range(pieces):
                term_copy(2, j).start()

    def merge(j):
        cut = columns_of(j)
        landed(relay.at[:, cut], rl_r.at[j])
        tst[1, :, cut] = (pul[2, :, cut] + relay[:, cut].astype(f32)).astype(bf16)
        term_copy(2, j).start()

    def merge_on_x1(j):
        pl.when(x == 1)(lambda: merge(j))

    def across_copy(j):
        cut = columns_of(j)
        return remote(ast1.at[:, cut], arec1.at[:, cut], a1_s, a1_r.at[j], (t, across))

    def side_of(i):
        return 1 - y if SIDES[i] else y

    def tile_arrives(s):
        for j in range(wv.shape[0]):
            @pl.when(jnp.logical_or(s == 1, x == 0))
            def _():
                landed(nr.at[s, :, j * columns : (j + 1) * columns], en_r.at[s - 1, j])

        landed(metan.at[s - 1], mn_r.at[s - 1])
        tile_columns(s, metan[s - 1])

    def send_hst():
        hst[...] = (2.0 * acc[diag]).astype(bf16)
        remote(hst, hrec, h_s, h_r, (t, mate)).start()

    def send_ast():
        landed(hrec, h_r)
        ast1[...] = (2.0 * acc[across] + hrec[...].astype(f32)).astype(bf16)
        for j in range(pieces):
            across_copy(j).start()

    def step(i, held, coming, low, before):
        arriving = i == TILES.index(1) - 1

        def next_product():
            if i + 1 < STEPS:
                coming[...] = dot(nr[TILES[i + 1]], side_rows(side_of(i + 1)), NT)

        if i == SIDES.index(1):
            with scope("distances"):
                for peer in (across, diag):
                    landed(dpr.at[peer], d_r.at[peer])
        with scope("chunk"):
            if not arriving:
                next_product()
            if i:
                products(i - 1, before)
            if i == last_of(TILES, 1) + 1:
                send_first()
            if i == last_of(SIDES, 1) + 1:
                send_hst()
            pairs(TILES[i], side_of(i), held, low)
        if arriving:
            with scope("tile1"):
                tile_arrives(1)
            next_product()

    with scope("tile2"):
        tile_arrives(2)
    with scope("distance"):
        landed(dpr.at[mate], d_r.at[mate])
    with scope("scores"):
        for i in range(0, STEPS, 2):
            step(i, prod, prod2, low, low2)
            step(i + 1, prod2, prod, low2, low)

    for a in range(4):
        for k in range(4):
            row = 4 * (a % 2) + k
            st[a // 2, row : row + 1, :] = jnp.sum(stp[a, k], axis=0, keepdims=True)
    for n, peer in enumerate(peers):
        push_drained(st, strec.at[r], st_s.at[n], st_r.at[r], (t, peer))
    with scope("last"):
        products(STEPS - 1, low2)
        send_second()
        merge_on_x1(0)
        send_ast()
        merge_on_x1(1)
        ast0[...] = (2.0 * acc[mate]).astype(bf16)
        push_drained(ast0, arec0, a0_s, a0_r, (t, mate))

    def features():
        with scope("features"):
            for n in (q_mate, q_side, q_diag):
                landed(fc.at[n], fc_r.at[n])
            for n in range(4):
                for i in range(4):
                    fct[i * 128 : (i + 1) * 128, n * quarter : (n + 1) * quarter] = jnp.transpose(fc[n, i])

    strec[r] = st[...]
    features()
    merge_on_x1(2)
    with scope("statistics"):
        for peer in peers:
            landed(strec.at[peer], st_r.at[peer])
    for a in range(4):
        part = slice(4 * (a % 2), 4 * (a % 2) + 4)
        tot[a, 0:4, :] = (
            strec[0, a // 2, part] + strec[1, a // 2, part] + strec[2, a // 2, part] + strec[3, a // 2, part]
        )
    loss_ref[...] = tot[r, 0:1, :] * (1.0 / (SMOOTHING_SCALE * 3.0 * tile))

    with scope("pulls"):
        row_sub = lax.broadcasted_iota(jnp.int32, (SUB, quarter), 0).astype(f32)
        lane = lax.broadcasted_iota(jnp.int32, (SUB, quarter), 1).astype(f32)
        share = 1.0 / (3.0 * tile)
        for k in range(3):
            place[k] = spread_rows(meta[r, 1 + k : 2 + k, :])
            pulled[k] = spread_rows(tot[r, 1 + k : 2 + k, :] * meta[r, 4:5, :] * share)

        def listed(i, carry):
            at = pl.ds(pl.multiple_of(i * SUB, SUB), SUB)
            first = (r * quarter + i * SUB).astype(f32)
            gained = jnp.zeros((SUB, 128), f32)
            for n in range(4):
                given = jnp.zeros((SUB, quarter), f32)
                wgt = meta[n, 4:5, :] * share
                for k in range(3):
                    hit = row_sub == meta[n, 1 + k : 2 + k, :] - first
                    given = given + jnp.where(hit, tot[n, 1 + k : 2 + k, :] * wgt, 0.0)
                gained = gained + (given[:, :128] + given[:, 128:])
                for k in range(3):
                    hit = lane == twice(place[k, at]) - float(n * quarter)
                    given = given + jnp.where(hit, twice(pulled[k, at]), 0.0)
                high = given.astype(bf16)
                comb[0, at, n * quarter : (n + 1) * quarter] = high
                comb[1, at, n * quarter : (n + 1) * quarter] = (given - high.astype(f32)).astype(bf16)
            cs[1, at] = gained
            return carry

        lax.fori_loop(0, quarter // SUB, listed, 0)
        cs[2] = jnp.broadcast_to(sums_over_lanes(1) - sums_over_lanes(0), (quarter, 128))

    def side_copy(j):
        return remote(ga.at[j, q], ga.at[j, q], g_s.at[1], g_r.at[j, q], (tx, r))

    def mate_copy(j):
        return remote(ga.at[j, q], ga.at[j, q], g_s.at[0], g_r.at[j, q], (t, mate))

    def forward_copy(j):
        return remote(ga.at[j, q_side], ga.at[j, q_side], g_s.at[2], g_r.at[j, q_side], (t, mate))

    def part_copy(j):
        return remote(yst.at[j], yrec.at[j], y_s, y_r.at[j], (t, across))

    def hop(j, i, h):
        return remote(
            pst.at[j, i, h], prec.at[j, z], p_s.at[i, h], p_r.at[j], (2 * (2 * c + i) + x, 2 * y + h)
        )

    def away(i, h):
        return jnp.logical_or(2 * c + i != z, c != h)

    def gather(j):
        cut = columns_of(j)
        rows_cut = ea[:, :, cut].reshape(tile, piece)
        net = acc[r, :, cut] + pul[0, :, cut] + cs[2, :, :piece] * ea[r, :, cut].astype(f32)
        net = net - dot(comb[0], rows_cut) - dot(comb[1], rows_cut)
        total = 2.0 * net + arec0[:, cut].astype(f32)
        landed(arec1.at[:, cut], a1_r.at[j])
        total = total + arec1[:, cut].astype(f32)
        @pl.when(x == 0)
        def _():
            landed(trec.at[0, :, cut], t_r.at[0, j])

        landed(trec.at[1, :, cut], t_r.at[1, j])
        total = total + trec[0, :, cut].astype(f32) + trec[1, :, cut].astype(f32)
        ga[j, q] = total.astype(bf16)
        side_copy(j).start()
        mate_copy(j).start()

    def forward(j):
        landed(ga.at[j, q_side], g_r.at[j, q_side])
        forward_copy(j).start()

    def multiply(j):
        for n in (q_mate, q_diag):
            landed(ga.at[j, n], g_r.at[j, n])
        part = dot(fct[...], ga[j].reshape(tile, piece))
        top, bottom = part[: 4 * half], part[4 * half :]
        yown[j] = jnp.where(y == 0, top, bottom)
        yst[j] = jnp.where(y == 0, bottom, top).astype(bf16)
        part_copy(j).start()

    def scatter(j):
        landed(yrec.at[j], y_r.at[j])
        total = (yown[j] + yrec[j].astype(f32)).astype(bf16)
        for i in range(2):
            for h in range(2):
                pst[j, i, h] = total[(2 * i + h) * half : (2 * i + h + 1) * half]
        for i in range(2):
            for h in range(2):
                @pl.when(away(i, h))
                def _():
                    hop(j, i, h).start()

                @pl.when(jnp.logical_not(away(i, h)))
                def _():
                    prec[j, z] = pst[j, i, h]

    def finish(j):
        pl.when(z // 2 != c)(lambda: landed(prec.at[j], p_r.at[j]))
        pl.when(z // 2 == c)(lambda: landed(prec.at[j, 0 : nb // 2 - 1], p_r.at[j]))
        result = prec[j, 0].astype(f32)
        for source in range(1, nb // 2):
            result = result + prec[j, source].astype(f32)
        out_ref[:, columns_of(j)] = result

    with scope("mate"):
        landed(arec0, a0_r)

    def stages(i, carry):
        @pl.when(i < pieces)
        def _():
            with scope("gather"):
                gather(i)

        @pl.when(jnp.logical_and(x == 1, i + AHEAD < pieces))
        def _():
            with scope("merge"):
                merge(i + AHEAD)

        for lag, name, work in zip(LAGS, ("forward", "multiply", "scatter"), (forward, multiply, scatter)):
            @pl.when(jnp.logical_and(i >= lag, i < pieces + lag))
            def _():
                with scope(name):
                    work(i - lag)

        return carry

    lax.fori_loop(0, pieces + LAGS[-1], stages, 0)

    def close(j, carry):
        with scope("finish"):
            finish(j)
        return carry

    lax.fori_loop(0, pieces, close, 0)

    with scope("drain"):
        for n, source in enumerate((q, q, q_side)):
            drained(ga.at[:, source], g_s.at[n])
        drained(yst, y_s)
        for i in range(2):
            for h in range(2):
                @pl.when(away(i, h))
                def _():
                    drained(pst.at[:, i, h], p_s.at[i, h])
        for n, source in enumerate((mate, r, across)):
            drained(ea.at[source], ea_s.at[n])
        for n in range(2):
            drained(nr.at[n], en_s.at[n])
            drained(tst.at[n], t_s.at[n])
        for n in range(3):
            drained(fc.at[q], fc_s.at[n])
        drained(ast1, a1_s)
        drained(hst, h_s)
        for source, semaphore in drains:
            drained(source, semaphore)


def results(loss_ref, grad_ref, loss_out, grad_out):
    loss_out[...] = loss_ref[0]
    grad_out[...] = grad_ref[...]


def fused(features, head_weight, labels, pos_index, pair_mask, loss_weight):
    quarter, depth = features.shape
    width = head_weight.shape[1]
    nb = lax.axis_size("blk")
    share = depth // (4 * nb)
    f32, bf16 = jnp.float32, jnp.bfloat16
    dma = pltpu.SemaphoreType.DMA
    vmem = pl.BlockSpec(memory_space=pltpu.VMEM)
    hbm = pl.BlockSpec(memory_space=pl.ANY)
    block = (quarter, width)
    small = (8, quarter)
    piece = width // PIECES
    loss, grad = pl.pallas_call(
        kernel,
        out_shape=(pltpu.VMEM((1, quarter), f32), pltpu.VMEM((share, width), f32)),
        in_specs=[hbm] * 6,
        out_specs=(vmem, vmem),
        scratch_shapes=[
            pltpu.VMEM((1, quarter), jnp.int32),
            pltpu.VMEM(pos_index.shape[::-1], jnp.int32),
            pltpu.VMEM((1, quarter), f32),
            pltpu.VMEM(pair_mask.shape, jnp.int32),
            pltpu.VMEM((quarter, depth), bf16),
            pltpu.VMEM((3, depth, width // 3), bf16),
            pltpu.VMEM((4,) + block, bf16),
            pltpu.VMEM((3,) + block, bf16),
            pltpu.VMEM((4,) + small, f32),
            pltpu.VMEM((2,) + small, f32),
            pltpu.VMEM((3,) + small, f32),
            pltpu.VMEM((4, 4, quarter, 128), bf16),
            pltpu.VMEM((512, 4 * quarter), bf16),
            pltpu.VMEM((4,) + block, f32),
            pltpu.VMEM((3,) + block, f32),
            pltpu.VMEM((3, quarter, 128), f32),
            pltpu.VMEM((quarter, 2 * quarter), f32),
            pltpu.VMEM((quarter, 2 * quarter), f32),
            pltpu.VMEM((2 * quarter, quarter), f32),
            pltpu.VMEM((quarter, 2 * quarter), bf16),
            pltpu.VMEM((quarter, 2 * quarter), bf16),
            pltpu.VMEM((2, quarter, 4 * quarter), bf16),
            pltpu.VMEM((3, quarter, 128), f32),
            pltpu.VMEM((3, quarter, 128), f32),
            pltpu.VMEM((4,) + small, f32),
            pltpu.VMEM((2 * quarter, 128), f32),
            pltpu.VMEM((3, quarter, 128), f32),
            pltpu.VMEM((3, quarter, 128), f32),
            pltpu.VMEM((4, 4) + small, f32),
            pltpu.VMEM((2,) + small, f32),
            pltpu.VMEM((4, 2) + small, f32),
            pltpu.VMEM((4,) + small, f32),
            pltpu.VMEM((2,) + block, bf16),
            pltpu.VMEM((2,) + block, bf16),
            pltpu.VMEM(block, bf16),
            pltpu.VMEM(block, bf16),
            pltpu.VMEM(block, bf16),
            pltpu.VMEM(block, bf16),
            pltpu.VMEM(block, bf16),
            pltpu.VMEM(block, bf16),
            pltpu.VMEM(block, bf16),
            pltpu.VMEM((PIECES, 4, quarter, piece), bf16),
            pltpu.VMEM((PIECES, 4 * share, piece), f32),
            pltpu.VMEM((PIECES, 4 * share, piece), bf16),
            pltpu.VMEM((PIECES, 4 * share, piece), bf16),
            pltpu.VMEM((PIECES, 2, 2, share, piece), bf16),
            pltpu.VMEM((PIECES, nb // 2, share, piece), bf16),
            dma(()), dma((3,)), dma((3,)), dma((4, 3)), dma((3,)), dma((4,)), dma((2,)), dma((2, 3)), dma((2,)), dma((2,)),
            dma((3,)), dma((4,)), dma((3,)), dma((4,)), dma((2,)), dma((2, PIECES)), dma((PIECES,)), dma(()), dma(()),
            dma(()), dma((PIECES,)), dma(()), dma(()), dma((3,)), dma((4,)),
            dma((3,)), dma((PIECES, 4)), dma(()), dma((PIECES,)), dma((2, 2)), dma((PIECES,)), dma((4,)),
        ],
        compiler_params=pltpu.CompilerParams(
            collective_id=0, has_side_effects=True, vmem_limit_bytes=56 * 1024 * 1024
        ),
    )(features, head_weight, labels[None, :], pos_index.T, loss_weight[None, :], pair_mask)
    return pl.pallas_call(
        results,
        out_shape=(jax.ShapeDtypeStruct((quarter,), f32), jax.ShapeDtypeStruct((share, width), f32)),
        in_specs=[vmem] * 2,
        out_specs=(vmem, vmem),
    )(*(pltpu.with_memory_space_constraint(part, pltpu.VMEM) for part in (loss, grad)))


def solution(mesh):
    body = fused if mesh.shape["blk"] == 8 and mesh.shape["rows"] == 4 else local
    return jax.shard_map(
        body,
        mesh=mesh,
        in_specs=(
            P(("blk", "rows"), None),
            P(),
            P(("blk", "rows")),
            P(("blk", "rows"), None),
            P("blk", None),
            P(("blk", "rows")),
        ),
        out_specs=(P(("blk", "rows")), P(("blk", "rows"), None)),
        check_vma=False,
    )
```
